768 devices in a mesh: wave: 12 (over z), lev: 64 (over y, x, core).
Axes of the slice: x: 4, y: 8, z: 12, core: 2. Of those that a mesh axis runs over, the one named last changes fastest.
Arguments:
- spec: bfloat16 [24, 64, 2, 1280], P('wave', 'lev'), may hold values from -0.59765625 to 0.59765625
- legendre: bfloat16 [24, 1280, 1200], P('wave', 'lev'), may hold values from -0.15625 to 0.15625
- gauss_w: float32 [1200], replicated, may hold values from 0.5 to 1.5
- cycle_len: int32 [1200], replicated, may hold values from 20 to 4816, as said below
- wave_map: int32 [24], replicated, may hold values from 0 to 23, as said below
Outputs:
- grid: bfloat16 [2, 600, 64, 4864], P(None, 'wave', 'lev')
- spec_out: float32 [24, 64, 2, 1280], P('wave', 'lev')
The draws below stay inside these ranges and needn't reach their ends.
Inputs may be any that keep to these rules, and one draw needn't show every extreme that they name: `wave_map`: A permutation of 0 .. 23; slot r of each index of wave (slots are numbered 2 to an index) holds a value from the r-th group of 12 consecutive values. `cycle_len`: entry 2r is the point count of the r-th cycle from the pole, entry 2r + 1 that of cycle 1200 - 1 - r; cycle j has a multiple of 4 points between max(20, 8 + 4 j) and 20 + 4 j, and cycle 1200 - 1 exactly 20 + 4 (1199); the southern cycle mirrors the northern one.
All inputs are finite; a program needn't handle non-finite values.
Results may differ from the reference program's by a relative error of at most 0.0055.
Values may be sent and summed in bfloat16 or wider, within the bound.
A program may use at most 32 MiB of HBM per device.

```python
import math
import jax
import jax.numpy as jnp
from jax import lax

NN = 1280
NH = 1200
M_DEV = 2
MW = 24
FIELDS = 64
LPAD = 4864
N_WAVE = 12


def draw_wave_map(key, part):
    shuffled = jax.random.permutation(jax.random.fold_in(key, 11), N_WAVE)
    slot_ids = jnp.arange(MW, dtype=jnp.int32)
    holder = slot_ids // M_DEV
    rounds = slot_ids % M_DEV
    placed = shuffled[holder]
    within = jnp.where(rounds % 2 == 0, placed, N_WAVE - 1 - placed)
    return (rounds * N_WAVE + within).astype(jnp.int32)


def draw_cycle_len(key, part):
    packed = jnp.arange(NH, dtype=jnp.int32)
    row_ids = packed // 2
    latitude = jnp.where(packed % 2 == 0, row_ids, NH - 1 - row_ids)
    reduction = jax.random.randint(jax.random.fold_in(key, 23), (NH,), 0, 4)
    reduction = jnp.where(latitude == NH - 1, 0, reduction)
    return jnp.maximum(20, 20 + 4 * latitude - 4 * reduction).astype(jnp.int32)


def steps_of(stream_key, shape, shards, low, high):
    def one(dim, blocks):
        steps = jax.random.uniform(jax.random.fold_in(jax.random.fold_in(stream_key, 6), dim), (blocks,), jnp.float32, low / len(shards), high / len(shards))
        return jnp.repeat(jnp.exp(steps), shape[dim] // blocks).reshape((-1,) + (1,) * (len(shape) - dim - 1))

    factor_of = one(*shards[0])
    for cut in shards[1:]:
        factor_of = factor_of * one(*cut)
    return factor_of


def gaussian(rng, extent, scale, bound, shards=(), kind=jnp.bfloat16):
    level = steps_of(rng, extent, shards, -0.22, 0.18) if shards else 1.0
    result = jax.random.normal(rng, extent, jnp.float32) * scale * level
    return jnp.minimum(jnp.maximum(result, -bound), bound).astype(kind)


def setup_inputs(seed: int = 0) -> dict:
    splits = jax.random.split(jax.random.key(seed), 6)
    return {
        "spec": gaussian(splits[0], (MW, FIELDS, 2, NN), 0.1, 0.59765625, ((0, 12), (1, 64))),
        "legendre": gaussian(splits[1], (MW, NN, NH), NN ** -0.5, 0.15625, ((0, 12), (1, 64))),
        "gauss_w": jnp.clip(jax.random.uniform(splits[2], (NH,), jnp.float32, 0.5, 1.5), 0.5, 1.5),
        "cycle_len": draw_cycle_len(jax.random.fold_in(splits[5], 71), 0),
        "wave_map": draw_wave_map(jax.random.fold_in(splits[5], 71), 0),
    }


def block_rows(row_total):
    for candidate in (10, 8, 6, 5, 4, 3, 2):
        if row_total % candidate == 0:
            return candidate
    return 1


def cycle_tables(lens_pair, orders, padded):
    position = jnp.arange(padded, dtype=jnp.int32)[None, :]
    first_len = lens_pair[:, 0:1]
    second = lens_pair[:, 1:2]
    upper_half = position >= first_len
    occupied = position < first_len + second
    offset = jnp.where(upper_half, position - first_len, position)
    length = jnp.where(upper_half, second, first_len)
    turn_count = (orders[None, :, None] * offset[:, None, :]) % length[:, None, :]
    angles = (2.0 * math.pi) * turn_count.astype(jnp.float32) / length[:, None, :].astype(jnp.float32)
    cosine = jnp.where(occupied[:, None, :], jnp.cos(angles), 0.0).astype(jnp.bfloat16)
    minus_sine = jnp.where(occupied[:, None, :], -jnp.sin(angles), 0.0).astype(jnp.bfloat16)
    return jnp.concatenate([cosine, minus_sine], 1), upper_half, occupied


def cycle_block(waves, lens_pair, weights, orders, padded):
    row_count = waves.shape[0]
    fields = waves.shape[3]
    slot_count = orders.shape[0]
    tables, upper_half, occupied = cycle_tables(lens_pair, orders, padded)
    double = jnp.where(orders == 0, 1.0, 2.0)
    resolved = 2 * orders[None, None, :] < lens_pair[:, :, None]
    widening = jnp.where(resolved, double[None, None, :], 0.0)
    scaled = (waves.astype(jnp.float32) * widening[:, None, :, None, None, :]).astype(jnp.bfloat16)
    scaled = scaled.reshape(row_count, 4 * fields, 2 * slot_count)
    images = jnp.einsum("rak,rkp->rap", scaled.astype(jnp.float32), tables.astype(jnp.float32))
    images = images.reshape(row_count, 2, 2, fields, padded)
    values = jnp.where(upper_half[:, None, None, :], images[:, :, 1], images[:, :, 0])
    values = jnp.where(occupied[:, None, None, :], values, 0.0).astype(jnp.bfloat16)
    squared = (values.astype(jnp.float32) * values.astype(jnp.float32)).astype(jnp.bfloat16)
    selector = jnp.stack([jnp.logical_not(upper_half), upper_half], 1)
    by_cycle = jnp.where(selector[:, None, :, None, :], squared[:, :, None, :, :].astype(jnp.float32), 0.0)
    by_cycle = by_cycle.reshape(row_count, 4 * fields, padded)
    returned = jnp.einsum("rap,rkp->rak", by_cycle, tables.astype(jnp.float32))
    returned = returned.reshape(row_count, 2, 2, fields, 2, slot_count)
    factor = jnp.where(resolved, weights[:, :, None] / lens_pair[:, :, None].astype(jnp.float32), 0.0)
    returned = (returned * factor[:, None, :, None, None, :]).astype(jnp.bfloat16)
    return values, returned


def legendre_inverse(spec, legendre, orders):
    degrees = jnp.arange(NN, dtype=jnp.int32)

    def one_slot(operands):
        coefficients, panel, order = operands
        retained = jnp.where(degrees[None, None, :] >= order, coefficients.astype(jnp.float32), 0.0)
        parity = jnp.where((degrees + order) % 2 == 0, 1.0, -1.0)
        panel_wide = panel.astype(jnp.float32)
        north = jnp.einsum("fcn,nq->fcq", retained, panel_wide)
        south = jnp.einsum("fcn,nq->fcq", retained * parity[None, None, :], panel_wide)
        return jnp.stack([north, south], 0).astype(jnp.bfloat16)

    return lax.map(one_slot, (spec, legendre, orders))


def legendre_direct(returned, legendre, orders):
    degrees = jnp.arange(NN, dtype=jnp.int32)

    def one_slot(operands):
        fourier, panel, order = operands
        both = jnp.einsum("hfcq,nq->hfcn", fourier.astype(jnp.float32), panel.astype(jnp.float32))
        parity = jnp.where((degrees + order) % 2 == 0, 1.0, -1.0)
        total = both[0] + parity[None, None, :] * both[1]
        return jnp.where(degrees[None, None, :] >= order, total, 0.0)

    return lax.map(one_slot, (returned, legendre, orders))


def reference(spec, legendre, gauss_w, cycle_len, wave_map):
    orders = ((wave_map * NN) // MW).astype(jnp.int32)
    fourier = legendre_inverse(spec, legendre, orders)
    row_total = NH // 2
    row_block = block_rows(row_total)
    blocks = row_total // row_block
    ordered = fourier.reshape(MW, 2, FIELDS, 2, row_total, 2).transpose(4, 1, 5, 2, 3, 0)
    ordered = ordered.reshape(blocks, row_block, 2, 2, FIELDS, 2, MW)

    def run_block(operands):
        return cycle_block(operands[0], operands[1], operands[2], orders, LPAD)

    values, returned = lax.map(run_block, (ordered, cycle_len.reshape(blocks, row_block, 2), gauss_w.reshape(blocks, row_block, 2)))
    grid = values.reshape(row_total, 2, FIELDS, LPAD).transpose(1, 0, 2, 3)
    returned = returned.reshape(row_total, 2, 2, FIELDS, 2, MW).transpose(5, 1, 3, 4, 0, 2).reshape(MW, 2, FIELDS, 2, NH)
    spec_out = legendre_direct(returned, legendre, orders)
    return grid, spec_out
```

```python
import math

import jax
import jax.numpy as jnp
from jax import lax
from jax.experimental import pallas as pl
from jax.experimental.pallas import tpu as pltpu
from jax.sharding import PartitionSpec as P

LPAD = 4864
LANES = 128
BLOCKS = LPAD // LANES
ROWS = 2 * BLOCKS
ROWS_PAD = 80
SLOT_PAD = 32


def parity_of(degree_ids, own_orders):
    return jnp.where((degree_ids[None, :] + own_orders[:, None]) % 2 == 0, 1.0, -1.0)


def cos_sin_turns(turns):
    quarter = turns * 4.0
    whole = jnp.round(quarter)
    rest = (quarter - whole) * (0.5 * math.pi)
    square = rest * rest
    sine = rest + rest * square * (
        -1.6666666666e-1 + square * (8.3333331e-3 + square * (-1.98412698e-4 + square * 2.7557319e-6))
    )
    cosine = 1.0 + square * (
        -0.5 + square * (4.16666667e-2 + square * (-1.388888889e-3 + square * (2.48015873e-5 - square * 2.7557319e-7)))
    )
    step = whole.astype(jnp.int32) & 3
    swap = (step & 1) == 1
    cos_base = jnp.where(swap, sine, cosine)
    sin_base = jnp.where(swap, cosine, sine)
    cos_value = jnp.where((step == 1) | (step == 2), -cos_base, cos_base)
    sin_value = jnp.where(step >= 2, -sin_base, sin_base)
    return cos_value, sin_value


def turns_of(product, length, inverse):
    whole = jnp.round(product * inverse)
    return (product - whole * length) * inverse


def grid_kernel(len_ref, inv_ref, order_lane_ref, order_sub_ref, row_ref, grid_ref, back_ref):
    lane_f = lax.broadcasted_iota(jnp.int32, (ROWS_PAD, LANES), 1)
    row_f = lax.broadcasted_iota(jnp.int32, (ROWS_PAD, LANES), 0)
    block_start = (row_f // 2) * LANES
    position = block_start + lane_f
    block_start = block_start.astype(jnp.float32)
    second_lane = (lax.broadcasted_iota(jnp.int32, (1, LANES), 1) // SLOT_PAD) % 2 == 1
    sign = jnp.where(lax.broadcasted_iota(jnp.int32, (1, LANES), 1) < 64, 1.0, -1.0)
    order_lane = order_lane_ref[0:1, :]
    inner_lane = lax.broadcasted_iota(jnp.int32, (SLOT_PAD, LANES), 1).astype(jnp.float32)
    inner_product = order_sub_ref[...] * inner_lane
    north = (lax.broadcasted_iota(jnp.int32, (ROWS_PAD, LANES), 0) % 2) == 0
    zero_block = jnp.zeros((SLOT_PAD, LANES), jnp.bfloat16)

    def one_row(row):
        first = len_ref[row, 0]
        second = len_ref[row, 1]
        first_f = first.astype(jnp.float32)
        second_f = second.astype(jnp.float32)
        inv_first = inv_ref[row, 0]
        inv_second = inv_ref[row, 1]
        length_lane = jnp.where(second_lane, second_f, first_f)
        inverse_lane = jnp.where(second_lane, inv_second, inv_first)
        start_lane = jnp.where(second_lane, first_f, 0.0)
        outer = order_lane * (block_start - start_lane)
        outer_cos, outer_sin = cos_sin_turns(turns_of(outer, length_lane, inverse_lane))
        cos_a, sin_a = cos_sin_turns(turns_of(inner_product, first_f, inv_first))
        cos_b, sin_b = cos_sin_turns(turns_of(inner_product, second_f, inv_second))
        inner = jnp.concatenate(
            [
                jnp.concatenate([cos_a.astype(jnp.bfloat16), zero_block], 1),
                jnp.concatenate([zero_block, cos_b.astype(jnp.bfloat16)], 1),
                jnp.concatenate([(-sin_a).astype(jnp.bfloat16), zero_block], 1),
                jnp.concatenate([zero_block, (-sin_b).astype(jnp.bfloat16)], 1),
            ],
            0,
        )
        waves = row_ref[row]
        plain = jnp.where(north, waves[0:1, :], waves[1:2, :])
        crossed = jnp.where(north, waves[2:3, :], waves[3:4, :])
        spread = (plain * outer_cos + crossed * outer_sin).astype(jnp.bfloat16)
        images = lax.dot_general(
            spread, inner, (((1,), (0,)), ((), ())), preferred_element_type=jnp.float32
        )
        in_first = position < first
        occupied = position < first + second
        values = jnp.where(in_first, images[:, :LANES], jnp.where(occupied, images[:, LANES:], 0.0))
        values = values.astype(jnp.bfloat16)
        wide = values.astype(jnp.float32)
        squared = wide * wide
        by_cycle = jnp.concatenate(
            [
                jnp.where(in_first, squared, 0.0).astype(jnp.bfloat16),
                jnp.where(in_first, 0.0, squared).astype(jnp.bfloat16),
            ],
            1,
        )
        partial = lax.dot_general(
            by_cycle, inner, (((1,), (1,)), ((), ())), preferred_element_type=jnp.float32
        )
        cos_sum = jnp.sum((partial * outer_cos).reshape(ROWS_PAD // 8, 8, LANES), 0)
        sin_sum = jnp.sum((partial * outer_sin).reshape(ROWS_PAD // 8, 8, LANES), 0)
        total = cos_sum + sign * pltpu.roll(sin_sum, 64, 1)
        total = total + pltpu.roll(total, 4, 0)
        total = total + pltpu.roll(total, 2, 0)
        back_ref[row] = total * waves[4:5, :]
        return values

    @pl.loop(0, len_ref.shape[0] // 2)
    def _(pair):
        even = one_row(2 * pair)
        odd = one_row(2 * pair + 1)
        start = pl.multiple_of(pair * 2 * ROWS, 8)
        grid_ref[pl.ds(start, 2 * ROWS), :] = jnp.concatenate([even[:ROWS], odd[:ROWS]], 0)


def per_device(spec, legendre, gauss_w, cycle_len, wave_map):
    slots_dev = spec.shape[0]
    fields = spec.shape[1]
    degrees_all = spec.shape[3]
    slot_count = wave_map.shape[0]
    orders = wave_map * degrees_all // slot_count
    wave_pos = lax.axis_index("wave")
    own_orders = lax.dynamic_slice_in_dim(orders, wave_pos * slots_dev, slots_dev)
    degrees = jnp.arange(degrees_all, dtype=jnp.int32)
    retained = degrees[None, :] >= own_orders[:, None]
    coefficients = jnp.where(retained[:, None, None, :], spec, jnp.zeros((), jnp.bfloat16))
    panels = lax.all_gather(legendre, "lev", axis=1, tiled=True)
    sign_flip = parity_of(degrees, own_orders)
    flipped = (coefficients.astype(jnp.float32) * sign_flip[:, None, None, :]).astype(jnp.bfloat16)
    stacked = jnp.stack([coefficients, flipped], 1)
    fourier = jnp.einsum(
        "shfcn,snq->shfcq", stacked, panels, preferred_element_type=jnp.float32
    ).astype(jnp.bfloat16)
    cycle_waves = lax.all_to_all(fourier, "wave", split_axis=4, concat_axis=0, tiled=True)
    local_lats = cycle_waves.shape[4]
    row_total = local_lats // 2
    lat_start = wave_pos * local_lats
    lens = lax.dynamic_slice_in_dim(cycle_len, lat_start, local_lats).reshape(row_total, 2)
    weights = lax.dynamic_slice_in_dim(gauss_w, lat_start, local_lats).reshape(row_total, 2)
    double = jnp.where(orders == 0, 1.0, 2.0)
    resolved = 2 * orders[None, None, :] < lens[:, :, None]
    widening = jnp.where(resolved, double[None, None, :], 0.0)
    waves = cycle_waves.reshape(slot_count, 2, 2, row_total, 2).transpose(3, 1, 2, 4, 0)
    waves = waves.astype(jnp.float32) * widening[:, None, None, :, :]
    crossed = jnp.stack([-waves[:, :, 1], waves[:, :, 0]], 2)
    factor = jnp.where(resolved, weights[:, :, None] / lens[:, :, None].astype(jnp.float32), 0.0)
    factor = jnp.broadcast_to(factor[:, None, None], (row_total, 1, 2, 2, slot_count))
    rows = jnp.concatenate([waves, crossed, factor, jnp.zeros((row_total, 3, 2, 2, slot_count), jnp.float32)], 1)
    spare = SLOT_PAD - slot_count
    rows = jnp.pad(rows, ((0, 0), (0, 0), (0, 0), (0, 0), (0, spare))).reshape(row_total, 8, LANES)
    padded_orders = jnp.pad(orders.astype(jnp.float32), (0, spare))
    order_lane = jnp.broadcast_to(jnp.tile(padded_orders, 4)[None, :], (8, LANES))
    order_sub = jnp.broadcast_to(padded_orders[:, None], (SLOT_PAD, LANES))
    inverse = 1.0 / lens.astype(jnp.float32)
    smem = pl.BlockSpec(memory_space=pltpu.SMEM)
    vmem = pl.BlockSpec(memory_space=pltpu.VMEM)
    values, back = pl.pallas_call(
        grid_kernel,
        out_shape=(
            jax.ShapeDtypeStruct((row_total * ROWS, LANES), jnp.bfloat16),
            jax.ShapeDtypeStruct((row_total, 8, LANES), jnp.float32),
        ),
        in_specs=[smem, smem, vmem, vmem, vmem],
        out_specs=(vmem, vmem),
        name="cycles",
    )(lens, inverse, order_lane, order_sub, rows)
    grid = values.reshape(row_total, BLOCKS, 2, LANES).transpose(2, 0, 1, 3)
    grid = grid.reshape(2, row_total, 1, LPAD)
    returned = back[:, :2].reshape(row_total, 2, 2, 2, SLOT_PAD)[..., :slot_count].astype(jnp.bfloat16)
    returned = returned.transpose(4, 1, 2, 0, 3).reshape(slot_count, 2, fields, 2, local_lats)
    spectral = lax.all_to_all(returned, "wave", split_axis=0, concat_axis=4, tiled=True)
    both = jnp.einsum("shfcq,snq->shfcn", spectral, panels, preferred_element_type=jnp.float32)
    total = both[:, 0] + sign_flip[:, None, None, :] * both[:, 1]
    spec_out = jnp.where(retained[:, None, None, :], total, 0.0)
    return (grid, spec_out)


def solution(mesh):
    placed = (P("wave", "lev", None, None), P("wave", "lev", None), P(), P(), P())
    return jax.shard_map(
        per_device,
        mesh=mesh,
        in_specs=placed,
        out_specs=(P(None, "wave", "lev", None), P("wave", "lev", None, None)),
        check_vma=False,
    )
```

```python
import math

import jax
import jax.numpy as jnp
import numpy as np
from jax import lax
from jax.experimental import pallas as pl
from jax.experimental.pallas import tpu as pltpu
from jax.sharding import PartitionSpec as P

LPAD = 4864
LANES = 128
BLOCKS = LPAD // LANES
ROWS = 2 * BLOCKS
ROWS_PAD = 80
SLOT_PAD = 32
CYCLE_PAD = 64
WAVES = 12
LINES = 8
LEAF = 8
LATS = WAVES * LANES
MESH = pl.DeviceIdType.MESH
NT = (((1,), (1,)), ((), ()))


def cos_sin_turns(turns):
    quarter = turns * 4.0
    whole = jnp.round(quarter)
    rest = (quarter - whole) * (0.5 * math.pi)
    square = rest * rest
    sine = rest + rest * square * (
        -1.6666666666e-1 + square * (8.3333331e-3 + square * (-1.98412698e-4 + square * 2.7557319e-6))
    )
    cosine = 1.0 + square * (
        -0.5 + square * (4.16666667e-2 + square * (-1.388888889e-3 + square * (2.48015873e-5 - square * 2.7557319e-7)))
    )
    step = whole.astype(jnp.int32) & 3
    swap = (step & 1) == 1
    cos_base = jnp.where(swap, sine, cosine)
    sin_base = jnp.where(swap, cosine, sine)
    cos_value = jnp.where((step == 1) | (step == 2), -cos_base, cos_base)
    sin_value = jnp.where(step >= 2, -sin_base, sin_base)
    return cos_value, sin_value


def turns_of(product, length, inverse):
    whole = jnp.round(product * inverse)
    return (product - whole * length) * inverse


def where_am_i():
    wave = lax.axis_index("wave")
    lev = lax.axis_index("lev")
    line = lax.div(lev, LEAF)
    leaf = lax.rem(lev, LEAF)
    return wave, lev, line, leaf


def remote(source, target, send, receive, device):
    return pltpu.make_async_remote_copy(
        src_ref=source, dst_ref=target, send_sem=send, recv_sem=receive,
        device_id=device, device_id_type=MESH,
    )


def greet(devices):
    barrier = pltpu.get_barrier_semaphore()
    for device in devices:
        pl.semaphore_signal(barrier, inc=1, device_id=device, device_id_type=MESH)
    pl.semaphore_wait(barrier, len(devices))


def front_kernel(
    leg_ref, coef_ref, panel_ref, waves_ref, lhs, part, got, four,
    local_sem, chip_send, chip_recv, core_send, core_recv, coef_send, coef_recv,
    part_send, part_recv, wave_send, wave_recv,
):
    wave, lev, line, leaf = where_am_i()
    core = lax.rem(leaf, 2)
    chip = lax.div(leaf, 2)
    sibling = {"lev": lev + 1 - 2 * core}
    chips = [{"lev": line * LEAF + lax.rem(chip + d, 4) * 2 + core} for d in range(1, 4)]
    lines = [{"lev": lax.rem(line + d, LINES) * LEAF + leaf} for d in range(1, LINES)]
    waves = [{"wave": lax.rem(wave + d, WAVES)} for d in range(1, WAVES)]
    greet([sibling] + chips + lines + waves)

    copies = []
    for d in range(1, 4):
        copy = remote(leg_ref, panel_ref.at[leaf], chip_send.at[d - 1], chip_recv.at[d - 1], chips[d - 1])
        copy.start()
        copies.append(copy)
    for d in range(1, LINES):
        target = lax.rem(line + d, LINES)
        copy = remote(coef_ref.at[target], lhs.at[line], coef_send.at[d - 1], coef_recv.at[d - 1], lines[d - 1])
        copy.start()
        copies.append(copy)
    copy = remote(leg_ref, panel_ref.at[leaf], core_send.at[0], core_recv.at[0], sibling)
    copy.start()
    copies.append(copy)
    own_panel = pltpu.make_async_copy(leg_ref, panel_ref.at[leaf], local_sem.at[0])
    own_panel.start()
    own_coef = pltpu.make_async_copy(coef_ref.at[line], lhs.at[line], local_sem.at[1])
    own_coef.start()
    for d in range(1, 4):
        origin = lax.rem(chip + 4 - d, 4) * 2 + core
        block = panel_ref.at[origin]
        remote(block, block, chip_send.at[d - 1], chip_recv.at[d - 1], chips[d - 1]).wait_recv()
        copy = remote(block, block, core_send.at[d], core_recv.at[d], sibling)
        copy.start()
        copies.append(copy)
    own_panel.wait()
    own_coef.wait()
    for d in range(4):
        origin = lax.rem(chip + 4 - d, 4) * 2 + 1 - core
        block = panel_ref.at[origin]
        remote(block, block, core_send.at[d], core_recv.at[d], sibling).wait_recv()
    for d in range(1, LINES):
        block = lhs.at[lax.rem(line + LINES - d, LINES)]
        remote(block, block, coef_send.at[d - 1], coef_recv.at[d - 1], lines[d - 1]).wait_recv()

    depth = panel_ref.shape[1]
    panel = panel_ref[...].reshape(LEAF * depth, LATS)
    product = jnp.dot(
        lhs[...].reshape(LINES * 8, LEAF * depth), panel, preferred_element_type=jnp.float32
    )
    part[...] = product.reshape(LINES, 8, LATS)
    for d in range(1, LINES):
        target = lax.rem(line + d, LINES)
        copy = remote(part.at[target], got.at[d - 1], part_send.at[d - 1], part_recv.at[d - 1], lines[d - 1])
        copy.start()
        copies.append(copy)
    total = part[line]
    for d in range(1, LINES):
        block = got.at[d - 1]
        remote(block, block, part_send.at[d - 1], part_recv.at[d - 1], lines[d - 1]).wait_recv()
        total = total + got[d - 1]
    for w in range(WAVES):
        four[w] = total[:, w * LANES : (w + 1) * LANES].astype(jnp.bfloat16)
    for d in range(1, WAVES):
        target = lax.rem(wave + d, WAVES)
        copy = remote(four.at[target], waves_ref.at[wave], wave_send.at[d - 1], wave_recv.at[d - 1], waves[d - 1])
        copy.start()
        copies.append(copy)
    own_wave = pltpu.make_async_copy(four.at[wave], waves_ref.at[wave], local_sem.at[2])
    own_wave.start()
    own_wave.wait()
    for d in range(1, WAVES):
        block = waves_ref.at[lax.rem(wave + WAVES - d, WAVES)]
        remote(block, block, wave_send.at[d - 1], wave_recv.at[d - 1], waves[d - 1]).wait_recv()
    for copy in copies:
        copy.wait_send()


def back_kernel(
    ret_ref, panel_ref, out_ref, here, fields, part,
    local_sem, wave_send, wave_recv, line_send, line_recv, part_send, part_recv,
):
    wave, lev, line, leaf = where_am_i()
    lines = [{"lev": lax.rem(line + d, LINES) * LEAF + leaf} for d in range(1, LINES)]
    waves = [{"wave": lax.rem(wave + d, WAVES)} for d in range(1, WAVES)]
    greet(lines + waves)
    copies = []
    for d in range(1, WAVES):
        target = lax.rem(wave + d, WAVES)
        copy = remote(ret_ref.at[target], here.at[wave], wave_send.at[d - 1], wave_recv.at[d - 1], waves[d - 1])
        copy.start()
        copies.append(copy)
    own_wave = pltpu.make_async_copy(ret_ref.at[wave], here.at[wave], local_sem.at[0])
    own_wave.start()
    own_wave.wait()
    for d in range(1, WAVES):
        block = here.at[lax.rem(wave + WAVES - d, WAVES)]
        remote(block, block, wave_send.at[d - 1], wave_recv.at[d - 1], waves[d - 1]).wait_recv()
    for d in range(1, LINES):
        copy = remote(here, fields.at[line], line_send.at[d - 1], line_recv.at[d - 1], lines[d - 1])
        copy.start()
        copies.append(copy)
    own_line = pltpu.make_async_copy(here, fields.at[line], local_sem.at[1])
    own_line.start()
    own_line.wait()
    for d in range(1, LINES):
        block = fields.at[lax.rem(line + LINES - d, LINES)]
        remote(block, block, line_send.at[d - 1], line_recv.at[d - 1], lines[d - 1]).wait_recv()
    depth = panel_ref.shape[1]
    panel = panel_ref[...].reshape(LEAF * depth, LATS)
    lhs = jnp.concatenate([fields[:, w].reshape(LINES * 8, LANES) for w in range(WAVES)], 1)
    product = lax.dot_general(lhs, panel, NT, preferred_element_type=jnp.float32)
    part[...] = product.reshape(LINES, 8, LEAF * depth)
    for d in range(1, LINES):
        target = lax.rem(line + d, LINES)
        copy = remote(part.at[target], out_ref.at[line], part_send.at[d - 1], part_recv.at[d - 1], lines[d - 1])
        copy.start()
        copies.append(copy)
    own_part = pltpu.make_async_copy(part.at[line], out_ref.at[line], local_sem.at[2])
    own_part.start()
    own_part.wait()
    for d in range(1, LINES):
        block = out_ref.at[lax.rem(line + LINES - d, LINES)]
        remote(block, block, part_send.at[d - 1], part_recv.at[d - 1], lines[d - 1]).wait_recv()
    for copy in copies:
        copy.wait_send()


def grid_kernel(
    len_ref, inv_ref, order_lane_ref, order_sub_ref, keep_ref, factor_ref, wave_ref, spread_ref, gather_ref,
    grid_ref, ret_ref, plain_ref, cross_ref, sum_ref,
):
    lane_f = lax.broadcasted_iota(jnp.int32, (ROWS_PAD, LANES), 1)
    row_f = lax.broadcasted_iota(jnp.int32, (ROWS_PAD, LANES), 0)
    block_start = (row_f // 2) * LANES
    position = block_start + lane_f
    block_start = block_start.astype(jnp.float32)
    second_lane = (lax.broadcasted_iota(jnp.int32, (1, LANES), 1) // SLOT_PAD) % 2 == 1
    sign = jnp.where(lax.broadcasted_iota(jnp.int32, (1, LANES), 1) < 64, 1.0, -1.0)
    order_lane = order_lane_ref[0:1, :]
    inner_lane = lax.broadcasted_iota(jnp.int32, (SLOT_PAD, LANES), 1).astype(jnp.float32)
    inner_product = order_sub_ref[...] * inner_lane
    north = (lax.broadcasted_iota(jnp.int32, (ROWS_PAD, LANES), 0) % 2) == 0
    arrived = wave_ref[...].reshape(WAVES * 8, LANES)
    turned = lax.dot_general(
        arrived, spread_ref[...], (((0,), (0,)), ((), ())), preferred_element_type=jnp.float32
    )
    for h in range(2):
        part = turned[:, h * LANES : (h + 1) * LANES]
        part = jnp.where(second_lane, part[CYCLE_PAD:], part[:CYCLE_PAD]) * keep_ref[...]
        plain_ref[h] = part
        cross_ref[h] = -sign * pltpu.roll(part, 64, 1)
    sum_ref[...] = jnp.zeros_like(sum_ref)
    zero_block = jnp.zeros((SLOT_PAD, LANES), jnp.bfloat16)

    def one_row(row):
        first = len_ref[row, 0]
        second = len_ref[row, 1]
        first_f = first.astype(jnp.float32)
        second_f = second.astype(jnp.float32)
        inv_first = inv_ref[row, 0]
        inv_second = inv_ref[row, 1]
        length_lane = jnp.where(second_lane, second_f, first_f)
        inverse_lane = jnp.where(second_lane, inv_second, inv_first)
        start_lane = jnp.where(second_lane, first_f, 0.0)
        outer = order_lane * (block_start - start_lane)
        outer_cos, outer_sin = cos_sin_turns(turns_of(outer, length_lane, inverse_lane))
        cos_a, sin_a = cos_sin_turns(turns_of(inner_product, first_f, inv_first))
        cos_b, sin_b = cos_sin_turns(turns_of(inner_product, second_f, inv_second))
        inner = jnp.concatenate(
            [
                jnp.concatenate([cos_a.astype(jnp.bfloat16), zero_block], 1),
                jnp.concatenate([zero_block, cos_b.astype(jnp.bfloat16)], 1),
                jnp.concatenate([(-sin_a).astype(jnp.bfloat16), zero_block], 1),
                jnp.concatenate([zero_block, (-sin_b).astype(jnp.bfloat16)], 1),
            ],
            0,
        )
        plain = jnp.where(north, plain_ref[0, pl.ds(row, 1), :], plain_ref[1, pl.ds(row, 1), :])
        crossed = jnp.where(north, cross_ref[0, pl.ds(row, 1), :], cross_ref[1, pl.ds(row, 1), :])
        spread = (plain * outer_cos + crossed * outer_sin).astype(jnp.bfloat16)
        images = lax.dot_general(
            spread, inner, (((1,), (0,)), ((), ())), preferred_element_type=jnp.float32
        )
        in_first = position < first
        occupied = position < first + second
        values = jnp.where(in_first, images[:, :LANES], jnp.where(occupied, images[:, LANES:], 0.0))
        values = values.astype(jnp.bfloat16)
        wide = values.astype(jnp.float32)
        squared = wide * wide
        by_cycle = jnp.concatenate(
            [
                jnp.where(in_first, squared, 0.0).astype(jnp.bfloat16),
                jnp.where(in_first, 0.0, squared).astype(jnp.bfloat16),
            ],
            1,
        )
        partial = lax.dot_general(
            by_cycle, inner, (((1,), (1,)), ((), ())), preferred_element_type=jnp.float32
        )
        cos_sum = jnp.sum((partial * outer_cos).reshape(ROWS_PAD // 8, 8, LANES), 0)
        sin_sum = jnp.sum((partial * outer_sin).reshape(ROWS_PAD // 8, 8, LANES), 0)
        total = cos_sum + sign * pltpu.roll(sin_sum, 64, 1)
        total = total + pltpu.roll(total, 4, 0)
        total = total + pltpu.roll(total, 2, 0)
        sum_ref[0, pl.ds(row, 1), :] = total[0:1, :]
        sum_ref[1, pl.ds(row, 1), :] = total[1:2, :]
        return values

    @pl.loop(0, len_ref.shape[0] // 2)
    def _(pair):
        even = one_row(2 * pair)
        odd = one_row(2 * pair + 1)
        start = pl.multiple_of(pair * 2 * ROWS, 8)
        grid_ref[pl.ds(start, 2 * ROWS), :] = jnp.concatenate([even[:ROWS], odd[:ROWS]], 0)

    sums = jnp.concatenate([sum_ref[0] * factor_ref[...], sum_ref[1] * factor_ref[...]], 1).astype(jnp.bfloat16)
    returned = jnp.concatenate(
        [
            lax.dot_general(gather_ref[cycle], sums, NT, preferred_element_type=jnp.float32)
            for cycle in range(2)
        ],
        1,
    )
    ret_ref[...] = returned.astype(jnp.bfloat16).reshape(WAVES, 8, LANES)

def per_device(spec, legendre, gauss_w, cycle_len, wave_map):
    slots_dev, _, _, degrees_all = spec.shape
    depth = legendre.shape[1]
    slot_count = wave_map.shape[0]
    orders = wave_map * degrees_all // slot_count
    wave_pos = lax.axis_index("wave")
    own_orders = lax.dynamic_slice_in_dim(orders, wave_pos * slots_dev, slots_dev)
    degrees = jnp.arange(degrees_all, dtype=jnp.int32)
    local_lats = cycle_len.shape[0] // WAVES
    row_total = local_lats // 2
    spare = SLOT_PAD - slot_count

    panel = legendre.transpose(1, 0, 2).reshape(depth * slots_dev, WAVES, row_total, 2).transpose(0, 1, 3, 2)
    panel = jnp.pad(panel, ((0, 0), (0, 0), (0, 0), (0, CYCLE_PAD - row_total))).reshape(depth * slots_dev, LATS)

    retained = degrees[None, :] >= own_orders[:, None]
    odd = (degrees[None, :] + own_orders[:, None]) % 2 == 1
    coefficients = jnp.where(retained[:, None, :], spec[:, 0], jnp.zeros((), jnp.bfloat16))
    flipped = jnp.where(odd[:, None, :], -coefficients, coefficients)
    stacked = jnp.stack([coefficients, flipped], 1).reshape(slots_dev, 4, LINES, degrees_all // LINES, 1)
    same = jnp.arange(slots_dev)[:, None, None, None, None] == jnp.arange(slots_dev)
    coef = jnp.where(same, stacked, jnp.zeros((), jnp.bfloat16)).transpose(2, 0, 1, 3, 4)
    coef = coef.reshape(LINES, 8, degrees_all // LINES * slots_dev)

    vmem = pl.BlockSpec(memory_space=pltpu.VMEM)
    smem = pl.BlockSpec(memory_space=pltpu.SMEM)
    dma = pltpu.SemaphoreType.DMA
    width = LEAF * depth * slots_dev
    panels, arrived = pl.pallas_call(
        front_kernel,
        out_shape=(
            jax.ShapeDtypeStruct((LEAF, depth * slots_dev, LATS), jnp.bfloat16),
            jax.ShapeDtypeStruct((WAVES, 8, LANES), jnp.bfloat16),
        ),
        in_specs=[vmem, vmem],
        out_specs=(vmem, vmem),
        scratch_shapes=[
            pltpu.VMEM((LINES, 8, width), jnp.bfloat16),
            pltpu.VMEM((LINES, 8, LATS), jnp.float32),
            pltpu.VMEM((LINES - 1, 8, LATS), jnp.float32),
            pltpu.VMEM((WAVES, 8, LANES), jnp.bfloat16),
            dma((3,)), dma((3,)), dma((3,)), dma((4,)), dma((4,)),
            dma((LINES - 1,)), dma((LINES - 1,)), dma((LINES - 1,)), dma((LINES - 1,)),
            dma((WAVES - 1,)), dma((WAVES - 1,)),
        ],
        compiler_params=pltpu.CompilerParams(collective_id=0, has_side_effects=True),
        name="front",
    )(panel, coef)

    lat_start = wave_pos * local_lats
    lens = lax.dynamic_slice_in_dim(cycle_len, lat_start, local_lats).reshape(row_total, 2)
    weights = lax.dynamic_slice_in_dim(gauss_w, lat_start, local_lats).reshape(row_total, 2)
    inverse = 1.0 / lens.astype(jnp.float32)
    lane = jnp.arange(LANES)
    lane_slot = lane % SLOT_PAD
    lane_cycle = lane // SLOT_PAD % 2
    padded = jnp.pad(orders, (0, spare))
    order_lane = jnp.tile(padded, 4)
    lens_lane = jnp.where(lane_cycle[None, :] == 1, lens[:, 1:2], lens[:, 0:1])
    weights_lane = jnp.where(lane_cycle[None, :] == 1, weights[:, 1:2], weights[:, 0:1])
    resolved = (2 * order_lane[None, :] < lens_lane) & (lane_slot < slot_count)[None, :]
    double = jnp.where(order_lane == 0, 1.0, 2.0)
    fill = ((0, CYCLE_PAD - row_total), (0, 0))
    keep = jnp.pad(jnp.where(resolved, double[None, :], 0.0), fill)
    factor = jnp.pad(jnp.where(resolved, weights_lane / lens_lane.astype(jnp.float32), 0.0), fill)
    order_lane = jnp.broadcast_to(order_lane.astype(jnp.float32)[None, :], (8, LANES))
    order_sub = jnp.broadcast_to(padded.astype(jnp.float32)[:, None], (SLOT_PAD, LANES))

    line = np.arange(WAVES * 8)
    line_slot, line_half, line_part = line // 8 * 2 + line % 8 // 4, line // 2 % 2, line % 2
    both = np.arange(2 * LANES)
    both_half, both_part, both_cycle, both_slot = both // LANES, both // 64 % 2, both // 32 % 2, both % 32
    match = (
        (line_slot[:, None] == both_slot) & (line_half[:, None] == both_half) & (line_part[:, None] == both_part)
    )
    spread = jnp.asarray(match, jnp.bfloat16)
    gather = jnp.asarray(np.stack([match & (both_cycle == 0), match & (both_cycle == 1)]), jnp.bfloat16)

    values, returned = pl.pallas_call(
        grid_kernel,
        out_shape=(
            jax.ShapeDtypeStruct((row_total * ROWS, LANES), jnp.bfloat16),
            jax.ShapeDtypeStruct((WAVES, 8, LANES), jnp.bfloat16),
        ),
        in_specs=[smem, smem] + [vmem] * 7,
        out_specs=(vmem, vmem),
        scratch_shapes=[pltpu.VMEM((2, CYCLE_PAD, LANES), jnp.float32)] * 3,
        name="cycles",
    )(lens, inverse, order_lane, order_sub, keep, factor, arrived, spread, gather)
    grid = values.reshape(row_total, BLOCKS, 2, LANES).transpose(2, 0, 1, 3)
    grid = grid.reshape(2, row_total, 1, LPAD)

    blocks = pl.pallas_call(
        back_kernel,
        out_shape=jax.ShapeDtypeStruct((LINES, 8, width), jnp.float32),
        in_specs=[vmem, vmem],
        out_specs=vmem,
        scratch_shapes=[
            pltpu.VMEM((WAVES, 8, LANES), jnp.bfloat16),
            pltpu.VMEM((LINES, WAVES, 8, LANES), jnp.bfloat16),
            pltpu.VMEM((LINES, 8, width), jnp.float32),
            dma((3,)), dma((WAVES - 1,)), dma((WAVES - 1,)),
            dma((LINES - 1,)), dma((LINES - 1,)), dma((LINES - 1,)), dma((LINES - 1,)),
        ],
        compiler_params=pltpu.CompilerParams(collective_id=1, has_side_effects=True),
        name="back",
    )(returned, panels)
    blocks = blocks.reshape(LINES, slots_dev, 2, 2, degrees_all // LINES, slots_dev)
    sign_flip = jnp.where(odd, -1.0, 1.0).reshape(slots_dev, 1, LINES, degrees_all // LINES)
    mine = jnp.stack([blocks[:, s, :, :, :, s] for s in range(slots_dev)]).transpose(0, 2, 3, 1, 4)
    total = mine[:, 0] + sign_flip * mine[:, 1]
    total = total.reshape(slots_dev, 1, 2, degrees_all)
    spec_out = jnp.where(retained[:, None, None, :], total, 0.0)
    return (grid, spec_out)


def solution(mesh):
    placed = (P("wave", "lev", None, None), P("wave", "lev", None), P(), P(), P())
    return jax.shard_map(
        per_device,
        mesh=mesh,
        in_specs=placed,
        out_specs=(P(None, "wave", "lev", None), P("wave", "lev", None, None)),
        check_vma=False,
    )
```

```python
import math

import jax
import jax.numpy as jnp
import numpy as np
from jax import lax
from jax.experimental import pallas as pl
from jax.experimental.pallas import tpu as pltpu
from jax.sharding import PartitionSpec as P

LPAD = 4864
LANES = 128
BLOCKS = LPAD // LANES
ROWS = 2 * BLOCKS
ROWS_PAD = 80
SLOT_PAD = 32
CYCLE_PAD = 64
WAVES = 12
LINES = 8
LEAF = 8
LATS = 1200
OWN = LATS // WAVES
DEGREES = 1280
SPAN = DEGREES // LINES
SLOTS = 24
MESH = pl.DeviceIdType.MESH
NT = (((1,), (1,)), ((), ()))


def cos_sin_turns(turns):
    quarter = turns * 4.0
    whole = jnp.round(quarter)
    rest = (quarter - whole) * (0.5 * math.pi)
    square = rest * rest
    sine = rest + rest * square * (
        -1.6666666666e-1 + square * (8.3333331e-3 + square * (-1.98412698e-4 + square * 2.7557319e-6))
    )
    cosine = 1.0 + square * (
        -0.5 + square * (4.16666667e-2 + square * (-1.388888889e-3 + square * (2.48015873e-5 - square * 2.7557319e-7)))
    )
    step = whole.astype(jnp.int32) & 3
    swap = (step & 1) == 1
    cos_base = jnp.where(swap, sine, cosine)
    sin_base = jnp.where(swap, cosine, sine)
    cos_value = jnp.where((step == 1) | (step == 2), -cos_base, cos_base)
    sin_value = jnp.where(step >= 2, -sin_base, sin_base)
    return cos_value, sin_value


def turns_of(product, length, inverse):
    whole = jnp.round(product * inverse)
    return (product - whole * length) * inverse


def where_am_i():
    wave = lax.axis_index("wave")
    lev = lax.axis_index("lev")
    line = lax.div(lev, LEAF)
    leaf = lax.rem(lev, LEAF)
    return wave, lev, line, leaf


def remote(source, target, send, receive, device):
    return pltpu.make_async_remote_copy(
        src_ref=source, dst_ref=target, send_sem=send, recv_sem=receive,
        device_id=device, device_id_type=MESH,
    )


def order_of(map_ref, wave, slot):
    return map_ref[wave * 2 + slot] * DEGREES // SLOTS


def greet(devices):
    barrier = pltpu.get_barrier_semaphore()
    for device in devices:
        pl.semaphore_signal(barrier, inc=1, device_id=device, device_id_type=MESH)
    pl.semaphore_wait(barrier, len(devices))


def front_kernel(
    map_ref, leg_ref, spec_ref, panel_ref, waves_ref, lhs, part, got, four,
    local_sem, chip_send, chip_recv, core_send, core_recv, coef_send, coef_recv,
    part_send, part_recv, wave_send, wave_recv,
):
    wave, lev, line, leaf = where_am_i()
    core = lax.rem(leaf, 2)
    chip = lax.div(leaf, 2)
    sibling = {"lev": lev + 1 - 2 * core}
    chips = [{"lev": line * LEAF + lax.rem(chip + d, 4) * 2 + core} for d in range(1, 4)]
    lines = [{"lev": lax.rem(line + d, LINES) * LEAF + leaf} for d in range(1, LINES)]
    waves = [{"wave": lax.rem(wave + d, WAVES)} for d in range(1, WAVES)]
    greet([sibling] + chips + lines + waves)

    copies = []
    for d in range(1, 4):
        copy = remote(leg_ref, panel_ref.at[leaf], chip_send.at[d - 1], chip_recv.at[d - 1], chips[d - 1])
        copy.start()
        copies.append(copy)
    for d in range(1, LINES):
        copy = remote(spec_ref, lhs.at[line], coef_send.at[d - 1], coef_recv.at[d - 1], lines[d - 1])
        copy.start()
        copies.append(copy)
    copy = remote(leg_ref, panel_ref.at[leaf], core_send.at[0], core_recv.at[0], sibling)
    copy.start()
    copies.append(copy)
    own_panel = pltpu.make_async_copy(leg_ref, panel_ref.at[leaf], local_sem.at[0])
    own_panel.start()
    own_coef = pltpu.make_async_copy(spec_ref, lhs.at[line], local_sem.at[1])
    own_coef.start()
    width = panel_ref.shape[0] * panel_ref.shape[1]
    picked = lax.broadcasted_iota(jnp.int32, (DEGREES, width), 0) - line * SPAN
    widen = jnp.where(picked == lax.broadcasted_iota(jnp.int32, (DEGREES, width), 1) // 2, 1.0, 0.0)
    widen = widen.astype(jnp.bfloat16)
    four[...] = jnp.zeros_like(four)
    own_coef.wait()
    for d in range(1, LINES):
        block = lhs.at[lax.rem(line + LINES - d, LINES)]
        remote(block, block, coef_send.at[d - 1], coef_recv.at[d - 1], lines[d - 1]).wait_recv()
    coef = jnp.dot(lhs[...].reshape(LINES * 8, DEGREES), widen, preferred_element_type=jnp.float32)
    kind = lax.broadcasted_iota(jnp.int32, coef.shape, 0) % 8
    column = lax.broadcasted_iota(jnp.int32, coef.shape, 1)
    degree = column // 2 + line * SPAN
    order = jnp.where(kind >= 4, order_of(map_ref, wave, 1), order_of(map_ref, wave, 0))
    coef = jnp.where((kind // 4 == column % 2) & (degree >= order), coef, 0.0)
    coef = jnp.where((kind // 2 % 2 == 1) & ((degree + order) % 2 == 1), -coef, coef)
    coef = coef.astype(jnp.bfloat16)
    for d in range(1, 4):
        origin = lax.rem(chip + 4 - d, 4) * 2 + core
        block = panel_ref.at[origin]
        remote(block, block, chip_send.at[d - 1], chip_recv.at[d - 1], chips[d - 1]).wait_recv()
        copy = remote(block, block, core_send.at[d], core_recv.at[d], sibling)
        copy.start()
        copies.append(copy)
    own_panel.wait()
    for d in range(4):
        origin = lax.rem(chip + 4 - d, 4) * 2 + 1 - core
        block = panel_ref.at[origin]
        remote(block, block, core_send.at[d], core_recv.at[d], sibling).wait_recv()
    product = jnp.dot(coef, panel_ref[...].reshape(width, LATS), preferred_element_type=jnp.float32)
    part[...] = product.reshape(LINES, 8, LATS)
    for d in range(1, LINES):
        target = lax.rem(line + d, LINES)
        copy = remote(part.at[target], got.at[d - 1], part_send.at[d - 1], part_recv.at[d - 1], lines[d - 1])
        copy.start()
        copies.append(copy)
    total = part[line]
    for d in range(1, LINES):
        block = got.at[d - 1]
        remote(block, block, part_send.at[d - 1], part_recv.at[d - 1], lines[d - 1]).wait_recv()
        total = total + got[d - 1]
    for w in range(WAVES):
        four[w, :, :OWN] = total[:, w * OWN : (w + 1) * OWN].astype(jnp.bfloat16)
    for d in range(1, WAVES):
        target = lax.rem(wave + d, WAVES)
        copy = remote(four.at[target], waves_ref.at[wave], wave_send.at[d - 1], wave_recv.at[d - 1], waves[d - 1])
        copy.start()
        copies.append(copy)
    own_wave = pltpu.make_async_copy(four.at[wave], waves_ref.at[wave], local_sem.at[2])
    own_wave.start()
    own_wave.wait()
    for d in range(1, WAVES):
        block = waves_ref.at[lax.rem(wave + WAVES - d, WAVES)]
        remote(block, block, wave_send.at[d - 1], wave_recv.at[d - 1], waves[d - 1]).wait_recv()
    for copy in copies:
        copy.wait_send()


def back_kernel(
    map_ref, ret_ref, panel_ref, out_ref, here, fields, part, final,
    local_sem, wave_send, wave_recv, line_send, line_recv, part_send, part_recv,
):
    wave, lev, line, leaf = where_am_i()
    lines = [{"lev": lax.rem(line + d, LINES) * LEAF + leaf} for d in range(1, LINES)]
    waves = [{"wave": lax.rem(wave + d, WAVES)} for d in range(1, WAVES)]
    greet(lines + waves)
    copies = []
    for d in range(1, WAVES):
        target = lax.rem(wave + d, WAVES)
        copy = remote(ret_ref.at[target], here.at[wave], wave_send.at[d - 1], wave_recv.at[d - 1], waves[d - 1])
        copy.start()
        copies.append(copy)
    own_wave = pltpu.make_async_copy(ret_ref.at[wave], here.at[wave], local_sem.at[0])
    own_wave.start()
    own_wave.wait()
    for d in range(1, WAVES):
        block = here.at[lax.rem(wave + WAVES - d, WAVES)]
        remote(block, block, wave_send.at[d - 1], wave_recv.at[d - 1], waves[d - 1]).wait_recv()
    for d in range(1, LINES):
        copy = remote(here, fields.at[line], line_send.at[d - 1], line_recv.at[d - 1], lines[d - 1])
        copy.start()
        copies.append(copy)
    own_line = pltpu.make_async_copy(here, fields.at[line], local_sem.at[1])
    own_line.start()
    own_line.wait()
    for d in range(1, LINES):
        block = fields.at[lax.rem(line + LINES - d, LINES)]
        remote(block, block, line_send.at[d - 1], line_recv.at[d - 1], lines[d - 1]).wait_recv()
    depth = panel_ref.shape[1]
    panel = panel_ref[...].reshape(LEAF * depth, LATS)
    lhs = jnp.concatenate(
        [fields[:, w].reshape(LINES * 8, LANES)[:, :OWN].astype(jnp.float32) for w in range(WAVES)], 1
    ).astype(jnp.bfloat16)
    product = lax.dot_general(lhs, panel, NT, preferred_element_type=jnp.float32)
    width = LEAF * depth
    kind = lax.broadcasted_iota(jnp.int32, product.shape, 0) % 8
    column = lax.broadcasted_iota(jnp.int32, product.shape, 1)
    order = jnp.where(kind >= 4, order_of(map_ref, wave, 1), order_of(map_ref, wave, 0))
    degree = column // 2 + line * SPAN
    product = jnp.where((kind // 4 == column % 2) & (degree >= order), product, 0.0)
    product = jnp.where((kind // 2 % 2 == 1) & ((degree + order) % 2 == 1), -product, product)
    narrow = lax.broadcasted_iota(jnp.int32, (width, SPAN), 0) // 2 == lax.broadcasted_iota(jnp.int32, (width, SPAN), 1)
    narrow = jnp.where(narrow, 1.0, 0.0)
    product = jnp.dot(
        product, narrow, precision=lax.Precision.HIGHEST, preferred_element_type=jnp.float32
    ).reshape(LINES, 8, SPAN)
    part[...] = product
    for d in range(1, LINES):
        target = lax.rem(line + d, LINES)
        copy = remote(part.at[target], final.at[line], part_send.at[d - 1], part_recv.at[d - 1], lines[d - 1])
        copy.start()
        copies.append(copy)
    own_part = pltpu.make_async_copy(part.at[line], final.at[line], local_sem.at[2])
    own_part.start()
    own_part.wait()
    for d in range(1, LINES):
        block = final.at[lax.rem(line + LINES - d, LINES)]
        remote(block, block, part_send.at[d - 1], part_recv.at[d - 1], lines[d - 1]).wait_recv()
    total = jnp.concatenate([final[y] for y in range(LINES)], 1)
    for s in range(2):
        out_ref[s] = total[4 * s : 4 * s + 2] + total[4 * s + 2 : 4 * s + 4]
    for copy in copies:
        copy.wait_send()


def grid_kernel(
    len_ref, weight_ref, order_ref, wave_ref, spread_ref, gather_ref, natural_ref,
    grid_ref, ret_ref, turned_ref, plain_ref, cross_ref, sum_ref,
):
    first_lat = lax.axis_index("wave") * OWN
    order_lane = order_ref[0:1, :]
    order_lane = order_lane + pltpu.roll(order_lane, 32, 1)
    order_lane = order_lane + pltpu.roll(order_lane, 64, 1)
    lane_slot = lax.broadcasted_iota(jnp.int32, (1, LANES), 1) % SLOT_PAD
    double = jnp.where(lane_slot < SLOTS, jnp.where(order_lane == 0.0, 1.0, 2.0), 0.0)
    order_sub = jnp.broadcast_to(order_lane, (LANES, LANES)).T[:SLOT_PAD]
    lane_f = lax.broadcasted_iota(jnp.int32, (ROWS_PAD, LANES), 1)
    row_f = lax.broadcasted_iota(jnp.int32, (ROWS_PAD, LANES), 0)
    block_start = (row_f // 2) * LANES
    position = block_start + lane_f
    block_start = block_start.astype(jnp.float32)
    second_lane = (lax.broadcasted_iota(jnp.int32, (1, LANES), 1) // SLOT_PAD) % 2 == 1
    sign = jnp.where(lax.broadcasted_iota(jnp.int32, (1, LANES), 1) < 64, 1.0, -1.0)
    inner_lane = lax.broadcasted_iota(jnp.int32, (SLOT_PAD, LANES), 1).astype(jnp.float32)
    inner_product = order_sub * inner_lane
    north = (lax.broadcasted_iota(jnp.int32, (ROWS_PAD, LANES), 0) % 2) == 0
    arrived = wave_ref[...].reshape(WAVES * 8, LANES)
    turned = lax.dot_general(
        arrived, spread_ref[...], (((0,), (0,)), ((), ())), preferred_element_type=jnp.float32
    )
    for h in range(2):
        turned_ref[...] = turned[:, h * LANES : (h + 1) * LANES]
        part = jnp.where(
            second_lane, turned_ref[pl.ds(1, CYCLE_PAD, 2), :], turned_ref[pl.ds(0, CYCLE_PAD, 2), :]
        )
        part = part * double
        plain_ref[h] = part
        cross_ref[h] = -sign * pltpu.roll(part, 64, 1)
    sum_ref[...] = jnp.zeros_like(sum_ref)
    zero_block = jnp.zeros((SLOT_PAD, LANES), jnp.bfloat16)

    def one_row(row):
        first = len_ref[first_lat + 2 * row]
        second = len_ref[first_lat + 2 * row + 1]
        first_f = first.astype(jnp.float32)
        second_f = second.astype(jnp.float32)
        length_lane = jnp.where(second_lane, second_f, first_f)
        start_lane = jnp.where(second_lane, first_f, 0.0)
        inverse_lane = 1.0 / length_lane
        inv_first = inverse_lane[:, 0:1]
        inv_second = inverse_lane[:, SLOT_PAD : SLOT_PAD + 1]
        weight_lane = jnp.where(
            second_lane, weight_ref[first_lat + 2 * row + 1], weight_ref[first_lat + 2 * row]
        )
        resolved = 2.0 * order_lane < length_lane
        factor = jnp.where(resolved, weight_lane * inverse_lane, 0.0)
        outer = order_lane * (block_start - start_lane)
        outer_cos, outer_sin = cos_sin_turns(turns_of(outer, length_lane, inverse_lane))
        cos_a, sin_a = cos_sin_turns(turns_of(inner_product, first_f, inv_first))
        cos_b, sin_b = cos_sin_turns(turns_of(inner_product, second_f, inv_second))
        inner = jnp.concatenate(
            [
                jnp.concatenate([cos_a.astype(jnp.bfloat16), zero_block], 1),
                jnp.concatenate([zero_block, cos_b.astype(jnp.bfloat16)], 1),
                jnp.concatenate([(-sin_a).astype(jnp.bfloat16), zero_block], 1),
                jnp.concatenate([zero_block, (-sin_b).astype(jnp.bfloat16)], 1),
            ],
            0,
        )
        plain = jnp.where(north, plain_ref[0, pl.ds(row, 1), :], plain_ref[1, pl.ds(row, 1), :])
        crossed = jnp.where(north, cross_ref[0, pl.ds(row, 1), :], cross_ref[1, pl.ds(row, 1), :])
        spread = jnp.where(resolved, plain * outer_cos + crossed * outer_sin, 0.0).astype(jnp.bfloat16)
        images = lax.dot_general(
            spread, inner, (((1,), (0,)), ((), ())), preferred_element_type=jnp.float32
        )
        in_first = position < first
        occupied = position < first + second
        values = jnp.where(in_first, images[:, :LANES], jnp.where(occupied, images[:, LANES:], 0.0))
        values = values.astype(jnp.bfloat16)
        wide = values.astype(jnp.float32)
        squared = wide * wide
        by_cycle = jnp.concatenate(
            [
                jnp.where(in_first, squared, 0.0).astype(jnp.bfloat16),
                jnp.where(in_first, 0.0, squared).astype(jnp.bfloat16),
            ],
            1,
        )
        partial = lax.dot_general(
            by_cycle, inner, (((1,), (1,)), ((), ())), preferred_element_type=jnp.float32
        )
        cos_sum = jnp.sum((partial * outer_cos).reshape(ROWS_PAD // 8, 8, LANES), 0)
        sin_sum = jnp.sum((partial * outer_sin).reshape(ROWS_PAD // 8, 8, LANES), 0)
        total = cos_sum + sign * pltpu.roll(sin_sum, 64, 1)
        total = total + pltpu.roll(total, 4, 0)
        total = total + pltpu.roll(total, 2, 0)
        sum_ref[0, pl.ds(row, 1), :] = total[0:1, :] * factor
        sum_ref[1, pl.ds(row, 1), :] = total[1:2, :] * factor
        return values

    @pl.loop(0, OWN // 4)
    def _(pair):
        even = one_row(2 * pair)
        odd = one_row(2 * pair + 1)
        start = pl.multiple_of(pair * 2 * ROWS, 8)
        grid_ref[pl.ds(start, 2 * ROWS), :] = jnp.concatenate([even[:ROWS], odd[:ROWS]], 0)

    sums = jnp.concatenate([sum_ref[0], sum_ref[1]], 1).astype(jnp.bfloat16)
    returned = jnp.concatenate(
        [
            lax.dot_general(gather_ref[cycle], sums, NT, preferred_element_type=jnp.float32)
            for cycle in range(2)
        ],
        1,
    )
    returned = jnp.dot(returned.astype(jnp.bfloat16), natural_ref[...], preferred_element_type=jnp.float32)
    ret_ref[...] = returned.astype(jnp.bfloat16).reshape(WAVES, 8, LANES)

def per_device(spec, legendre, gauss_w, cycle_len, wave_map):
    slots_dev = spec.shape[0]
    depth = legendre.shape[1]
    row_total = OWN // 2
    panel = legendre.transpose(1, 0, 2).reshape(depth * slots_dev, LATS)
    doubled = jnp.broadcast_to(spec, (slots_dev, 2, 2, DEGREES)).reshape(8, DEGREES)
    orders = (wave_map * DEGREES // SLOTS).astype(jnp.float32)
    orders = jnp.broadcast_to(jnp.pad(orders, (0, LANES - SLOTS))[None, :], (8, LANES))

    vmem = pl.BlockSpec(memory_space=pltpu.VMEM)
    smem = pl.BlockSpec(memory_space=pltpu.SMEM)
    dma = pltpu.SemaphoreType.DMA
    width = LEAF * depth * slots_dev
    panels, arrived = pl.pallas_call(
        front_kernel,
        out_shape=(
            jax.ShapeDtypeStruct((LEAF, depth * slots_dev, LATS), jnp.bfloat16),
            jax.ShapeDtypeStruct((WAVES, 8, LANES), jnp.bfloat16),
        ),
        in_specs=[smem, vmem, vmem],
        out_specs=(vmem, vmem),
        scratch_shapes=[
            pltpu.VMEM((LINES, 8, DEGREES), jnp.bfloat16),
            pltpu.VMEM((LINES, 8, LATS), jnp.float32),
            pltpu.VMEM((LINES - 1, 8, LATS), jnp.float32),
            pltpu.VMEM((WAVES, 8, LANES), jnp.bfloat16),
            dma((3,)), dma((3,)), dma((3,)), dma((4,)), dma((4,)),
            dma((LINES - 1,)), dma((LINES - 1,)), dma((LINES - 1,)), dma((LINES - 1,)),
            dma((WAVES - 1,)), dma((WAVES - 1,)),
        ],
        compiler_params=pltpu.CompilerParams(collective_id=0, has_side_effects=True),
        name="front",
    )(wave_map, panel, doubled)

    line = np.arange(WAVES * 8)
    line_slot, line_half, line_part = line // 8 * 2 + line % 8 // 4, line // 2 % 2, line % 2
    both = np.arange(2 * LANES)
    both_half, both_part, both_cycle, both_slot = both // LANES, both // 64 % 2, both // 32 % 2, both % 32
    match = (
        (line_slot[:, None] == both_slot) & (line_half[:, None] == both_half) & (line_part[:, None] == both_part)
    )
    spread = jnp.asarray(match, jnp.bfloat16)
    packed = np.arange(LANES)
    natural = (packed % CYCLE_PAD < row_total)[:, None] & (
        (packed % CYCLE_PAD * 2 + packed // CYCLE_PAD)[:, None] == packed[None, :]
    )
    natural = jnp.asarray(natural, jnp.bfloat16)
    gather = jnp.asarray(np.stack([match & (both_cycle == 0), match & (both_cycle == 1)]), jnp.bfloat16)

    values, returned = pl.pallas_call(
        grid_kernel,
        out_shape=(
            jax.ShapeDtypeStruct((row_total * ROWS, LANES), jnp.bfloat16),
            jax.ShapeDtypeStruct((WAVES, 8, LANES), jnp.bfloat16),
        ),
        in_specs=[smem, smem] + [vmem] * 5,
        out_specs=(vmem, vmem),
        scratch_shapes=[pltpu.VMEM((LANES, LANES), jnp.float32)] + [pltpu.VMEM((2, CYCLE_PAD, LANES), jnp.float32)] * 3,
        name="cycles",
    )(cycle_len, gauss_w, orders, arrived, spread, gather, natural)
    grid = values.reshape(row_total, BLOCKS, 2, LANES).transpose(2, 0, 1, 3)
    grid = grid.reshape(2, row_total, 1, LPAD)

    spec_out = pl.pallas_call(
        back_kernel,
        out_shape=jax.ShapeDtypeStruct((slots_dev, 2, DEGREES), jnp.float32),
        in_specs=[smem, vmem, vmem],
        out_specs=vmem,
        scratch_shapes=[
            pltpu.VMEM((WAVES, 8, LANES), jnp.bfloat16),
            pltpu.VMEM((LINES, WAVES, 8, LANES), jnp.bfloat16),
            pltpu.VMEM((LINES, 8, SPAN), jnp.float32),
            pltpu.VMEM((LINES, 8, SPAN), jnp.float32),
            dma((3,)), dma((WAVES - 1,)), dma((WAVES - 1,)),
            dma((LINES - 1,)), dma((LINES - 1,)), dma((LINES - 1,)), dma((LINES - 1,)),
        ],
        compiler_params=pltpu.CompilerParams(collective_id=1, has_side_effects=True),
        name="back",
    )(wave_map, returned, panels)
    spec_out = spec_out.reshape(slots_dev, 1, 2, DEGREES)
    return (grid, spec_out)


def solution(mesh):
    placed = (P("wave", "lev", None, None), P("wave", "lev", None), P(), P(), P())
    return jax.shard_map(
        per_device,
        mesh=mesh,
        in_specs=placed,
        out_specs=(P(None, "wave", "lev", None), P("wave", "lev", None, None)),
        check_vma=False,
    )
```

```python
import math

import jax
import jax.numpy as jnp
import numpy as np
from jax import lax
from jax.experimental import pallas as pl
from jax.experimental.pallas import tpu as pltpu
from jax.sharding import PartitionSpec as P

LPAD = 4864
LANES = 128
BLOCKS = LPAD // LANES
ROWS_PAD = 80
SLOT_PAD = 32
CYCLE_PAD = 64
WAVES = 12
LINES = 8
LEAF = 8
LATS = 1200
OWN = LATS // WAVES
GRID_ROWS = OWN // 2
DEGREES = 1280
SPAN = DEGREES // LINES
SLOTS = 24
EARLY_ROWS = 20
MESH = pl.DeviceIdType.MESH
NT = (((1,), (1,)), ((), ()))


def cos_sin_turns(turns):
    quarter = turns * 4.0
    whole = jnp.round(quarter)
    rest = (quarter - whole) * (0.5 * math.pi)
    square = rest * rest
    sine = rest + rest * square * (
        -1.6666666666e-1 + square * (8.3333331e-3 + square * (-1.98412698e-4 + square * 2.7557319e-6))
    )
    cosine = 1.0 + square * (
        -0.5 + square * (4.16666667e-2 + square * (-1.388888889e-3 + square * (2.48015873e-5 - square * 2.7557319e-7)))
    )
    step = whole.astype(jnp.int32) & 3
    swap = (step & 1) == 1
    cos_base = jnp.where(swap, sine, cosine)
    sin_base = jnp.where(swap, cosine, sine)
    cos_value = jnp.where((step == 1) | (step == 2), -cos_base, cos_base)
    sin_value = jnp.where(step >= 2, -sin_base, sin_base)
    return cos_value, sin_value


def turns_of(product, length, inverse):
    whole = jnp.round(product * inverse)
    return (product - whole * length) * inverse


def remote(source, target, send, receive, device):
    return pltpu.make_async_remote_copy(
        src_ref=source, dst_ref=target, send_sem=send, recv_sem=receive,
        device_id=device, device_id_type=MESH,
    )


def order_of(map_ref, wave, slot):
    return map_ref[wave * 2 + slot] * DEGREES // SLOTS


def whole_kernel(
    map_ref, len_ref, weight_ref, order_ref, leg_ref, spec_ref, spread_ref, gather_ref, natural_ref,
    grid_ref, out_ref,
    panel_ref, lhs, part, got, four, waves_ref, turned_ref, plain_ref, cross_ref, sum_ref,
    cos_ref, sin_ref, inner_ref, ret_ref, here, fields, piece, final,
    local_sem, chip_send, chip_recv, core_send, core_recv, coef_send, coef_recv, part_send, part_recv,
    wave_send, wave_recv, turn_send, turn_recv, line_send, line_recv, piece_send, piece_recv,
):
    wave = lax.axis_index("wave")
    lev = lax.axis_index("lev")
    line = lax.div(lev, LEAF)
    leaf = lax.rem(lev, LEAF)
    core = lax.rem(leaf, 2)
    chip = lax.div(leaf, 2)
    sibling = {"lev": lev + 1 - 2 * core}
    chips = [{"lev": line * LEAF + lax.rem(chip + d, 4) * 2 + core} for d in range(1, 4)]
    lines = [{"lev": lax.rem(line + d, LINES) * LEAF + leaf} for d in range(1, LINES)]
    waves = [{"wave": lax.rem(wave + d, WAVES)} for d in range(1, WAVES)]
    peers = waves + lines + chips + [sibling]
    barrier = pltpu.get_barrier_semaphore()
    for device in peers:
        pl.semaphore_signal(barrier, inc=1, device_id=device, device_id_type=MESH)

    first_lat = wave * OWN
    order_lane = order_ref[0:1, :]
    order_lane = order_lane + pltpu.roll(order_lane, 32, 1)
    order_lane = order_lane + pltpu.roll(order_lane, 64, 1)
    lane = lax.broadcasted_iota(jnp.int32, (1, LANES), 1)
    double = jnp.where(lane % SLOT_PAD < SLOTS, jnp.where(order_lane == 0.0, 1.0, 2.0), 0.0)
    order_sub = jnp.broadcast_to(order_lane, (LANES, LANES)).T[:SLOT_PAD]
    lane_f = lax.broadcasted_iota(jnp.int32, (ROWS_PAD, LANES), 1)
    row_f = lax.broadcasted_iota(jnp.int32, (ROWS_PAD, LANES), 0)
    block_start = (row_f // 2) * LANES
    position = block_start + lane_f
    block_start = block_start.astype(jnp.float32)
    second_lane = lane // SLOT_PAD % 2 == 1
    sign = jnp.where(lane < 64, 1.0, -1.0)
    inner_lane = lax.broadcasted_iota(jnp.int32, (SLOT_PAD, LANES), 1).astype(jnp.float32)
    inner_product = order_sub * inner_lane
    north = row_f % 2 == 0
    zero_block = jnp.zeros((SLOT_PAD, LANES), jnp.bfloat16)

    def tables(row):
        first_f = len_ref[first_lat + 2 * row].astype(jnp.float32)
        second_f = len_ref[first_lat + 2 * row + 1].astype(jnp.float32)
        length_lane = jnp.where(second_lane, second_f, first_f)
        start_lane = jnp.where(second_lane, first_f, 0.0)
        inverse_lane = 1.0 / length_lane
        inv_first = inverse_lane[:, 0:1]
        inv_second = inverse_lane[:, SLOT_PAD : SLOT_PAD + 1]
        outer = order_lane * (block_start - start_lane)
        outer_cos, outer_sin = cos_sin_turns(turns_of(outer, length_lane, inverse_lane))
        cos_ref[row] = outer_cos
        sin_ref[row] = outer_sin
        cos_a, sin_a = cos_sin_turns(turns_of(inner_product, first_f, inv_first))
        cos_b, sin_b = cos_sin_turns(turns_of(inner_product, second_f, inv_second))
        inner_ref[row] = jnp.concatenate(
            [
                jnp.concatenate([cos_a.astype(jnp.bfloat16), zero_block], 1),
                jnp.concatenate([zero_block, cos_b.astype(jnp.bfloat16)], 1),
                jnp.concatenate([(-sin_a).astype(jnp.bfloat16), zero_block], 1),
                jnp.concatenate([zero_block, (-sin_b).astype(jnp.bfloat16)], 1),
            ],
            0,
        )

    @pl.loop(0, EARLY_ROWS)
    def _(row):
        tables(row)

    pl.semaphore_wait(barrier, len(peers))

    copies = []

    def send(*details):
        copy = remote(*details)
        copy.start()
        copies.append(copy)

    for d in range(1, 4):
        send(leg_ref, panel_ref.at[leaf], chip_send.at[d - 1], chip_recv.at[d - 1], chips[d - 1])
    for d in range(1, LINES):
        send(spec_ref, lhs.at[line], coef_send.at[d - 1], coef_recv.at[d - 1], lines[d - 1])
    send(leg_ref, panel_ref.at[leaf], core_send.at[0], core_recv.at[0], sibling)
    own_panel = pltpu.make_async_copy(leg_ref, panel_ref.at[leaf], local_sem.at[0])
    own_panel.start()
    own_coef = pltpu.make_async_copy(spec_ref, lhs.at[line], local_sem.at[1])
    own_coef.start()

    @pl.loop(EARLY_ROWS, GRID_ROWS)
    def _(row):
        tables(row)

    width = panel_ref.shape[0] * panel_ref.shape[1]
    picked = lax.broadcasted_iota(jnp.int32, (DEGREES, width), 0) - line * SPAN
    widen = jnp.where(picked == lax.broadcasted_iota(jnp.int32, (DEGREES, width), 1) // 2, 1.0, 0.0)
    widen = widen.astype(jnp.bfloat16)
    four[...] = jnp.zeros_like(four)
    sum_ref[...] = jnp.zeros_like(sum_ref)
    for d in range(1, 4):
        block = panel_ref.at[lax.rem(chip + 4 - d, 4) * 2 + core]
        remote(block, block, chip_send.at[d - 1], chip_recv.at[d - 1], chips[d - 1]).wait_recv()
        send(block, block, core_send.at[d], core_recv.at[d], sibling)
    own_coef.wait()
    for d in range(1, LINES):
        block = lhs.at[lax.rem(line + LINES - d, LINES)]
        remote(block, block, coef_send.at[d - 1], coef_recv.at[d - 1], lines[d - 1]).wait_recv()
    coef = jnp.dot(lhs[...].reshape(LINES * 8, DEGREES), widen, preferred_element_type=jnp.float32)
    kind = lax.broadcasted_iota(jnp.int32, coef.shape, 0) % 8
    column = lax.broadcasted_iota(jnp.int32, coef.shape, 1)
    degree = column // 2 + line * SPAN
    order = jnp.where(kind >= 4, order_of(map_ref, wave, 1), order_of(map_ref, wave, 0))
    kept = (kind // 4 == column % 2) & (degree >= order)
    negated = (kind // 2 % 2 == 1) & ((degree + order) % 2 == 1)
    coef = jnp.where(kept, coef, 0.0)
    coef = jnp.where(negated, -coef, coef).astype(jnp.bfloat16)
    own_panel.wait()
    for d in range(4):
        block = panel_ref.at[lax.rem(chip + 4 - d, 4) * 2 + 1 - core]
        remote(block, block, core_send.at[d], core_recv.at[d], sibling).wait_recv()
    product = jnp.dot(coef, panel_ref[...].reshape(width, LATS), preferred_element_type=jnp.float32)
    part[...] = product.reshape(LINES, 8, LATS)
    for d in range(1, LINES):
        target = lax.rem(line + d, LINES)
        send(part.at[target], got.at[d - 1], part_send.at[d - 1], part_recv.at[d - 1], lines[d - 1])
    total = part[line]
    for d in range(1, LINES):
        block = got.at[d - 1]
        remote(block, block, part_send.at[d - 1], part_recv.at[d - 1], lines[d - 1]).wait_recv()
        total = total + got[d - 1]
    for w in range(WAVES):
        four[w, :, :OWN] = total[:, w * OWN : (w + 1) * OWN].astype(jnp.bfloat16)
    for d in range(1, WAVES):
        target = lax.rem(wave + d, WAVES)
        send(four.at[target], waves_ref.at[wave], wave_send.at[d - 1], wave_recv.at[d - 1], waves[d - 1])
    own_wave = pltpu.make_async_copy(four.at[wave], waves_ref.at[wave], local_sem.at[2])
    own_wave.start()
    own_wave.wait()
    for d in range(1, WAVES):
        block = waves_ref.at[lax.rem(wave + WAVES - d, WAVES)]
        remote(block, block, wave_send.at[d - 1], wave_recv.at[d - 1], waves[d - 1]).wait_recv()

    arrived = waves_ref[...].reshape(WAVES * 8, LANES)
    turned = lax.dot_general(
        arrived, spread_ref[...], (((0,), (0,)), ((), ())), preferred_element_type=jnp.float32
    )
    for h in range(2):
        turned_ref[...] = turned[:, h * LANES : (h + 1) * LANES]
        half = jnp.where(
            second_lane, turned_ref[pl.ds(1, CYCLE_PAD, 2), :], turned_ref[pl.ds(0, CYCLE_PAD, 2), :]
        )
        half = half * double
        plain_ref[h] = half
        cross_ref[h] = -sign * pltpu.roll(half, 64, 1)

    @pl.loop(0, GRID_ROWS)
    def _(row):
        first = len_ref[first_lat + 2 * row]
        second = len_ref[first_lat + 2 * row + 1]
        length_lane = jnp.where(second_lane, second.astype(jnp.float32), first.astype(jnp.float32))
        weight_lane = jnp.where(
            second_lane, weight_ref[first_lat + 2 * row + 1], weight_ref[first_lat + 2 * row]
        )
        resolved = 2.0 * order_lane < length_lane
        factor = jnp.where(resolved, weight_lane / length_lane, 0.0)
        inner = inner_ref[row]
        plain = jnp.where(north, plain_ref[0, pl.ds(row, 1), :], plain_ref[1, pl.ds(row, 1), :])
        crossed = jnp.where(north, cross_ref[0, pl.ds(row, 1), :], cross_ref[1, pl.ds(row, 1), :])
        spread = jnp.where(resolved, plain * cos_ref[row] + crossed * sin_ref[row], 0.0).astype(jnp.bfloat16)
        images = jnp.dot(spread, inner, preferred_element_type=jnp.float32)
        in_first = position < first
        occupied = position < first + second
        values = jnp.where(in_first, images[:, :LANES], jnp.where(occupied, images[:, LANES:], 0.0))
        values = values.astype(jnp.bfloat16)
        for block in range(BLOCKS):
            grid_ref[row, :, block * LANES : (block + 1) * LANES] = values[2 * block : 2 * block + 2]
        wide = values.astype(jnp.float32)
        squared = wide * wide
        by_cycle = jnp.concatenate(
            [
                jnp.where(in_first, squared, 0.0).astype(jnp.bfloat16),
                jnp.where(in_first, 0.0, squared).astype(jnp.bfloat16),
            ],
            1,
        )
        partial = lax.dot_general(by_cycle, inner, NT, preferred_element_type=jnp.float32)
        cos_sum = jnp.sum((partial * cos_ref[row]).reshape(ROWS_PAD // 8, 8, LANES), 0)
        sin_sum = jnp.sum((partial * sin_ref[row]).reshape(ROWS_PAD // 8, 8, LANES), 0)
        total = cos_sum + sign * pltpu.roll(sin_sum, 64, 1)
        total = total + pltpu.roll(total, 4, 0)
        total = total + pltpu.roll(total, 2, 0)
        sum_ref[0, pl.ds(row, 1), :] = total[0:1, :] * factor
        sum_ref[1, pl.ds(row, 1), :] = total[1:2, :] * factor

    sums = jnp.concatenate([sum_ref[0], sum_ref[1]], 1).astype(jnp.bfloat16)
    returned = jnp.concatenate(
        [
            lax.dot_general(gather_ref[cycle], sums, NT, preferred_element_type=jnp.float32)
            for cycle in range(2)
        ],
        1,
    )
    returned = jnp.dot(returned.astype(jnp.bfloat16), natural_ref[...], preferred_element_type=jnp.float32)
    ret_ref[...] = returned.astype(jnp.bfloat16).reshape(WAVES, 8, LANES)

    for d in range(1, WAVES):
        target = lax.rem(wave + d, WAVES)
        send(ret_ref.at[target], here.at[wave], turn_send.at[d - 1], turn_recv.at[d - 1], waves[d - 1])
    own_turn = pltpu.make_async_copy(ret_ref.at[wave], here.at[wave], local_sem.at[3])
    own_turn.start()
    own_turn.wait()
    for d in range(1, WAVES):
        block = here.at[lax.rem(wave + WAVES - d, WAVES)]
        remote(block, block, turn_send.at[d - 1], turn_recv.at[d - 1], waves[d - 1]).wait_recv()
    for d in range(1, LINES):
        send(here, fields.at[line], line_send.at[d - 1], line_recv.at[d - 1], lines[d - 1])
    own_line = pltpu.make_async_copy(here, fields.at[line], local_sem.at[4])
    own_line.start()
    own_line.wait()
    for d in range(1, LINES):
        block = fields.at[lax.rem(line + LINES - d, LINES)]
        remote(block, block, line_send.at[d - 1], line_recv.at[d - 1], lines[d - 1]).wait_recv()
    columns = jnp.concatenate(
        [fields[:, w].reshape(LINES * 8, LANES)[:, :OWN].astype(jnp.float32) for w in range(WAVES)], 1
    ).astype(jnp.bfloat16)
    product = lax.dot_general(
        columns, panel_ref[...].reshape(width, LATS), NT, preferred_element_type=jnp.float32
    )
    product = jnp.where(kept, product, 0.0)
    product = jnp.where(negated, -product, product)
    narrow = lax.broadcasted_iota(jnp.int32, (width, SPAN), 0) // 2 == lax.broadcasted_iota(jnp.int32, (width, SPAN), 1)
    product = jnp.dot(
        product, jnp.where(narrow, 1.0, 0.0), precision=lax.Precision.HIGHEST, preferred_element_type=jnp.float32
    )
    piece[...] = product.reshape(LINES, 8, SPAN)
    for d in range(1, LINES):
        target = lax.rem(line + d, LINES)
        send(piece.at[target], final.at[line], piece_send.at[d - 1], piece_recv.at[d - 1], lines[d - 1])
    own_piece = pltpu.make_async_copy(piece.at[line], final.at[line], local_sem.at[5])
    own_piece.start()
    own_piece.wait()
    for d in range(1, LINES):
        block = final.at[lax.rem(line + LINES - d, LINES)]
        remote(block, block, piece_send.at[d - 1], piece_recv.at[d - 1], lines[d - 1]).wait_recv()
    result = jnp.concatenate([final[y] for y in range(LINES)], 1)
    for s in range(2):
        out_ref[s] = result[4 * s : 4 * s + 2] + result[4 * s + 2 : 4 * s + 4]
    for copy in copies:
        copy.wait_send()


def per_device(spec, legendre, gauss_w, cycle_len, wave_map):
    slots_dev = spec.shape[0]
    depth = legendre.shape[1] * slots_dev
    panel = legendre.transpose(1, 0, 2).reshape(depth, LATS)
    doubled = jnp.broadcast_to(spec, (slots_dev, 2, 2, DEGREES)).reshape(8, DEGREES)
    orders = (wave_map * DEGREES // SLOTS).astype(jnp.float32)
    orders = jnp.broadcast_to(jnp.pad(orders, (0, LANES - SLOTS))[None, :], (8, LANES))

    line = np.arange(WAVES * 8)
    line_slot, line_half, line_part = line // 8 * 2 + line % 8 // 4, line // 2 % 2, line % 2
    both = np.arange(2 * LANES)
    both_half, both_part, both_cycle, both_slot = both // LANES, both // 64 % 2, both // 32 % 2, both % 32
    match = (
        (line_slot[:, None] == both_slot) & (line_half[:, None] == both_half) & (line_part[:, None] == both_part)
    )
    spread = jnp.asarray(match, jnp.bfloat16)
    packed = np.arange(LANES)
    natural = (packed % CYCLE_PAD < GRID_ROWS)[:, None] & (
        (packed % CYCLE_PAD * 2 + packed // CYCLE_PAD)[:, None] == packed[None, :]
    )
    natural = jnp.asarray(natural, jnp.bfloat16)
    gather = jnp.asarray(np.stack([match & (both_cycle == 0), match & (both_cycle == 1)]), jnp.bfloat16)

    vmem = pl.BlockSpec(memory_space=pltpu.VMEM)
    smem = pl.BlockSpec(memory_space=pltpu.SMEM)
    dma = pltpu.SemaphoreType.DMA
    bf16, f32 = jnp.bfloat16, jnp.float32
    grid, spec_out = pl.pallas_call(
        whole_kernel,
        out_shape=(
            jax.ShapeDtypeStruct((GRID_ROWS, 2, LPAD), bf16),
            jax.ShapeDtypeStruct((slots_dev, 2, DEGREES), f32),
        ),
        in_specs=[smem] * 3 + [vmem] * 6,
        out_specs=(vmem, vmem),
        scratch_shapes=[
            pltpu.VMEM((LEAF, depth, LATS), bf16),
            pltpu.VMEM((LINES, 8, DEGREES), bf16),
            pltpu.VMEM((LINES, 8, LATS), f32),
            pltpu.VMEM((LINES - 1, 8, LATS), f32),
            pltpu.VMEM((WAVES, 8, LANES), bf16),
            pltpu.VMEM((WAVES, 8, LANES), bf16),
            pltpu.VMEM((LANES, LANES), f32),
            pltpu.VMEM((2, CYCLE_PAD, LANES), f32),
            pltpu.VMEM((2, CYCLE_PAD, LANES), f32),
            pltpu.VMEM((2, CYCLE_PAD, LANES), f32),
            pltpu.VMEM((GRID_ROWS, ROWS_PAD, LANES), f32),
            pltpu.VMEM((GRID_ROWS, ROWS_PAD, LANES), f32),
            pltpu.VMEM((GRID_ROWS, LANES, 2 * LANES), bf16),
            pltpu.VMEM((WAVES, 8, LANES), bf16),
            pltpu.VMEM((WAVES, 8, LANES), bf16),
            pltpu.VMEM((LINES, WAVES, 8, LANES), bf16),
            pltpu.VMEM((LINES, 8, SPAN), f32),
            pltpu.VMEM((LINES, 8, SPAN), f32),
            dma((6,)), dma((3,)), dma((3,)), dma((4,)), dma((4,)),
            dma((LINES - 1,)), dma((LINES - 1,)), dma((LINES - 1,)), dma((LINES - 1,)),
            dma((WAVES - 1,)), dma((WAVES - 1,)), dma((WAVES - 1,)), dma((WAVES - 1,)),
            dma((LINES - 1,)), dma((LINES - 1,)), dma((LINES - 1,)), dma((LINES - 1,)),
        ],
        compiler_params=pltpu.CompilerParams(collective_id=0, has_side_effects=True),
        name="whole",
    )(wave_map, cycle_len, gauss_w, orders, panel, doubled, spread, gather, natural)
    grid = grid.transpose(1, 0, 2).reshape(2, GRID_ROWS, 1, LPAD)
    return (grid, spec_out.reshape(slots_dev, 1, 2, DEGREES))


def solution(mesh):
    placed = (P("wave", "lev", None, None), P("wave", "lev", None), P(), P(), P())
    return jax.shard_map(
        per_device,
        mesh=mesh,
        in_specs=placed,
        out_specs=(P(None, "wave", "lev", None), P("wave", "lev", None, None)),
        check_vma=False,
    )
```

```python
import math

import jax
import jax.numpy as jnp
import numpy as np
from jax import lax
from jax.experimental import pallas as pl
from jax.experimental.pallas import tpu as pltpu
from jax.sharding import PartitionSpec as P

LPAD = 4864
LANES = 128
BLOCKS = LPAD // LANES
ROWS_PAD = 80
SLOT_PAD = 32
CYCLE_PAD = 64
WAVES = 12
LINES = 8
LEAF = 8
LATS = 1200
OWN = LATS // WAVES
GRID_ROWS = OWN // 2
DEGREES = 1280
SPAN = DEGREES // LEAF
RUN = SPAN // LINES
SLOTS = 24
EARLY_ROWS = 20
STEP_ROWS = 10
CUTS = ((0, 24), (24, 16))
MESH = pl.DeviceIdType.MESH
NT = (((1,), (1,)), ((), ()))


def cos_sin_turns(turns):
    quarter = turns * 4.0
    whole = jnp.round(quarter)
    rest = (quarter - whole) * (0.5 * math.pi)
    square = rest * rest
    sine = rest + rest * square * (
        -1.6666666666e-1 + square * (8.3333331e-3 + square * (-1.98412698e-4 + square * 2.7557319e-6))
    )
    cosine = 1.0 + square * (
        -0.5 + square * (4.16666667e-2 + square * (-1.388888889e-3 + square * (2.48015873e-5 - square * 2.7557319e-7)))
    )
    step = whole.astype(jnp.int32) & 3
    swap = (step & 1) == 1
    cos_base = jnp.where(swap, sine, cosine)
    sin_base = jnp.where(swap, cosine, sine)
    cos_value = jnp.where((step == 1) | (step == 2), -cos_base, cos_base)
    sin_value = jnp.where(step >= 2, -sin_base, sin_base)
    return cos_value, sin_value


def turns_of(product, length, inverse):
    whole = jnp.round(product * inverse)
    return (product - whole * length) * inverse


def remote(source, target, send, receive, device):
    return pltpu.make_async_remote_copy(
        src_ref=source, dst_ref=target, send_sem=send, recv_sem=receive,
        device_id=device, device_id_type=MESH,
    )


def order_of(map_ref, wave, slot):
    return map_ref[wave * 2 + slot] * DEGREES // SLOTS


def whole_kernel(
    map_ref, len_ref, weight_ref, order_ref, leg_ref, spec_ref, spread_ref, gather_ref, natural_ref,
    grid_ref, out_ref,
    panel_ref, lhs, part, got, four, waves_ref, turned_ref, plain_ref, cross_ref, sum_ref,
    cos_ref, sin_ref, inner_ref, ret_ref, here, fields, piece, final,
    local_sem, ring_send, ring_recv, coef_send, coef_recv, part_send, part_recv,
    wave_send, wave_recv, turn_send, turn_recv, line_send, line_recv, piece_send, piece_recv,
):
    wave = lax.axis_index("wave")
    lev = lax.axis_index("lev")
    line = lax.div(lev, LEAF)
    leaf = lax.rem(lev, LEAF)
    ring = [{"lev": lax.rem(line + d, LINES) * LEAF + leaf} for d in (1, LINES - 1)]
    leaves = [{"lev": line * LEAF + lax.rem(leaf + d, LEAF)} for d in range(1, LEAF)]
    waves = [{"wave": lax.rem(wave + d, WAVES)} for d in range(1, WAVES)]
    peers = waves + leaves + ring
    barrier = pltpu.get_barrier_semaphore()
    for device in peers:
        pl.semaphore_signal(barrier, inc=1, device_id=device, device_id_type=MESH)

    first_lat = wave * OWN
    order_lane = order_ref[0:1, :]
    order_lane = order_lane + pltpu.roll(order_lane, 32, 1)
    order_lane = order_lane + pltpu.roll(order_lane, 64, 1)
    lane = lax.broadcasted_iota(jnp.int32, (1, LANES), 1)
    double = jnp.where(lane % SLOT_PAD < SLOTS, jnp.where(order_lane == 0.0, 1.0, 2.0), 0.0)
    order_sub = jnp.broadcast_to(order_lane, (LANES, LANES)).T[:SLOT_PAD]
    lane_f = lax.broadcasted_iota(jnp.int32, (ROWS_PAD, LANES), 1)
    row_f = lax.broadcasted_iota(jnp.int32, (ROWS_PAD, LANES), 0)
    block_start = (row_f // 2) * LANES
    position = block_start + lane_f
    block_start = block_start.astype(jnp.float32)
    second_lane = lane // SLOT_PAD % 2 == 1
    sign = jnp.where(lane < 64, 1.0, -1.0)
    inner_lane = lax.broadcasted_iota(jnp.int32, (SLOT_PAD, LANES), 1).astype(jnp.float32)
    inner_product = order_sub * inner_lane
    north = row_f % 2 == 0
    zero_block = jnp.zeros((SLOT_PAD, LANES), jnp.bfloat16)

    def tables(row):
        first_f = len_ref[first_lat + 2 * row].astype(jnp.float32)
        second_f = len_ref[first_lat + 2 * row + 1].astype(jnp.float32)
        length_lane = jnp.where(second_lane, second_f, first_f)
        start_lane = jnp.where(second_lane, first_f, 0.0)
        inverse_lane = 1.0 / length_lane
        inv_first = inverse_lane[:, 0:1]
        inv_second = inverse_lane[:, SLOT_PAD : SLOT_PAD + 1]
        outer = order_lane * (block_start - start_lane)
        outer_cos, outer_sin = cos_sin_turns(turns_of(outer, length_lane, inverse_lane))
        cos_ref[row] = outer_cos
        sin_ref[row] = outer_sin
        cos_a, sin_a = cos_sin_turns(turns_of(inner_product, first_f, inv_first))
        cos_b, sin_b = cos_sin_turns(turns_of(inner_product, second_f, inv_second))
        inner_ref[row] = jnp.concatenate(
            [
                jnp.concatenate([cos_a.astype(jnp.bfloat16), zero_block], 1),
                jnp.concatenate([zero_block, cos_b.astype(jnp.bfloat16)], 1),
                jnp.concatenate([(-sin_a).astype(jnp.bfloat16), zero_block], 1),
                jnp.concatenate([zero_block, (-sin_b).astype(jnp.bfloat16)], 1),
            ],
            0,
        )

    @pl.loop(0, EARLY_ROWS)
    def _(row):
        tables(row)

    pl.semaphore_wait(barrier, len(peers))

    copies = []

    def send(*details):
        copy = remote(*details)
        copy.start()
        copies.append(copy)

    def ring_copy(source, block, way, hop, cut):
        start, size = CUTS[cut]
        target = panel_ref.at[block, pl.ds(start, size), :]
        return (
            target if source is None else source.at[pl.ds(start, size), :],
            target,
            ring_send.at[way, hop - 1, cut],
            ring_recv.at[way, hop - 1, cut],
            ring[way],
        )

    for cut in range(2):
        for way in range(2):
            send(*ring_copy(leg_ref, line, way, 1, cut))
    own_panel = pltpu.make_async_copy(leg_ref, panel_ref.at[line], local_sem.at[0])
    own_panel.start()
    for d in range(1, LEAF):
        send(spec_ref, lhs.at[leaf], coef_send.at[d - 1], coef_recv.at[d - 1], leaves[d - 1])
    own_coef = pltpu.make_async_copy(spec_ref, lhs.at[leaf], local_sem.at[1])
    own_coef.start()

    for hop in range(1, 4):

        @pl.loop(EARLY_ROWS + (hop - 1) * STEP_ROWS, EARLY_ROWS + hop * STEP_ROWS)
        def _(row):
            tables(row)

        for cut in range(2):
            for way in range(2):
                origin = lax.rem(line + (LINES - hop if way == 0 else hop), LINES)
                remote(*ring_copy(None, origin, way, hop, cut)).wait_recv()
                if hop < 3 or cut == way:
                    send(*ring_copy(None, origin, way, hop + 1, cut))

    width = panel_ref.shape[0] * panel_ref.shape[1]
    column = lax.broadcasted_iota(jnp.int32, (1, width), 1)
    degree = column // (2 * RUN) * SPAN + leaf * RUN + column % (2 * RUN) // 2
    widen = jnp.where(lax.broadcasted_iota(jnp.int32, (DEGREES, width), 0) == degree, 1.0, 0.0)
    widen = widen.astype(jnp.bfloat16)
    four[...] = jnp.zeros_like(four)
    sum_ref[...] = jnp.zeros_like(sum_ref)
    own_coef.wait()
    for d in range(1, LEAF):
        block = lhs.at[lax.rem(leaf + LEAF - d, LEAF)]
        remote(block, block, coef_send.at[d - 1], coef_recv.at[d - 1], leaves[d - 1]).wait_recv()
    coef = jnp.dot(lhs[...].reshape(LEAF * 8, DEGREES), widen, preferred_element_type=jnp.float32)
    kind = lax.broadcasted_iota(jnp.int32, coef.shape, 0) % 8
    order = jnp.where(kind >= 4, order_of(map_ref, wave, 1), order_of(map_ref, wave, 0))
    kept = (kind // 4 == column % 2) & (degree >= order)
    negated = (kind // 2 % 2 == 1) & ((degree + order) % 2 == 1)
    coef = jnp.where(kept, coef, 0.0)
    coef = jnp.where(negated, -coef, coef).astype(jnp.bfloat16)
    own_panel.wait()
    far = lax.rem(line + LINES // 2, LINES)
    for cut in range(2):
        remote(*ring_copy(None, far, cut, 4, cut)).wait_recv()
    product = jnp.dot(coef, panel_ref[...].reshape(width, LATS), preferred_element_type=jnp.float32)
    part[...] = product.reshape(LEAF, 8, LATS)
    for d in range(1, LEAF):
        target = lax.rem(leaf + d, LEAF)
        send(part.at[target], got.at[d - 1], part_send.at[d - 1], part_recv.at[d - 1], leaves[d - 1])
    total = part[leaf]
    for d in range(1, LEAF):
        block = got.at[d - 1]
        remote(block, block, part_send.at[d - 1], part_recv.at[d - 1], leaves[d - 1]).wait_recv()
        total = total + got[d - 1]
    for w in range(WAVES):
        four[w, :, :OWN] = total[:, w * OWN : (w + 1) * OWN].astype(jnp.bfloat16)
    for d in range(1, WAVES):
        target = lax.rem(wave + d, WAVES)
        send(four.at[target], waves_ref.at[wave], wave_send.at[d - 1], wave_recv.at[d - 1], waves[d - 1])
    own_wave = pltpu.make_async_copy(four.at[wave], waves_ref.at[wave], local_sem.at[2])
    own_wave.start()
    own_wave.wait()
    for d in range(1, WAVES):
        block = waves_ref.at[lax.rem(wave + WAVES - d, WAVES)]
        remote(block, block, wave_send.at[d - 1], wave_recv.at[d - 1], waves[d - 1]).wait_recv()

    arrived = waves_ref[...].reshape(WAVES * 8, LANES)
    turned = lax.dot_general(
        arrived, spread_ref[...], (((0,), (0,)), ((), ())), preferred_element_type=jnp.float32
    )
    for h in range(2):
        turned_ref[...] = turned[:, h * LANES : (h + 1) * LANES]
        half = jnp.where(
            second_lane, turned_ref[pl.ds(1, CYCLE_PAD, 2), :], turned_ref[pl.ds(0, CYCLE_PAD, 2), :]
        )
        half = half * double
        plain_ref[h] = half
        cross_ref[h] = -sign * pltpu.roll(half, 64, 1)

    @pl.loop(0, GRID_ROWS)
    def _(row):
        first = len_ref[first_lat + 2 * row]
        second = len_ref[first_lat + 2 * row + 1]
        length_lane = jnp.where(second_lane, second.astype(jnp.float32), first.astype(jnp.float32))
        weight_lane = jnp.where(
            second_lane, weight_ref[first_lat + 2 * row + 1], weight_ref[first_lat + 2 * row]
        )
        resolved = 2.0 * order_lane < length_lane
        factor = jnp.where(resolved, weight_lane / length_lane, 0.0)
        inner = inner_ref[row]
        plain = jnp.where(north, plain_ref[0, pl.ds(row, 1), :], plain_ref[1, pl.ds(row, 1), :])
        crossed = jnp.where(north, cross_ref[0, pl.ds(row, 1), :], cross_ref[1, pl.ds(row, 1), :])
        spread = jnp.where(resolved, plain * cos_ref[row] + crossed * sin_ref[row], 0.0).astype(jnp.bfloat16)
        images = jnp.dot(spread, inner, preferred_element_type=jnp.float32)
        in_first = position < first
        occupied = position < first + second
        values = jnp.where(in_first, images[:, :LANES], jnp.where(occupied, images[:, LANES:], 0.0))
        values = values.astype(jnp.bfloat16)
        for block in range(BLOCKS):
            grid_ref[row, :, block * LANES : (block + 1) * LANES] = values[2 * block : 2 * block + 2]
        wide = values.astype(jnp.float32)
        squared = wide * wide
        by_cycle = jnp.concatenate(
            [
                jnp.where(in_first, squared, 0.0).astype(jnp.bfloat16),
                jnp.where(in_first, 0.0, squared).astype(jnp.bfloat16),
            ],
            1,
        )
        partial = lax.dot_general(by_cycle, inner, NT, preferred_element_type=jnp.float32)
        cos_sum = jnp.sum((partial * cos_ref[row]).reshape(ROWS_PAD // 8, 8, LANES), 0)
        sin_sum = jnp.sum((partial * sin_ref[row]).reshape(ROWS_PAD // 8, 8, LANES), 0)
        total = cos_sum + sign * pltpu.roll(sin_sum, 64, 1)
        total = total + pltpu.roll(total, 4, 0)
        total = total + pltpu.roll(total, 2, 0)
        sum_ref[0, pl.ds(row, 1), :] = total[0:1, :] * factor
        sum_ref[1, pl.ds(row, 1), :] = total[1:2, :] * factor

    sums = jnp.concatenate([sum_ref[0], sum_ref[1]], 1).astype(jnp.bfloat16)
    returned = jnp.concatenate(
        [
            lax.dot_general(gather_ref[cycle], sums, NT, preferred_element_type=jnp.float32)
            for cycle in range(2)
        ],
        1,
    )
    returned = jnp.dot(returned.astype(jnp.bfloat16), natural_ref[...], preferred_element_type=jnp.float32)
    ret_ref[...] = returned.astype(jnp.bfloat16).reshape(WAVES, 8, LANES)

    for d in range(1, WAVES):
        target = lax.rem(wave + d, WAVES)
        send(ret_ref.at[target], here.at[wave], turn_send.at[d - 1], turn_recv.at[d - 1], waves[d - 1])
    own_turn = pltpu.make_async_copy(ret_ref.at[wave], here.at[wave], local_sem.at[3])
    own_turn.start()
    own_turn.wait()
    for d in range(1, WAVES):
        block = here.at[lax.rem(wave + WAVES - d, WAVES)]
        remote(block, block, turn_send.at[d - 1], turn_recv.at[d - 1], waves[d - 1]).wait_recv()
    for d in range(1, LEAF):
        send(here, fields.at[leaf], line_send.at[d - 1], line_recv.at[d - 1], leaves[d - 1])
    own_line = pltpu.make_async_copy(here, fields.at[leaf], local_sem.at[4])
    own_line.start()
    own_line.wait()
    for d in range(1, LEAF):
        block = fields.at[lax.rem(leaf + LEAF - d, LEAF)]
        remote(block, block, line_send.at[d - 1], line_recv.at[d - 1], leaves[d - 1]).wait_recv()
    columns = jnp.concatenate(
        [fields[:, w].reshape(LEAF * 8, LANES)[:, :OWN].astype(jnp.float32) for w in range(WAVES)], 1
    ).astype(jnp.bfloat16)
    product = lax.dot_general(
        columns, panel_ref[...].reshape(width, LATS), NT, preferred_element_type=jnp.float32
    )
    product = jnp.where(kept, product, 0.0)
    product = jnp.where(negated, -product, product)
    narrow = lax.broadcasted_iota(jnp.int32, (width, SPAN), 0) // 2 == lax.broadcasted_iota(jnp.int32, (width, SPAN), 1)
    product = jnp.dot(
        product, jnp.where(narrow, 1.0, 0.0), precision=lax.Precision.HIGHEST, preferred_element_type=jnp.float32
    )
    piece[...] = product.reshape(LEAF, 8, SPAN)
    for d in range(1, LEAF):
        target = lax.rem(leaf + d, LEAF)
        send(piece.at[target], final.at[leaf], piece_send.at[d - 1], piece_recv.at[d - 1], leaves[d - 1])
    own_piece = pltpu.make_async_copy(piece.at[leaf], final.at[leaf], local_sem.at[5])
    own_piece.start()
    own_piece.wait()
    for d in range(1, LEAF):
        block = final.at[lax.rem(leaf + LEAF - d, LEAF)]
        remote(block, block, piece_send.at[d - 1], piece_recv.at[d - 1], leaves[d - 1]).wait_recv()
    pieces = [final[k] for k in range(LEAF)]
    result = jnp.concatenate(
        [pieces[k][:, y * RUN : (y + 1) * RUN] for y in range(LINES) for k in range(LEAF)], 1
    )
    for s in range(2):
        out_ref[s] = result[4 * s : 4 * s + 2] + result[4 * s + 2 : 4 * s + 4]
    for copy in copies:
        copy.wait_send()


def per_device(spec, legendre, gauss_w, cycle_len, wave_map):
    slots_dev = spec.shape[0]
    depth = legendre.shape[1] * slots_dev
    panel = legendre.transpose(1, 0, 2).reshape(depth, LATS)
    doubled = jnp.broadcast_to(spec, (slots_dev, 2, 2, DEGREES)).reshape(8, DEGREES)
    orders = (wave_map * DEGREES // SLOTS).astype(jnp.float32)
    orders = jnp.broadcast_to(jnp.pad(orders, (0, LANES - SLOTS))[None, :], (8, LANES))

    line = np.arange(WAVES * 8)
    line_slot, line_half, line_part = line // 8 * 2 + line % 8 // 4, line // 2 % 2, line % 2
    both = np.arange(2 * LANES)
    both_half, both_part, both_cycle, both_slot = both // LANES, both // 64 % 2, both // 32 % 2, both % 32
    match = (
        (line_slot[:, None] == both_slot) & (line_half[:, None] == both_half) & (line_part[:, None] == both_part)
    )
    spread = jnp.asarray(match, jnp.bfloat16)
    packed = np.arange(LANES)
    natural = (packed % CYCLE_PAD < GRID_ROWS)[:, None] & (
        (packed % CYCLE_PAD * 2 + packed // CYCLE_PAD)[:, None] == packed[None, :]
    )
    natural = jnp.asarray(natural, jnp.bfloat16)
    gather = jnp.asarray(np.stack([match & (both_cycle == 0), match & (both_cycle == 1)]), jnp.bfloat16)

    vmem = pl.BlockSpec(memory_space=pltpu.VMEM)
    smem = pl.BlockSpec(memory_space=pltpu.SMEM)
    dma = pltpu.SemaphoreType.DMA
    bf16, f32 = jnp.bfloat16, jnp.float32
    grid, spec_out = pl.pallas_call(
        whole_kernel,
        out_shape=(
            jax.ShapeDtypeStruct((GRID_ROWS, 2, LPAD), bf16),
            jax.ShapeDtypeStruct((slots_dev, 2, DEGREES), f32),
        ),
        in_specs=[smem] * 3 + [vmem] * 6,
        out_specs=(vmem, vmem),
        scratch_shapes=[
            pltpu.VMEM((LINES, depth, LATS), bf16),
            pltpu.VMEM((LEAF, 8, DEGREES), bf16),
            pltpu.VMEM((LEAF, 8, LATS), f32),
            pltpu.VMEM((LEAF - 1, 8, LATS), f32),
            pltpu.VMEM((WAVES, 8, LANES), bf16),
            pltpu.VMEM((WAVES, 8, LANES), bf16),
            pltpu.VMEM((LANES, LANES), f32),
            pltpu.VMEM((2, CYCLE_PAD, LANES), f32),
            pltpu.VMEM((2, CYCLE_PAD, LANES), f32),
            pltpu.VMEM((2, CYCLE_PAD, LANES), f32),
            pltpu.VMEM((GRID_ROWS, ROWS_PAD, LANES), f32),
            pltpu.VMEM((GRID_ROWS, ROWS_PAD, LANES), f32),
            pltpu.VMEM((GRID_ROWS, LANES, 2 * LANES), bf16),
            pltpu.VMEM((WAVES, 8, LANES), bf16),
            pltpu.VMEM((WAVES, 8, LANES), bf16),
            pltpu.VMEM((LEAF, WAVES, 8, LANES), bf16),
            pltpu.VMEM((LEAF, 8, SPAN), f32),
            pltpu.VMEM((LEAF, 8, SPAN), f32),
            dma((6,)), dma((2, 4, 2)), dma((2, 4, 2)),
            dma((LEAF - 1,)), dma((LEAF - 1,)), dma((LEAF - 1,)), dma((LEAF - 1,)),
            dma((WAVES - 1,)), dma((WAVES - 1,)), dma((WAVES - 1,)), dma((WAVES - 1,)),
            dma((LEAF - 1,)), dma((LEAF - 1,)), dma((LEAF - 1,)), dma((LEAF - 1,)),
        ],
        compiler_params=pltpu.CompilerParams(collective_id=0, has_side_effects=True),
        name="whole",
    )(wave_map, cycle_len, gauss_w, orders, panel, doubled, spread, gather, natural)
    grid = grid.transpose(1, 0, 2).reshape(2, GRID_ROWS, 1, LPAD)
    return (grid, spec_out.reshape(slots_dev, 1, 2, DEGREES))


def solution(mesh):
    placed = (P("wave", "lev", None, None), P("wave", "lev", None), P(), P(), P())
    return jax.shard_map(
        per_device,
        mesh=mesh,
        in_specs=placed,
        out_specs=(P(None, "wave", "lev", None), P("wave", "lev", None, None)),
        check_vma=False,
    )
```

```python
import math

import jax
import jax.numpy as jnp
import numpy as np
from jax import lax
from jax.experimental import pallas as pl
from jax.experimental.pallas import tpu as pltpu
from jax.sharding import PartitionSpec as P

LPAD = 4864
LANES = 128
BLOCKS = LPAD // LANES
ROWS_PAD = 80
SLOT_PAD = 32
CYCLE_PAD = 64
WAVES = 12
LINES = 8
LEAF = 8
LATS = 1200
OWN = LATS // WAVES
GRID_ROWS = OWN // 2
DEGREES = 1280
SPAN = DEGREES // LEAF
RUN = SPAN // LINES
SLOTS = 24
EARLY_ROWS = 20
STEP_ROWS = 10
UNROLL = 5
CUTS = ((0, 24), (24, 16))
MESH = pl.DeviceIdType.MESH
NT = (((1,), (1,)), ((), ()))


def cos_sin_turns(turns):
    quarter = turns * 4.0
    whole = jnp.round(quarter)
    rest = (quarter - whole) * (0.5 * math.pi)
    square = rest * rest
    sine = rest + rest * square * (
        -1.6666666666e-1 + square * (8.3333331e-3 + square * (-1.98412698e-4 + square * 2.7557319e-6))
    )
    cosine = 1.0 + square * (
        -0.5 + square * (4.16666667e-2 + square * (-1.388888889e-3 + square * (2.48015873e-5 - square * 2.7557319e-7)))
    )
    step = whole.astype(jnp.int32) & 3
    swap = (step & 1) == 1
    cos_base = jnp.where(swap, sine, cosine)
    sin_base = jnp.where(swap, cosine, sine)
    cos_value = jnp.where((step == 1) | (step == 2), -cos_base, cos_base)
    sin_value = jnp.where(step >= 2, -sin_base, sin_base)
    return cos_value, sin_value


def turns_of(product, length, inverse):
    whole = jnp.round(product * inverse)
    return (product - whole * length) * inverse


def remote(source, target, send, receive, device):
    return pltpu.make_async_remote_copy(
        src_ref=source, dst_ref=target, send_sem=send, recv_sem=receive,
        device_id=device, device_id_type=MESH,
    )


def order_of(map_ref, wave, slot):
    return map_ref[wave * 2 + slot] * DEGREES // SLOTS


def whole_kernel(
    map_ref, len_ref, weight_ref, leg_ref, spec_ref, spread_ref, gather_ref, natural_ref,
    grid_ref, out_ref,
    panel_ref, lhs, part, got, four, waves_ref, turned_ref, plain_ref, cross_ref, sum_ref,
    cos_ref, sin_ref, inner_ref, ret_ref, here, fields, piece, final,
    local_sem, ring_send, ring_recv, coef_send, coef_recv, part_send, part_recv,
    wave_send, wave_recv, turn_send, turn_recv, line_send, line_recv, piece_send, piece_recv,
):
    wave = lax.axis_index("wave")
    lev = lax.axis_index("lev")
    line = lax.div(lev, LEAF)
    leaf = lax.rem(lev, LEAF)
    ring = [{"lev": lax.rem(line + d, LINES) * LEAF + leaf} for d in (1, LINES - 1)]
    leaves = [{"lev": line * LEAF + lax.rem(leaf + d, LEAF)} for d in range(1, LEAF)]
    waves = [{"wave": lax.rem(wave + d, WAVES)} for d in range(1, WAVES)]
    peers = waves + leaves + ring
    barrier = pltpu.get_barrier_semaphore()
    for device in peers:
        pl.semaphore_signal(barrier, inc=1, device_id=device, device_id_type=MESH)

    first_lat = wave * OWN
    lane = lax.broadcasted_iota(jnp.int32, (1, LANES), 1)
    order_lane = jnp.zeros((1, LANES), jnp.int32)
    for slot in range(SLOTS):
        order_lane = jnp.where(lane % SLOT_PAD == slot, map_ref[slot] * DEGREES // SLOTS, order_lane)
    order_lane = order_lane.astype(jnp.float32)
    double = jnp.where(lane % SLOT_PAD < SLOTS, jnp.where(order_lane == 0.0, 1.0, 2.0), 0.0)
    order_sub = jnp.broadcast_to(order_lane, (LANES, LANES)).T[:SLOT_PAD]
    lane_f = lax.broadcasted_iota(jnp.int32, (ROWS_PAD, LANES), 1)
    row_f = lax.broadcasted_iota(jnp.int32, (ROWS_PAD, LANES), 0)
    block_start = (row_f // 2) * LANES
    position = block_start + lane_f
    block_start = block_start.astype(jnp.float32)
    second_lane = lane // SLOT_PAD % 2 == 1
    sign = jnp.where(lane < 64, 1.0, -1.0)
    inner_lane = lax.broadcasted_iota(jnp.int32, (SLOT_PAD, LANES), 1).astype(jnp.float32)
    inner_product = order_sub * inner_lane
    north = row_f % 2 == 0
    zero_block = jnp.zeros((SLOT_PAD, LANES), jnp.bfloat16)

    def tables(row):
        first_f = len_ref[first_lat + 2 * row].astype(jnp.float32)
        second_f = len_ref[first_lat + 2 * row + 1].astype(jnp.float32)
        length_lane = jnp.where(second_lane, second_f, first_f)
        start_lane = jnp.where(second_lane, first_f, 0.0)
        inverse_lane = 1.0 / length_lane
        inv_first = inverse_lane[:, 0:1]
        inv_second = inverse_lane[:, SLOT_PAD : SLOT_PAD + 1]
        outer = order_lane * (block_start - start_lane)
        outer_cos, outer_sin = cos_sin_turns(turns_of(outer, length_lane, inverse_lane))
        cos_ref[row] = outer_cos
        sin_ref[row] = outer_sin
        cos_a, sin_a = cos_sin_turns(turns_of(inner_product, first_f, inv_first))
        cos_b, sin_b = cos_sin_turns(turns_of(inner_product, second_f, inv_second))
        inner_ref[row] = jnp.concatenate(
            [
                jnp.concatenate([cos_a.astype(jnp.bfloat16), zero_block], 1),
                jnp.concatenate([zero_block, cos_b.astype(jnp.bfloat16)], 1),
                jnp.concatenate([(-sin_a).astype(jnp.bfloat16), zero_block], 1),
                jnp.concatenate([zero_block, (-sin_b).astype(jnp.bfloat16)], 1),
            ],
            0,
        )

    @pl.loop(0, EARLY_ROWS)
    def _(row):
        tables(row)

    pl.semaphore_wait(barrier, len(peers))

    copies = []

    def send(*details):
        copy = remote(*details)
        copy.start()
        copies.append(copy)

    def ring_copy(source, block, way, hop, cut):
        start, size = CUTS[cut]
        target = panel_ref.at[block, pl.ds(start, size), :]
        return (
            target if source is None else source.at[pl.ds(start, size), :],
            target,
            ring_send.at[way, hop - 1, cut],
            ring_recv.at[way, hop - 1, cut],
            ring[way],
        )

    for cut in range(2):
        for way in range(2):
            send(*ring_copy(leg_ref, line, way, 1, cut))
    own_panel = pltpu.make_async_copy(leg_ref, panel_ref.at[line], local_sem.at[0])
    own_panel.start()
    for d in range(1, LEAF):
        send(spec_ref, lhs.at[leaf], coef_send.at[d - 1], coef_recv.at[d - 1], leaves[d - 1])
    own_coef = pltpu.make_async_copy(spec_ref, lhs.at[leaf], local_sem.at[1])
    own_coef.start()

    for hop in range(1, 4):

        @pl.loop(EARLY_ROWS + (hop - 1) * STEP_ROWS, EARLY_ROWS + hop * STEP_ROWS)
        def _(row):
            tables(row)

        for cut in range(2):
            for way in range(2):
                origin = lax.rem(line + (LINES - hop if way == 0 else hop), LINES)
                remote(*ring_copy(None, origin, way, hop, cut)).wait_recv()
                if hop < 3 or cut == way:
                    send(*ring_copy(None, origin, way, hop + 1, cut))

    width = panel_ref.shape[0] * panel_ref.shape[1]
    column = lax.broadcasted_iota(jnp.int32, (1, width), 1)
    degree = column // (2 * RUN) * SPAN + leaf * RUN + column % (2 * RUN) // 2
    widen = jnp.where(lax.broadcasted_iota(jnp.int32, (DEGREES, width), 0) == degree, 1.0, 0.0)
    widen = widen.astype(jnp.bfloat16)
    four[...] = jnp.zeros_like(four)
    sum_ref[...] = jnp.zeros_like(sum_ref)
    own_coef.wait()
    for d in range(1, LEAF):
        block = lhs.at[lax.rem(leaf + LEAF - d, LEAF)]
        remote(block, block, coef_send.at[d - 1], coef_recv.at[d - 1], leaves[d - 1]).wait_recv()
    coef = jnp.dot(lhs[...].reshape(LEAF * 8, DEGREES), widen, preferred_element_type=jnp.float32)
    kind = lax.broadcasted_iota(jnp.int32, coef.shape, 0) % 8
    order = jnp.where(kind >= 4, order_of(map_ref, wave, 1), order_of(map_ref, wave, 0))
    kept = (kind // 4 == column % 2) & (degree >= order)
    negated = (kind // 2 % 2 == 1) & ((degree + order) % 2 == 1)
    coef = jnp.where(kept, coef, 0.0)
    coef = jnp.where(negated, -coef, coef).astype(jnp.bfloat16)
    own_panel.wait()
    far = lax.rem(line + LINES // 2, LINES)
    for cut in range(2):
        remote(*ring_copy(None, far, cut, 4, cut)).wait_recv()
    product = jnp.dot(coef, panel_ref[...].reshape(width, LATS), preferred_element_type=jnp.float32)
    part[...] = product.reshape(LEAF, 8, LATS)
    for d in range(1, LEAF):
        target = lax.rem(leaf + d, LEAF)
        send(part.at[target], got.at[d - 1], part_send.at[d - 1], part_recv.at[d - 1], leaves[d - 1])
    total = part[leaf]
    for d in range(1, LEAF):
        block = got.at[d - 1]
        remote(block, block, part_send.at[d - 1], part_recv.at[d - 1], leaves[d - 1]).wait_recv()
        total = total + got[d - 1]
    for w in range(WAVES):
        four[w, :, :OWN] = total[:, w * OWN : (w + 1) * OWN].astype(jnp.bfloat16)
    for d in range(1, WAVES):
        target = lax.rem(wave + d, WAVES)
        send(four.at[target], waves_ref.at[wave], wave_send.at[d - 1], wave_recv.at[d - 1], waves[d - 1])
    own_wave = pltpu.make_async_copy(four.at[wave], waves_ref.at[wave], local_sem.at[2])
    own_wave.start()
    own_wave.wait()
    for d in range(1, WAVES):
        block = waves_ref.at[lax.rem(wave + WAVES - d, WAVES)]
        remote(block, block, wave_send.at[d - 1], wave_recv.at[d - 1], waves[d - 1]).wait_recv()

    arrived = waves_ref[...].reshape(WAVES * 8, LANES)
    turned = lax.dot_general(
        arrived, spread_ref[...], (((0,), (0,)), ((), ())), preferred_element_type=jnp.float32
    )
    for h in range(2):
        turned_ref[...] = turned[:, h * LANES : (h + 1) * LANES]
        half = jnp.where(
            second_lane, turned_ref[pl.ds(1, CYCLE_PAD, 2), :], turned_ref[pl.ds(0, CYCLE_PAD, 2), :]
        )
        half = half * double
        plain_ref[h] = half
        cross_ref[h] = -sign * pltpu.roll(half, 64, 1)

    def transform(row):
        first = len_ref[first_lat + 2 * row]
        second = len_ref[first_lat + 2 * row + 1]
        length_lane = jnp.where(second_lane, second.astype(jnp.float32), first.astype(jnp.float32))
        weight_lane = jnp.where(
            second_lane, weight_ref[first_lat + 2 * row + 1], weight_ref[first_lat + 2 * row]
        )
        resolved = 2.0 * order_lane < length_lane
        factor = jnp.where(resolved, weight_lane / length_lane, 0.0)
        inner = inner_ref[row]
        plain = jnp.where(north, plain_ref[0, pl.ds(row, 1), :], plain_ref[1, pl.ds(row, 1), :])
        crossed = jnp.where(north, cross_ref[0, pl.ds(row, 1), :], cross_ref[1, pl.ds(row, 1), :])
        spread = jnp.where(resolved, plain * cos_ref[row] + crossed * sin_ref[row], 0.0).astype(jnp.bfloat16)
        images = jnp.dot(spread, inner, preferred_element_type=jnp.float32)
        in_first = position < first
        occupied = position < first + second
        values = jnp.where(in_first, images[:, :LANES], jnp.where(occupied, images[:, LANES:], 0.0))
        values = values.astype(jnp.bfloat16)
        for block in range(BLOCKS):
            grid_ref[row, :, block * LANES : (block + 1) * LANES] = values[2 * block : 2 * block + 2]
        wide = values.astype(jnp.float32)
        squared = wide * wide
        by_cycle = jnp.concatenate(
            [
                jnp.where(in_first, squared, 0.0).astype(jnp.bfloat16),
                jnp.where(in_first, 0.0, squared).astype(jnp.bfloat16),
            ],
            1,
        )
        partial = lax.dot_general(by_cycle, inner, NT, preferred_element_type=jnp.float32)
        cos_sum = jnp.sum((partial * cos_ref[row]).reshape(ROWS_PAD // 8, 8, LANES), 0)
        sin_sum = jnp.sum((partial * sin_ref[row]).reshape(ROWS_PAD // 8, 8, LANES), 0)
        total = cos_sum + sign * pltpu.roll(sin_sum, 64, 1)
        total = total + pltpu.roll(total, 4, 0)
        total = total + pltpu.roll(total, 2, 0)
        sum_ref[0, pl.ds(row, 1), :] = total[0:1, :] * factor
        sum_ref[1, pl.ds(row, 1), :] = total[1:2, :] * factor

    @pl.loop(0, GRID_ROWS // UNROLL)
    def _(step):
        for near in range(UNROLL):
            transform(step * UNROLL + near)

    sums = jnp.concatenate([sum_ref[0], sum_ref[1]], 1).astype(jnp.bfloat16)
    returned = jnp.concatenate(
        [
            lax.dot_general(gather_ref[cycle], sums, NT, preferred_element_type=jnp.float32)
            for cycle in range(2)
        ],
        1,
    )
    returned = jnp.dot(returned.astype(jnp.bfloat16), natural_ref[...], preferred_element_type=jnp.float32)
    ret_ref[...] = returned.astype(jnp.bfloat16).reshape(WAVES, 8, LANES)

    for d in range(1, WAVES):
        target = lax.rem(wave + d, WAVES)
        send(ret_ref.at[target], here.at[wave], turn_send.at[d - 1], turn_recv.at[d - 1], waves[d - 1])
    own_turn = pltpu.make_async_copy(ret_ref.at[wave], here.at[wave], local_sem.at[3])
    own_turn.start()
    own_turn.wait()
    for d in range(1, WAVES):
        block = here.at[lax.rem(wave + WAVES - d, WAVES)]
        remote(block, block, turn_send.at[d - 1], turn_recv.at[d - 1], waves[d - 1]).wait_recv()
    for d in range(1, LEAF):
        send(here, fields.at[leaf], line_send.at[d - 1], line_recv.at[d - 1], leaves[d - 1])
    own_line = pltpu.make_async_copy(here, fields.at[leaf], local_sem.at[4])
    own_line.start()
    own_line.wait()
    for d in range(1, LEAF):
        block = fields.at[lax.rem(leaf + LEAF - d, LEAF)]
        remote(block, block, line_send.at[d - 1], line_recv.at[d - 1], leaves[d - 1]).wait_recv()
    columns = jnp.concatenate(
        [fields[:, w].reshape(LEAF * 8, LANES)[:, :OWN].astype(jnp.float32) for w in range(WAVES)], 1
    ).astype(jnp.bfloat16)
    product = lax.dot_general(
        columns, panel_ref[...].reshape(width, LATS), NT, preferred_element_type=jnp.float32
    )
    product = jnp.where(kept, product, 0.0)
    product = jnp.where(negated, -product, product)
    narrow = lax.broadcasted_iota(jnp.int32, (width, SPAN), 0) // 2 == lax.broadcasted_iota(jnp.int32, (width, SPAN), 1)
    product = jnp.dot(
        product, jnp.where(narrow, 1.0, 0.0), precision=lax.Precision.HIGHEST, preferred_element_type=jnp.float32
    )
    piece[...] = product.reshape(LEAF, 8, SPAN)
    for d in range(1, LEAF):
        target = lax.rem(leaf + d, LEAF)
        send(piece.at[target], final.at[leaf], piece_send.at[d - 1], piece_recv.at[d - 1], leaves[d - 1])
    own_piece = pltpu.make_async_copy(piece.at[leaf], final.at[leaf], local_sem.at[5])
    own_piece.start()
    own_piece.wait()
    for d in range(1, LEAF):
        block = final.at[lax.rem(leaf + LEAF - d, LEAF)]
        remote(block, block, piece_send.at[d - 1], piece_recv.at[d - 1], leaves[d - 1]).wait_recv()
    pieces = [final[k] for k in range(LEAF)]
    result = jnp.concatenate(
        [pieces[k][:, y * RUN : (y + 1) * RUN] for y in range(LINES) for k in range(LEAF)], 1
    )
    for s in range(2):
        out_ref[s] = result[4 * s : 4 * s + 2] + result[4 * s + 2 : 4 * s + 4]
    for copy in copies:
        copy.wait_send()


def put_kernel(source, target, held, arrive, leave):
    count, size = held.shape[0], held.shape[1]
    spans = [pl.ds(part * size, size) for part in range(count)]
    incoming = [pltpu.make_async_copy(source.at[spans[i]], held.at[i], arrive.at[i]) for i in range(count)]
    outgoing = [pltpu.make_async_copy(held.at[i], target.at[spans[i]], leave.at[i]) for i in range(count)]
    for copy in incoming:
        copy.start()
    for i in range(count):
        incoming[i].wait()
        outgoing[i].start()
    for copy in outgoing:
        copy.wait()


def per_device(spec, legendre, gauss_w, cycle_len, wave_map):
    slots_dev = spec.shape[0]
    depth = legendre.shape[1] * slots_dev
    panel = legendre.transpose(1, 0, 2).reshape(depth, LATS)
    doubled = jnp.broadcast_to(spec, (slots_dev, 2, 2, DEGREES)).reshape(8, DEGREES)
    line = np.arange(WAVES * 8)
    line_slot, line_half, line_part = line // 8 * 2 + line % 8 // 4, line // 2 % 2, line % 2
    both = np.arange(2 * LANES)
    both_half, both_part, both_cycle, both_slot = both // LANES, both // 64 % 2, both // 32 % 2, both % 32
    match = (
        (line_slot[:, None] == both_slot) & (line_half[:, None] == both_half) & (line_part[:, None] == both_part)
    )
    spread = jnp.asarray(match, jnp.bfloat16)
    packed = np.arange(LANES)
    natural = (packed % CYCLE_PAD < GRID_ROWS)[:, None] & (
        (packed % CYCLE_PAD * 2 + packed // CYCLE_PAD)[:, None] == packed[None, :]
    )
    natural = jnp.asarray(natural, jnp.bfloat16)
    gather = jnp.asarray(np.stack([match & (both_cycle == 0), match & (both_cycle == 1)]), jnp.bfloat16)

    vmem = pl.BlockSpec(memory_space=pltpu.VMEM)
    smem = pl.BlockSpec(memory_space=pltpu.SMEM)
    dma = pltpu.SemaphoreType.DMA
    bf16, f32 = jnp.bfloat16, jnp.float32
    grid, spec_out = pl.pallas_call(
        whole_kernel,
        out_shape=(
            jax.ShapeDtypeStruct((GRID_ROWS, 2, LPAD), bf16),
            jax.ShapeDtypeStruct((slots_dev, 2, DEGREES), f32),
        ),
        in_specs=[smem] * 3 + [vmem] * 5,
        out_specs=(vmem, vmem),
        scratch_shapes=[
            pltpu.VMEM((LINES, depth, LATS), bf16),
            pltpu.VMEM((LEAF, 8, DEGREES), bf16),
            pltpu.VMEM((LEAF, 8, LATS), f32),
            pltpu.VMEM((LEAF - 1, 8, LATS), f32),
            pltpu.VMEM((WAVES, 8, LANES), bf16),
            pltpu.VMEM((WAVES, 8, LANES), bf16),
            pltpu.VMEM((LANES, LANES), f32),
            pltpu.VMEM((2, CYCLE_PAD, LANES), f32),
            pltpu.VMEM((2, CYCLE_PAD, LANES), f32),
            pltpu.VMEM((2, CYCLE_PAD, LANES), f32),
            pltpu.VMEM((GRID_ROWS, ROWS_PAD, LANES), f32),
            pltpu.VMEM((GRID_ROWS, ROWS_PAD, LANES), f32),
            pltpu.VMEM((GRID_ROWS, LANES, 2 * LANES), bf16),
            pltpu.VMEM((WAVES, 8, LANES), bf16),
            pltpu.VMEM((WAVES, 8, LANES), bf16),
            pltpu.VMEM((LEAF, WAVES, 8, LANES), bf16),
            pltpu.VMEM((LEAF, 8, SPAN), f32),
            pltpu.VMEM((LEAF, 8, SPAN), f32),
            dma((6,)), dma((2, 4, 2)), dma((2, 4, 2)),
            dma((LEAF - 1,)), dma((LEAF - 1,)), dma((LEAF - 1,)), dma((LEAF - 1,)),
            dma((WAVES - 1,)), dma((WAVES - 1,)), dma((WAVES - 1,)), dma((WAVES - 1,)),
            dma((LEAF - 1,)), dma((LEAF - 1,)), dma((LEAF - 1,)), dma((LEAF - 1,)),
        ],
        compiler_params=pltpu.CompilerParams(collective_id=0, has_side_effects=True),
        name="whole",
    )(wave_map, cycle_len, gauss_w, panel, doubled, spread, gather, natural)
    anywhere = pl.BlockSpec(memory_space=pl.ANY)
    grid = pl.pallas_call(
        put_kernel,
        out_shape=jax.ShapeDtypeStruct(grid.shape, bf16),
        in_specs=[anywhere],
        out_specs=anywhere,
        scratch_shapes=[pltpu.VMEM((5, GRID_ROWS // 5, 2, LPAD), bf16), dma((5,)), dma((5,))],
        name="put",
    )(grid)
    grid = grid.transpose(1, 0, 2).reshape(2, GRID_ROWS, 1, LPAD)
    return (grid, spec_out.reshape(slots_dev, 1, 2, DEGREES))


def solution(mesh):
    placed = (P("wave", "lev", None, None), P("wave", "lev", None), P(), P(), P())
    return jax.shard_map(
        per_device,
        mesh=mesh,
        in_specs=placed,
        out_specs=(P(None, "wave", "lev", None), P("wave", "lev", None, None)),
        check_vma=False,
    )
```

```python
import math

import jax
import jax.numpy as jnp
import numpy as np
from jax import lax
from jax.experimental import pallas as pl
from jax.experimental.pallas import tpu as pltpu
from jax.sharding import PartitionSpec as P

LPAD = 4864
LANES = 128
BLOCKS = LPAD // LANES
ROWS_PAD = 80
SLOT_PAD = 32
CYCLE_PAD = 64
WAVES = 12
LINES = 8
LEAF = 8
LATS = 1200
OWN = LATS // WAVES
GRID_ROWS = OWN // 2
DEGREES = 1280
SPAN = DEGREES // LEAF
RUN = SPAN // LINES
SLOTS = 24
EARLY_ROWS = 20
STEP_ROWS = 10
UNROLL = 10
TABLE_UNROLL = 1
CUTS = tuple((start, 8) for start in range(0, 40, 8))
MESH = pl.DeviceIdType.MESH
NT = (((1,), (1,)), ((), ()))


def cos_sin_turns(turns):
    quarter = turns * 4.0
    whole = jnp.round(quarter)
    rest = (quarter - whole) * (0.5 * math.pi)
    square = rest * rest
    sine = rest + rest * square * (
        -1.6666666666e-1 + square * (8.3333331e-3 + square * (-1.98412698e-4 + square * 2.7557319e-6))
    )
    cosine = 1.0 + square * (
        -0.5 + square * (4.16666667e-2 + square * (-1.388888889e-3 + square * (2.48015873e-5 - square * 2.7557319e-7)))
    )
    step = whole.astype(jnp.int32) & 3
    swap = (step & 1) == 1
    cos_base = jnp.where(swap, sine, cosine)
    sin_base = jnp.where(swap, cosine, sine)
    cos_value = jnp.where((step == 1) | (step == 2), -cos_base, cos_base)
    sin_value = jnp.where(step >= 2, -sin_base, sin_base)
    return cos_value, sin_value


def turns_of(product, length, inverse):
    whole = jnp.round(product * inverse)
    return (product - whole * length) * inverse


def remote(source, target, send, receive, device):
    return pltpu.make_async_remote_copy(
        src_ref=source, dst_ref=target, send_sem=send, recv_sem=receive,
        device_id=device, device_id_type=MESH,
    )


def order_of(map_ref, wave, slot):
    return map_ref[wave * 2 + slot] * DEGREES // SLOTS


def whole_kernel(
    map_ref, len_ref, weight_ref, stored_leg_ref, stored_spec_ref, spread_ref, gather_ref, natural_ref,
    grid_ref, out_ref,
    leg_ref, spec_ref, panel_ref, lhs, part, got, four, waves_ref, turned_ref, plain_ref, cross_ref, sum_ref,
    cos_ref, sin_ref, inner_ref, ret_ref, here, fields, piece, final,
    local_sem, ring_send, ring_recv, coef_send, coef_recv, part_send, part_recv,
    wave_send, wave_recv, turn_send, turn_recv, line_send, line_recv, piece_send, piece_recv,
):
    wave = lax.axis_index("wave")
    lev = lax.axis_index("lev")
    line = lax.div(lev, LEAF)
    leaf = lax.rem(lev, LEAF)
    ring = [{"lev": lax.rem(line + d, LINES) * LEAF + leaf} for d in (1, LINES - 1)]
    leaves = [{"lev": line * LEAF + lax.rem(leaf + d, LEAF)} for d in range(1, LEAF)]
    waves = [{"wave": lax.rem(wave + d, WAVES)} for d in range(1, WAVES)]
    peers = waves + leaves + ring
    barrier = pltpu.get_barrier_semaphore()
    for device in peers:
        pl.semaphore_signal(barrier, inc=1, device_id=device, device_id_type=MESH)

    for n in range(RUN):
        leg_ref[2 * n : 2 * n + 2, :] = stored_leg_ref[n]
    for s in range(2):
        for h in range(2):
            spec_ref[4 * s + 2 * h : 4 * s + 2 * h + 2, :] = stored_spec_ref[s]

    first_lat = wave * OWN
    lane = lax.broadcasted_iota(jnp.int32, (1, LANES), 1)
    order_lane = jnp.zeros((1, LANES), jnp.int32)
    for slot in range(SLOTS):
        order_lane = jnp.where(lane % SLOT_PAD == slot, map_ref[slot] * DEGREES // SLOTS, order_lane)
    order_lane = order_lane.astype(jnp.float32)
    double = jnp.where(lane % SLOT_PAD < SLOTS, jnp.where(order_lane == 0.0, 1.0, 2.0), 0.0)
    order_sub = jnp.broadcast_to(order_lane, (LANES, LANES)).T[:SLOT_PAD]
    lane_f = lax.broadcasted_iota(jnp.int32, (ROWS_PAD, LANES), 1)
    row_f = lax.broadcasted_iota(jnp.int32, (ROWS_PAD, LANES), 0)
    block_start = (row_f // 2) * LANES
    position = block_start + lane_f
    block_start = block_start.astype(jnp.float32)
    second_lane = lane // SLOT_PAD % 2 == 1
    sign = jnp.where(lane < 64, 1.0, -1.0)
    inner_lane = lax.broadcasted_iota(jnp.int32, (SLOT_PAD, LANES), 1).astype(jnp.float32)
    inner_product = order_sub * inner_lane
    north = row_f % 2 == 0
    zero_block = jnp.zeros((SLOT_PAD, LANES), jnp.bfloat16)

    def tables(row):
        first_f = len_ref[first_lat + 2 * row].astype(jnp.float32)
        second_f = len_ref[first_lat + 2 * row + 1].astype(jnp.float32)
        length_lane = jnp.where(second_lane, second_f, first_f)
        start_lane = jnp.where(second_lane, first_f, 0.0)
        inverse_lane = 1.0 / length_lane
        inv_first = inverse_lane[:, 0:1]
        inv_second = inverse_lane[:, SLOT_PAD : SLOT_PAD + 1]
        outer = order_lane * (block_start - start_lane)
        outer_cos, outer_sin = cos_sin_turns(turns_of(outer, length_lane, inverse_lane))
        cos_ref[row] = outer_cos
        sin_ref[row] = outer_sin
        cos_a, sin_a = cos_sin_turns(turns_of(inner_product, first_f, inv_first))
        cos_b, sin_b = cos_sin_turns(turns_of(inner_product, second_f, inv_second))
        inner_ref[row] = jnp.concatenate(
            [
                jnp.concatenate([cos_a.astype(jnp.bfloat16), zero_block], 1),
                jnp.concatenate([zero_block, cos_b.astype(jnp.bfloat16)], 1),
                jnp.concatenate([(-sin_a).astype(jnp.bfloat16), zero_block], 1),
                jnp.concatenate([zero_block, (-sin_b).astype(jnp.bfloat16)], 1),
            ],
            0,
        )

    def table_rows(start, count):
        @pl.loop(0, count // TABLE_UNROLL)
        def _(step):
            for near in range(TABLE_UNROLL):
                tables(start + step * TABLE_UNROLL + near)

    table_rows(0, EARLY_ROWS)

    pl.semaphore_wait(barrier, len(peers))

    copies = []

    def send(*details):
        copy = remote(*details)
        copy.start()
        copies.append(copy)

    def ring_copy(source, block, way, hop, cut):
        start, size = CUTS[cut]
        target = panel_ref.at[block, pl.ds(start, size), :]
        return (
            target if source is None else source.at[pl.ds(start, size), :],
            target,
            ring_send.at[way, hop - 1, cut],
            ring_recv.at[way, hop - 1, cut],
            ring[way],
        )

    for cut in range(len(CUTS)):
        for way in range(2):
            send(*ring_copy(leg_ref, line, way, 1, cut))
    own_panel = pltpu.make_async_copy(leg_ref, panel_ref.at[line], local_sem.at[0])
    own_panel.start()
    for d in range(1, LEAF):
        send(spec_ref, lhs.at[leaf], coef_send.at[d - 1], coef_recv.at[d - 1], leaves[d - 1])
    own_coef = pltpu.make_async_copy(spec_ref, lhs.at[leaf], local_sem.at[1])
    own_coef.start()

    for hop in range(1, 4):
        if hop == 1:
            table_rows(EARLY_ROWS, STEP_ROWS)
        for cut in range(len(CUTS)):
            for way in range(2):
                origin = lax.rem(line + (LINES - hop if way == 0 else hop), LINES)
                remote(*ring_copy(None, origin, way, hop, cut)).wait_recv()
                if hop < 3 or cut % 2 == way:
                    send(*ring_copy(None, origin, way, hop + 1, cut))

    width = panel_ref.shape[0] * panel_ref.shape[1]
    column = lax.broadcasted_iota(jnp.int32, (1, width), 1)
    degree = column // (2 * RUN) * SPAN + leaf * RUN + column % (2 * RUN) // 2
    widen = jnp.where(lax.broadcasted_iota(jnp.int32, (DEGREES, width), 0) == degree, 1.0, 0.0)
    widen = widen.astype(jnp.bfloat16)
    four[...] = jnp.zeros_like(four)
    sum_ref[...] = jnp.zeros_like(sum_ref)
    own_coef.wait()
    for d in range(1, LEAF):
        block = lhs.at[lax.rem(leaf + LEAF - d, LEAF)]
        remote(block, block, coef_send.at[d - 1], coef_recv.at[d - 1], leaves[d - 1]).wait_recv()
    coef = jnp.dot(lhs[...].reshape(LEAF * 8, DEGREES), widen, preferred_element_type=jnp.float32)
    kind = lax.broadcasted_iota(jnp.int32, coef.shape, 0) % 8
    order = jnp.where(kind >= 4, order_of(map_ref, wave, 1), order_of(map_ref, wave, 0))
    kept = (kind // 4 == column % 2) & (degree >= order)
    negated = (kind // 2 % 2 == 1) & ((degree + order) % 2 == 1)
    coef = jnp.where(kept, coef, 0.0)
    coef = jnp.where(negated, -coef, coef).astype(jnp.bfloat16)
    own_panel.wait()
    far = lax.rem(line + LINES // 2, LINES)
    for cut in range(len(CUTS)):
        remote(*ring_copy(None, far, cut % 2, 4, cut)).wait_recv()
    product = jnp.dot(coef, panel_ref[...].reshape(width, LATS), preferred_element_type=jnp.float32)
    part[...] = product.reshape(LEAF, 8, LATS)
    for d in range(1, LEAF):
        target = lax.rem(leaf + d, LEAF)
        send(part.at[target], got.at[d - 1], part_send.at[d - 1], part_recv.at[d - 1], leaves[d - 1])
    table_rows(EARLY_ROWS + STEP_ROWS, STEP_ROWS)
    total = part[leaf]
    for d in range(1, LEAF):
        block = got.at[d - 1]
        remote(block, block, part_send.at[d - 1], part_recv.at[d - 1], leaves[d - 1]).wait_recv()
        total = total + got[d - 1]
    for w in range(WAVES):
        four[w, :, :OWN] = total[:, w * OWN : (w + 1) * OWN].astype(jnp.bfloat16)
    for d in range(1, WAVES):
        target = lax.rem(wave + d, WAVES)
        send(four.at[target], waves_ref.at[wave], wave_send.at[d - 1], wave_recv.at[d - 1], waves[d - 1])
    own_wave = pltpu.make_async_copy(four.at[wave], waves_ref.at[wave], local_sem.at[2])
    own_wave.start()
    table_rows(EARLY_ROWS + 2 * STEP_ROWS, STEP_ROWS)
    own_wave.wait()
    for d in range(1, WAVES):
        block = waves_ref.at[lax.rem(wave + WAVES - d, WAVES)]
        remote(block, block, wave_send.at[d - 1], wave_recv.at[d - 1], waves[d - 1]).wait_recv()

    arrived = waves_ref[...].reshape(WAVES * 8, LANES)
    turned = lax.dot_general(
        arrived, spread_ref[...], (((0,), (0,)), ((), ())), preferred_element_type=jnp.float32
    )
    for h in range(2):
        turned_ref[...] = turned[:, h * LANES : (h + 1) * LANES]
        half = jnp.where(
            second_lane, turned_ref[pl.ds(1, CYCLE_PAD, 2), :], turned_ref[pl.ds(0, CYCLE_PAD, 2), :]
        )
        half = half * double
        plain_ref[h] = half
        cross_ref[h] = -sign * pltpu.roll(half, 64, 1)

    def transform(row):
        first = len_ref[first_lat + 2 * row]
        second = len_ref[first_lat + 2 * row + 1]
        length_lane = jnp.where(second_lane, second.astype(jnp.float32), first.astype(jnp.float32))
        weight_lane = jnp.where(
            second_lane, weight_ref[first_lat + 2 * row + 1], weight_ref[first_lat + 2 * row]
        )
        resolved = 2.0 * order_lane < length_lane
        factor = jnp.where(resolved, weight_lane / length_lane, 0.0)
        inner = inner_ref[row]
        plain = jnp.where(north, plain_ref[0, pl.ds(row, 1), :], plain_ref[1, pl.ds(row, 1), :])
        crossed = jnp.where(north, cross_ref[0, pl.ds(row, 1), :], cross_ref[1, pl.ds(row, 1), :])
        spread = jnp.where(resolved, plain * cos_ref[row] + crossed * sin_ref[row], 0.0).astype(jnp.bfloat16)
        images = jnp.dot(spread, inner, preferred_element_type=jnp.float32)
        in_first = position < first
        occupied = position < first + second
        values = jnp.where(in_first, images[:, :LANES], jnp.where(occupied, images[:, LANES:], 0.0))
        values = values.astype(jnp.bfloat16)
        for block in range(BLOCKS):
            grid_ref[row, :, block * LANES : (block + 1) * LANES] = values[2 * block : 2 * block + 2]
        wide = values.astype(jnp.float32)
        squared = wide * wide
        by_cycle = jnp.concatenate(
            [
                jnp.where(in_first, squared, 0.0).astype(jnp.bfloat16),
                jnp.where(in_first, 0.0, squared).astype(jnp.bfloat16),
            ],
            1,
        )
        partial = lax.dot_general(by_cycle, inner, NT, preferred_element_type=jnp.float32)
        cos_sum = jnp.sum((partial * cos_ref[row]).reshape(ROWS_PAD // 8, 8, LANES), 0)
        sin_sum = jnp.sum((partial * sin_ref[row]).reshape(ROWS_PAD // 8, 8, LANES), 0)
        total = cos_sum + sign * pltpu.roll(sin_sum, 64, 1)
        total = total + pltpu.roll(total, 4, 0)
        total = total + pltpu.roll(total, 2, 0)
        sum_ref[0, pl.ds(row, 1), :] = total[0:1, :] * factor
        sum_ref[1, pl.ds(row, 1), :] = total[1:2, :] * factor

    @pl.loop(0, GRID_ROWS // UNROLL)
    def _(step):
        for near in range(UNROLL):
            transform(step * UNROLL + near)

    sums = jnp.concatenate([sum_ref[0], sum_ref[1]], 1).astype(jnp.bfloat16)
    returned = jnp.concatenate(
        [
            lax.dot_general(gather_ref[cycle], sums, NT, preferred_element_type=jnp.float32)
            for cycle in range(2)
        ],
        1,
    )
    returned = jnp.dot(returned.astype(jnp.bfloat16), natural_ref[...], preferred_element_type=jnp.float32)
    ret_ref[...] = returned.astype(jnp.bfloat16).reshape(WAVES, 8, LANES)

    for d in range(1, WAVES):
        target = lax.rem(wave + d, WAVES)
        send(ret_ref.at[target], here.at[wave], turn_send.at[d - 1], turn_recv.at[d - 1], waves[d - 1])
    own_turn = pltpu.make_async_copy(ret_ref.at[wave], here.at[wave], local_sem.at[3])
    own_turn.start()
    own_turn.wait()
    for d in range(1, WAVES):
        block = here.at[lax.rem(wave + WAVES - d, WAVES)]
        remote(block, block, turn_send.at[d - 1], turn_recv.at[d - 1], waves[d - 1]).wait_recv()
    for d in range(1, LEAF):
        send(here, fields.at[leaf], line_send.at[d - 1], line_recv.at[d - 1], leaves[d - 1])
    own_line = pltpu.make_async_copy(here, fields.at[leaf], local_sem.at[4])
    own_line.start()
    own_line.wait()
    for d in range(1, LEAF):
        block = fields.at[lax.rem(leaf + LEAF - d, LEAF)]
        remote(block, block, line_send.at[d - 1], line_recv.at[d - 1], leaves[d - 1]).wait_recv()
    columns = jnp.concatenate(
        [fields[:, w].reshape(LEAF * 8, LANES)[:, :OWN].astype(jnp.float32) for w in range(WAVES)], 1
    ).astype(jnp.bfloat16)
    product = lax.dot_general(
        columns, panel_ref[...].reshape(width, LATS), NT, preferred_element_type=jnp.float32
    )
    product = jnp.where(kept, product, 0.0)
    product = jnp.where(negated, -product, product)
    narrow = lax.broadcasted_iota(jnp.int32, (width, SPAN), 0) // 2 == lax.broadcasted_iota(jnp.int32, (width, SPAN), 1)
    product = jnp.dot(
        product, jnp.where(narrow, 1.0, 0.0), precision=lax.Precision.HIGHEST, preferred_element_type=jnp.float32
    )
    piece[...] = product.reshape(LEAF, 8, SPAN)
    for d in range(1, LEAF):
        target = lax.rem(leaf + d, LEAF)
        send(piece.at[target], final.at[leaf], piece_send.at[d - 1], piece_recv.at[d - 1], leaves[d - 1])
    own_piece = pltpu.make_async_copy(piece.at[leaf], final.at[leaf], local_sem.at[5])
    own_piece.start()
    own_piece.wait()
    for d in range(1, LEAF):
        block = final.at[lax.rem(leaf + LEAF - d, LEAF)]
        remote(block, block, piece_send.at[d - 1], piece_recv.at[d - 1], leaves[d - 1]).wait_recv()
    pieces = [final[k] for k in range(LEAF)]
    result = jnp.concatenate(
        [pieces[k][:, y * RUN : (y + 1) * RUN] for y in range(LINES) for k in range(LEAF)], 1
    )
    for s in range(2):
        out_ref[s] = result[4 * s : 4 * s + 2] + result[4 * s + 2 : 4 * s + 4]
    for copy in copies:
        copy.wait_send()


def put_kernel(source, target, held, arrive, leave):
    count, size = held.shape[0], held.shape[1]
    spans = [pl.ds(part * size, size) for part in range(count)]
    incoming = [pltpu.make_async_copy(source.at[spans[i]], held.at[i], arrive.at[i]) for i in range(count)]
    outgoing = [pltpu.make_async_copy(held.at[i], target.at[spans[i]], leave.at[i]) for i in range(count)]
    for copy in incoming:
        copy.start()
    for i in range(count):
        incoming[i].wait()
        outgoing[i].start()
    for copy in outgoing:
        copy.wait()


def per_device(spec, legendre, gauss_w, cycle_len, wave_map):
    slots_dev = spec.shape[0]
    depth = legendre.shape[1] * slots_dev
    panel = legendre.transpose(1, 0, 2)
    coefficients = spec.reshape(slots_dev, 2, DEGREES)
    line = np.arange(WAVES * 8)
    line_slot, line_half, line_part = line // 8 * 2 + line % 8 // 4, line // 2 % 2, line % 2
    both = np.arange(2 * LANES)
    both_half, both_part, both_cycle, both_slot = both // LANES, both // 64 % 2, both // 32 % 2, both % 32
    match = (
        (line_slot[:, None] == both_slot) & (line_half[:, None] == both_half) & (line_part[:, None] == both_part)
    )
    spread = jnp.asarray(match, jnp.bfloat16)
    packed = np.arange(LANES)
    natural = (packed % CYCLE_PAD < GRID_ROWS)[:, None] & (
        (packed % CYCLE_PAD * 2 + packed // CYCLE_PAD)[:, None] == packed[None, :]
    )
    natural = jnp.asarray(natural, jnp.bfloat16)
    gather = jnp.asarray(np.stack([match & (both_cycle == 0), match & (both_cycle == 1)]), jnp.bfloat16)

    vmem = pl.BlockSpec(memory_space=pltpu.VMEM)
    smem = pl.BlockSpec(memory_space=pltpu.SMEM)
    dma = pltpu.SemaphoreType.DMA
    bf16, f32 = jnp.bfloat16, jnp.float32
    grid, spec_out = pl.pallas_call(
        whole_kernel,
        out_shape=(
            jax.ShapeDtypeStruct((GRID_ROWS, 2, LPAD), bf16),
            jax.ShapeDtypeStruct((slots_dev, 2, DEGREES), f32),
        ),
        in_specs=[smem] * 3 + [vmem] * 5,
        out_specs=(vmem, vmem),
        scratch_shapes=[
            pltpu.VMEM((depth, LATS), bf16),
            pltpu.VMEM((8, DEGREES), bf16),
            pltpu.VMEM((LINES, depth, LATS), bf16),
            pltpu.VMEM((LEAF, 8, DEGREES), bf16),
            pltpu.VMEM((LEAF, 8, LATS), f32),
            pltpu.VMEM((LEAF - 1, 8, LATS), f32),
            pltpu.VMEM((WAVES, 8, LANES), bf16),
            pltpu.VMEM((WAVES, 8, LANES), bf16),
            pltpu.VMEM((LANES, LANES), f32),
            pltpu.VMEM((2, CYCLE_PAD, LANES), f32),
            pltpu.VMEM((2, CYCLE_PAD, LANES), f32),
            pltpu.VMEM((2, CYCLE_PAD, LANES), f32),
            pltpu.VMEM((GRID_ROWS, ROWS_PAD, LANES), f32),
            pltpu.VMEM((GRID_ROWS, ROWS_PAD, LANES), f32),
            pltpu.VMEM((GRID_ROWS, LANES, 2 * LANES), bf16),
            pltpu.VMEM((WAVES, 8, LANES), bf16),
            pltpu.VMEM((WAVES, 8, LANES), bf16),
            pltpu.VMEM((LEAF, WAVES, 8, LANES), bf16),
            pltpu.VMEM((LEAF, 8, SPAN), f32),
            pltpu.VMEM((LEAF, 8, SPAN), f32),
            dma((6,)), dma((2, 4, len(CUTS))), dma((2, 4, len(CUTS))),
            dma((LEAF - 1,)), dma((LEAF - 1,)), dma((LEAF - 1,)), dma((LEAF - 1,)),
            dma((WAVES - 1,)), dma((WAVES - 1,)), dma((WAVES - 1,)), dma((WAVES - 1,)),
            dma((LEAF - 1,)), dma((LEAF - 1,)), dma((LEAF - 1,)), dma((LEAF - 1,)),
        ],
        compiler_params=pltpu.CompilerParams(collective_id=0, has_side_effects=True),
        name="whole",
    )(wave_map, cycle_len, gauss_w, panel, coefficients, spread, gather, natural)
    anywhere = pl.BlockSpec(memory_space=pl.ANY)
    grid = pl.pallas_call(
        put_kernel,
        out_shape=jax.ShapeDtypeStruct(grid.shape, bf16),
        in_specs=[anywhere],
        out_specs=anywhere,
        scratch_shapes=[pltpu.VMEM((5, GRID_ROWS // 5, 2, LPAD), bf16), dma((5,)), dma((5,))],
        name="put",
    )(grid)
    grid = grid.transpose(1, 0, 2).reshape(2, GRID_ROWS, 1, LPAD)
    return (grid, spec_out.reshape(slots_dev, 1, 2, DEGREES))


def solution(mesh):
    placed = (P("wave", "lev", None, None), P("wave", "lev", None), P(), P(), P())
    return jax.shard_map(
        per_device,
        mesh=mesh,
        in_specs=placed,
        out_specs=(P(None, "wave", "lev", None), P("wave", "lev", None, None)),
        check_vma=False,
    )
```

```python
import math

import jax
import jax.numpy as jnp
import numpy as np
from jax import lax
from jax.experimental import pallas as pl
from jax.experimental.pallas import tpu as pltpu
from jax.sharding import PartitionSpec as P

LPAD = 4864
LANES = 128
BLOCKS = LPAD // LANES
ROWS_PAD = 80
SLOT_PAD = 32
CYCLE_PAD = 64
WAVES = 12
LINES = 8
LEAF = 8
LATS = 1200
OWN = LATS // WAVES
GRID_ROWS = OWN // 2
DEGREES = 1280
SPAN = DEGREES // LEAF
RUN = SPAN // LINES
SLOTS = 24
EARLY_ROWS = 20
STEP_ROWS = 10
UNROLL = 10
TABLE_UNROLL = 1
CUTS = tuple((start, 8) for start in range(0, 40, 8))
FAR_LEAVES = (4, 3, 5, 2, 6, 1, 7)
FAR_WAVES = (6, 5, 7, 4, 8, 3, 9, 2, 10, 1, 11)
MESH = pl.DeviceIdType.MESH
NT = (((1,), (1,)), ((), ()))


def cos_sin_turns(turns):
    quarter = turns * 4.0
    whole = jnp.round(quarter)
    rest = (quarter - whole) * (0.5 * math.pi)
    square = rest * rest
    sine = rest + rest * square * (
        -1.6666666666e-1 + square * (8.3333331e-3 + square * (-1.98412698e-4 + square * 2.7557319e-6))
    )
    cosine = 1.0 + square * (
        -0.5 + square * (4.16666667e-2 + square * (-1.388888889e-3 + square * (2.48015873e-5 - square * 2.7557319e-7)))
    )
    step = whole.astype(jnp.int32) & 3
    swap = (step & 1) == 1
    cos_base = jnp.where(swap, sine, cosine)
    sin_base = jnp.where(swap, cosine, sine)
    cos_value = jnp.where((step == 1) | (step == 2), -cos_base, cos_base)
    sin_value = jnp.where(step >= 2, -sin_base, sin_base)
    return cos_value, sin_value


def turns_of(product, length, inverse):
    whole = jnp.round(product * inverse)
    return (product - whole * length) * inverse


def remote(source, target, send, receive, device):
    return pltpu.make_async_remote_copy(
        src_ref=source, dst_ref=target, send_sem=send, recv_sem=receive,
        device_id=device, device_id_type=MESH,
    )


def order_of(map_ref, wave, slot):
    return map_ref[wave * 2 + slot] * DEGREES // SLOTS


def whole_kernel(
    map_ref, len_ref, weight_ref, stored_leg_ref, stored_spec_ref, spread_ref, gather_ref, natural_ref,
    grid_out_ref, out_ref,
    grid_ref, leg_ref, spec_ref, panel_ref, lhs, part, got, four, waves_ref, turned_ref, plain_ref, cross_ref, sum_ref,
    cos_ref, sin_ref, inner_ref, ret_ref, here, fields, piece, final,
    local_sem, ring_send, ring_recv, coef_send, coef_recv, part_send, part_recv,
    wave_send, wave_recv, turn_send, turn_recv, line_send, line_recv, piece_send, piece_recv,
):
    wave = lax.axis_index("wave")
    lev = lax.axis_index("lev")
    line = lax.div(lev, LEAF)
    leaf = lax.rem(lev, LEAF)
    ring = [{"lev": lax.rem(line + d, LINES) * LEAF + leaf} for d in (1, LINES - 1)]
    leaves = [{"lev": line * LEAF + lax.rem(leaf + d, LEAF)} for d in range(1, LEAF)]
    waves = [{"wave": lax.rem(wave + d, WAVES)} for d in range(1, WAVES)]
    peers = waves + leaves + ring
    barrier = pltpu.get_barrier_semaphore()
    for device in peers:
        pl.semaphore_signal(barrier, inc=1, device_id=device, device_id_type=MESH)

    for n in range(RUN):
        leg_ref[2 * n : 2 * n + 2, :] = stored_leg_ref[n]
    for s in range(2):
        for h in range(2):
            spec_ref[4 * s + 2 * h : 4 * s + 2 * h + 2, :] = stored_spec_ref[s]

    first_lat = wave * OWN
    lane = lax.broadcasted_iota(jnp.int32, (1, LANES), 1)
    order_lane = jnp.zeros((1, LANES), jnp.int32)
    for slot in range(SLOTS):
        order_lane = jnp.where(lane % SLOT_PAD == slot, map_ref[slot] * DEGREES // SLOTS, order_lane)
    order_lane = order_lane.astype(jnp.float32)
    double = jnp.where(lane % SLOT_PAD < SLOTS, jnp.where(order_lane == 0.0, 1.0, 2.0), 0.0)
    order_sub = jnp.broadcast_to(order_lane, (LANES, LANES)).T[:SLOT_PAD]
    lane_f = lax.broadcasted_iota(jnp.int32, (ROWS_PAD, LANES), 1)
    row_f = lax.broadcasted_iota(jnp.int32, (ROWS_PAD, LANES), 0)
    block_start = (row_f // 2) * LANES
    position = block_start + lane_f
    block_start = block_start.astype(jnp.float32)
    second_lane = lane // SLOT_PAD % 2 == 1
    sign = jnp.where(lane < 64, 1.0, -1.0)
    inner_lane = lax.broadcasted_iota(jnp.int32, (SLOT_PAD, LANES), 1).astype(jnp.float32)
    inner_product = order_sub * inner_lane
    north = row_f % 2 == 0
    zero_block = jnp.zeros((SLOT_PAD, LANES), jnp.bfloat16)

    def tables(row):
        first_f = len_ref[first_lat + 2 * row].astype(jnp.float32)
        second_f = len_ref[first_lat + 2 * row + 1].astype(jnp.float32)
        length_lane = jnp.where(second_lane, second_f, first_f)
        start_lane = jnp.where(second_lane, first_f, 0.0)
        inverse_lane = 1.0 / length_lane
        inv_first = inverse_lane[:, 0:1]
        inv_second = inverse_lane[:, SLOT_PAD : SLOT_PAD + 1]
        outer = order_lane * (block_start - start_lane)
        outer_cos, outer_sin = cos_sin_turns(turns_of(outer, length_lane, inverse_lane))
        cos_ref[row] = outer_cos
        sin_ref[row] = outer_sin
        cos_a, sin_a = cos_sin_turns(turns_of(inner_product, first_f, inv_first))
        cos_b, sin_b = cos_sin_turns(turns_of(inner_product, second_f, inv_second))
        inner_ref[row] = jnp.concatenate(
            [
                jnp.concatenate([cos_a.astype(jnp.bfloat16), zero_block], 1),
                jnp.concatenate([zero_block, cos_b.astype(jnp.bfloat16)], 1),
                jnp.concatenate([(-sin_a).astype(jnp.bfloat16), zero_block], 1),
                jnp.concatenate([zero_block, (-sin_b).astype(jnp.bfloat16)], 1),
            ],
            0,
        )

    def table_rows(start, count):
        @pl.loop(0, count // TABLE_UNROLL)
        def _(step):
            for near in range(TABLE_UNROLL):
                tables(start + step * TABLE_UNROLL + near)

    table_rows(0, EARLY_ROWS)

    pl.semaphore_wait(barrier, len(peers))

    copies = []

    def send(*details):
        copy = remote(*details)
        copy.start()
        copies.append(copy)

    def ring_copy(source, block, way, hop, cut):
        start, size = CUTS[cut]
        target = panel_ref.at[block, pl.ds(start, size), :]
        return (
            target if source is None else source.at[pl.ds(start, size), :],
            target,
            ring_send.at[way, hop - 1, cut],
            ring_recv.at[way, hop - 1, cut],
            ring[way],
        )

    for cut in range(len(CUTS)):
        for way in range(2):
            send(*ring_copy(leg_ref, line, way, 1, cut))
    own_panel = pltpu.make_async_copy(leg_ref, panel_ref.at[line], local_sem.at[0])
    own_panel.start()
    for d in range(1, LEAF):
        send(spec_ref, lhs.at[leaf], coef_send.at[d - 1], coef_recv.at[d - 1], leaves[d - 1])
    own_coef = pltpu.make_async_copy(spec_ref, lhs.at[leaf], local_sem.at[1])
    own_coef.start()

    for hop in range(1, 4):
        if hop == 1:
            table_rows(EARLY_ROWS, STEP_ROWS)
        for cut in range(len(CUTS)):
            for way in range(2):
                origin = lax.rem(line + (LINES - hop if way == 0 else hop), LINES)
                remote(*ring_copy(None, origin, way, hop, cut)).wait_recv()
                if hop < 3 or cut % 2 == way:
                    send(*ring_copy(None, origin, way, hop + 1, cut))

    width = panel_ref.shape[0] * panel_ref.shape[1]
    column = lax.broadcasted_iota(jnp.int32, (1, width), 1)
    degree = column // (2 * RUN) * SPAN + leaf * RUN + column % (2 * RUN) // 2
    widen = jnp.where(lax.broadcasted_iota(jnp.int32, (DEGREES, width), 0) == degree, 1.0, 0.0)
    widen = widen.astype(jnp.bfloat16)
    four[...] = jnp.zeros_like(four)
    sum_ref[...] = jnp.zeros_like(sum_ref)
    own_coef.wait()
    for d in range(1, LEAF):
        block = lhs.at[lax.rem(leaf + LEAF - d, LEAF)]
        remote(block, block, coef_send.at[d - 1], coef_recv.at[d - 1], leaves[d - 1]).wait_recv()
    coef = jnp.dot(lhs[...].reshape(LEAF * 8, DEGREES), widen, preferred_element_type=jnp.float32)
    kind = lax.broadcasted_iota(jnp.int32, coef.shape, 0) % 8
    order = jnp.where(kind >= 4, order_of(map_ref, wave, 1), order_of(map_ref, wave, 0))
    kept = (kind // 4 == column % 2) & (degree >= order)
    negated = (kind // 2 % 2 == 1) & ((degree + order) % 2 == 1)
    coef = jnp.where(kept, coef, 0.0)
    coef = jnp.where(negated, -coef, coef).astype(jnp.bfloat16)
    own_panel.wait()
    far = lax.rem(line + LINES // 2, LINES)
    for cut in range(len(CUTS)):
        remote(*ring_copy(None, far, cut % 2, 4, cut)).wait_recv()
    product = jnp.dot(coef, panel_ref[...].reshape(width, LATS), preferred_element_type=jnp.float32)
    part[...] = product.reshape(LEAF, 8, LATS)
    for d in FAR_LEAVES:
        target = lax.rem(leaf + d, LEAF)
        send(part.at[target], got.at[d - 1], part_send.at[d - 1], part_recv.at[d - 1], leaves[d - 1])
    table_rows(EARLY_ROWS + STEP_ROWS, STEP_ROWS)
    total = part[leaf]
    for d in range(1, LEAF):
        block = got.at[d - 1]
        remote(block, block, part_send.at[d - 1], part_recv.at[d - 1], leaves[d - 1]).wait_recv()
        total = total + got[d - 1]
    for w in range(WAVES):
        four[w, :, :OWN] = total[:, w * OWN : (w + 1) * OWN].astype(jnp.bfloat16)
    for d in FAR_WAVES:
        target = lax.rem(wave + d, WAVES)
        send(four.at[target], waves_ref.at[wave], wave_send.at[d - 1], wave_recv.at[d - 1], waves[d - 1])
    own_wave = pltpu.make_async_copy(four.at[wave], waves_ref.at[wave], local_sem.at[2])
    own_wave.start()
    table_rows(EARLY_ROWS + 2 * STEP_ROWS, STEP_ROWS)
    own_wave.wait()
    for d in range(1, WAVES):
        block = waves_ref.at[lax.rem(wave + WAVES - d, WAVES)]
        remote(block, block, wave_send.at[d - 1], wave_recv.at[d - 1], waves[d - 1]).wait_recv()

    arrived = waves_ref[...].reshape(WAVES * 8, LANES)
    turned = lax.dot_general(
        arrived, spread_ref[...], (((0,), (0,)), ((), ())), preferred_element_type=jnp.float32
    )
    for h in range(2):
        turned_ref[...] = turned[:, h * LANES : (h + 1) * LANES]
        half = jnp.where(
            second_lane, turned_ref[pl.ds(1, CYCLE_PAD, 2), :], turned_ref[pl.ds(0, CYCLE_PAD, 2), :]
        )
        half = half * double
        plain_ref[h] = half
        cross_ref[h] = -sign * pltpu.roll(half, 64, 1)

    def transform(row):
        first = len_ref[first_lat + 2 * row]
        second = len_ref[first_lat + 2 * row + 1]
        length_lane = jnp.where(second_lane, second.astype(jnp.float32), first.astype(jnp.float32))
        weight_lane = jnp.where(
            second_lane, weight_ref[first_lat + 2 * row + 1], weight_ref[first_lat + 2 * row]
        )
        resolved = 2.0 * order_lane < length_lane
        factor = jnp.where(resolved, weight_lane / length_lane, 0.0)
        inner = inner_ref[row]
        plain = jnp.where(north, plain_ref[0, pl.ds(row, 1), :], plain_ref[1, pl.ds(row, 1), :])
        crossed = jnp.where(north, cross_ref[0, pl.ds(row, 1), :], cross_ref[1, pl.ds(row, 1), :])
        spread = jnp.where(resolved, plain * cos_ref[row] + crossed * sin_ref[row], 0.0).astype(jnp.bfloat16)
        images = jnp.dot(spread, inner, preferred_element_type=jnp.float32)
        in_first = position < first
        occupied = position < first + second
        values = jnp.where(in_first, images[:, :LANES], jnp.where(occupied, images[:, LANES:], 0.0))
        values = values.astype(jnp.bfloat16)
        for block in range(BLOCKS):
            grid_ref[row, :, block * LANES : (block + 1) * LANES] = values[2 * block : 2 * block + 2]
        wide = values.astype(jnp.float32)
        squared = wide * wide
        by_cycle = jnp.concatenate(
            [
                jnp.where(in_first, squared, 0.0).astype(jnp.bfloat16),
                jnp.where(in_first, 0.0, squared).astype(jnp.bfloat16),
            ],
            1,
        )
        partial = lax.dot_general(by_cycle, inner, NT, preferred_element_type=jnp.float32)
        cos_sum = jnp.sum((partial * cos_ref[row]).reshape(ROWS_PAD // 8, 8, LANES), 0)
        sin_sum = jnp.sum((partial * sin_ref[row]).reshape(ROWS_PAD // 8, 8, LANES), 0)
        total = cos_sum + sign * pltpu.roll(sin_sum, 64, 1)
        total = total + pltpu.roll(total, 4, 0)
        total = total + pltpu.roll(total, 2, 0)
        sum_ref[0, pl.ds(row, 1), :] = total[0:1, :] * factor
        sum_ref[1, pl.ds(row, 1), :] = total[1:2, :] * factor

    @pl.loop(0, GRID_ROWS // UNROLL)
    def _(step):
        for near in range(UNROLL):
            transform(step * UNROLL + near)

    own_grid = pltpu.make_async_copy(grid_ref, grid_out_ref, local_sem.at[6])
    own_grid.start()
    sums = jnp.concatenate([sum_ref[0], sum_ref[1]], 1).astype(jnp.bfloat16)
    returned = jnp.concatenate(
        [
            lax.dot_general(gather_ref[cycle], sums, NT, preferred_element_type=jnp.float32)
            for cycle in range(2)
        ],
        1,
    )
    returned = jnp.dot(returned.astype(jnp.bfloat16), natural_ref[...], preferred_element_type=jnp.float32)
    ret_ref[...] = returned.astype(jnp.bfloat16).reshape(WAVES, 8, LANES)

    for d in FAR_WAVES:
        target = lax.rem(wave + d, WAVES)
        send(ret_ref.at[target], here.at[wave], turn_send.at[d - 1], turn_recv.at[d - 1], waves[d - 1])
    own_turn = pltpu.make_async_copy(ret_ref.at[wave], here.at[wave], local_sem.at[3])
    own_turn.start()
    own_turn.wait()
    for d in range(1, WAVES):
        block = here.at[lax.rem(wave + WAVES - d, WAVES)]
        remote(block, block, turn_send.at[d - 1], turn_recv.at[d - 1], waves[d - 1]).wait_recv()
    for d in FAR_LEAVES:
        send(here, fields.at[leaf], line_send.at[d - 1], line_recv.at[d - 1], leaves[d - 1])
    own_line = pltpu.make_async_copy(here, fields.at[leaf], local_sem.at[4])
    own_line.start()
    own_line.wait()
    for d in range(1, LEAF):
        block = fields.at[lax.rem(leaf + LEAF - d, LEAF)]
        remote(block, block, line_send.at[d - 1], line_recv.at[d - 1], leaves[d - 1]).wait_recv()
    columns = jnp.concatenate(
        [fields[:, w].reshape(LEAF * 8, LANES)[:, :OWN].astype(jnp.float32) for w in range(WAVES)], 1
    ).astype(jnp.bfloat16)
    product = lax.dot_general(
        columns, panel_ref[...].reshape(width, LATS), NT, preferred_element_type=jnp.float32
    )
    product = jnp.where(kept, product, 0.0)
    product = jnp.where(negated, -product, product)
    narrow = lax.broadcasted_iota(jnp.int32, (width, SPAN), 0) // 2 == lax.broadcasted_iota(jnp.int32, (width, SPAN), 1)
    product = jnp.dot(
        product, jnp.where(narrow, 1.0, 0.0), precision=lax.Precision.HIGHEST, preferred_element_type=jnp.float32
    )
    piece[...] = product.reshape(LEAF, 8, SPAN)
    for d in FAR_LEAVES:
        target = lax.rem(leaf + d, LEAF)
        send(piece.at[target], final.at[leaf], piece_send.at[d - 1], piece_recv.at[d - 1], leaves[d - 1])
    own_piece = pltpu.make_async_copy(piece.at[leaf], final.at[leaf], local_sem.at[5])
    own_piece.start()
    own_piece.wait()
    for d in range(1, LEAF):
        block = final.at[lax.rem(leaf + LEAF - d, LEAF)]
        remote(block, block, piece_send.at[d - 1], piece_recv.at[d - 1], leaves[d - 1]).wait_recv()
    pieces = [final[k] for k in range(LEAF)]
    result = jnp.concatenate(
        [pieces[k][:, y * RUN : (y + 1) * RUN] for y in range(LINES) for k in range(LEAF)], 1
    )
    for s in range(2):
        out_ref[s] = result[4 * s : 4 * s + 2] + result[4 * s + 2 : 4 * s + 4]
    for copy in copies:
        copy.wait_send()
    own_grid.wait()


def put_kernel(source, small_source, target, small_target, held, small, arrive, leave):
    count, size = held.shape[0], held.shape[1]
    spans = [pl.ds(part * size, size) for part in range(count)]
    incoming = [pltpu.make_async_copy(source.at[spans[i]], held.at[i], arrive.at[i]) for i in range(count)]
    outgoing = [pltpu.make_async_copy(held.at[i], target.at[spans[i]], leave.at[i]) for i in range(count)]
    incoming.append(pltpu.make_async_copy(small_source, small, arrive.at[count]))
    outgoing.append(pltpu.make_async_copy(small, small_target, leave.at[count]))
    for copy in incoming:
        copy.start()
    for i in range(count + 1):
        incoming[i].wait()
        outgoing[i].start()
    for copy in outgoing:
        copy.wait()


def per_device(spec, legendre, gauss_w, cycle_len, wave_map):
    slots_dev = spec.shape[0]
    depth = legendre.shape[1] * slots_dev
    panel = legendre.transpose(1, 0, 2)
    coefficients = spec.reshape(slots_dev, 2, DEGREES)
    line = np.arange(WAVES * 8)
    line_slot, line_half, line_part = line // 8 * 2 + line % 8 // 4, line // 2 % 2, line % 2
    both = np.arange(2 * LANES)
    both_half, both_part, both_cycle, both_slot = both // LANES, both // 64 % 2, both // 32 % 2, both % 32
    match = (
        (line_slot[:, None] == both_slot) & (line_half[:, None] == both_half) & (line_part[:, None] == both_part)
    )
    spread = jnp.asarray(match, jnp.bfloat16)
    packed = np.arange(LANES)
    natural = (packed % CYCLE_PAD < GRID_ROWS)[:, None] & (
        (packed % CYCLE_PAD * 2 + packed // CYCLE_PAD)[:, None] == packed[None, :]
    )
    natural = jnp.asarray(natural, jnp.bfloat16)
    gather = jnp.asarray(np.stack([match & (both_cycle == 0), match & (both_cycle == 1)]), jnp.bfloat16)

    vmem = pl.BlockSpec(memory_space=pltpu.VMEM)
    smem = pl.BlockSpec(memory_space=pltpu.SMEM)
    anywhere = pl.BlockSpec(memory_space=pl.ANY)
    dma = pltpu.SemaphoreType.DMA
    bf16, f32 = jnp.bfloat16, jnp.float32
    grid, spec_out = pl.pallas_call(
        whole_kernel,
        out_shape=(
            jax.ShapeDtypeStruct((GRID_ROWS, 2, LPAD), bf16),
            jax.ShapeDtypeStruct((slots_dev, 2, DEGREES), f32),
        ),
        in_specs=[smem] * 3 + [vmem] * 5,
        out_specs=(anywhere, vmem),
        scratch_shapes=[
            pltpu.VMEM((GRID_ROWS, 2, LPAD), bf16),
            pltpu.VMEM((depth, LATS), bf16),
            pltpu.VMEM((8, DEGREES), bf16),
            pltpu.VMEM((LINES, depth, LATS), bf16),
            pltpu.VMEM((LEAF, 8, DEGREES), bf16),
            pltpu.VMEM((LEAF, 8, LATS), f32),
            pltpu.VMEM((LEAF - 1, 8, LATS), f32),
            pltpu.VMEM((WAVES, 8, LANES), bf16),
            pltpu.VMEM((WAVES, 8, LANES), bf16),
            pltpu.VMEM((LANES, LANES), f32),
            pltpu.VMEM((2, CYCLE_PAD, LANES), f32),
            pltpu.VMEM((2, CYCLE_PAD, LANES), f32),
            pltpu.VMEM((2, CYCLE_PAD, LANES), f32),
            pltpu.VMEM((GRID_ROWS, ROWS_PAD, LANES), f32),
            pltpu.VMEM((GRID_ROWS, ROWS_PAD, LANES), f32),
            pltpu.VMEM((GRID_ROWS, LANES, 2 * LANES), bf16),
            pltpu.VMEM((WAVES, 8, LANES), bf16),
            pltpu.VMEM((WAVES, 8, LANES), bf16),
            pltpu.VMEM((LEAF, WAVES, 8, LANES), bf16),
            pltpu.VMEM((LEAF, 8, SPAN), f32),
            pltpu.VMEM((LEAF, 8, SPAN), f32),
            dma((7,)), dma((2, 4, len(CUTS))), dma((2, 4, len(CUTS))),
            dma((LEAF - 1,)), dma((LEAF - 1,)), dma((LEAF - 1,)), dma((LEAF - 1,)),
            dma((WAVES - 1,)), dma((WAVES - 1,)), dma((WAVES - 1,)), dma((WAVES - 1,)),
            dma((LEAF - 1,)), dma((LEAF - 1,)), dma((LEAF - 1,)), dma((LEAF - 1,)),
        ],
        compiler_params=pltpu.CompilerParams(collective_id=0, has_side_effects=True),
        name="whole",
    )(wave_map, cycle_len, gauss_w, panel, coefficients, spread, gather, natural)
    grid, spec_out = pl.pallas_call(
        put_kernel,
        out_shape=(
            jax.ShapeDtypeStruct(grid.shape, bf16),
            jax.ShapeDtypeStruct(spec_out.shape, f32),
        ),
        in_specs=[anywhere] * 2,
        out_specs=(anywhere,) * 2,
        scratch_shapes=[
            pltpu.VMEM((5, GRID_ROWS // 5, 2, LPAD), bf16),
            pltpu.VMEM(spec_out.shape, f32),
            dma((6,)), dma((6,)),
        ],
        name="put",
    )(grid, spec_out)
    grid = grid.transpose(1, 0, 2).reshape(2, GRID_ROWS, 1, LPAD)
    return (grid, spec_out.reshape(slots_dev, 1, 2, DEGREES))


def solution(mesh):
    placed = (P("wave", "lev", None, None), P("wave", "lev", None), P(), P(), P())
    return jax.shard_map(
        per_device,
        mesh=mesh,
        in_specs=placed,
        out_specs=(P(None, "wave", "lev", None), P("wave", "lev", None, None)),
        check_vma=False,
    )
```

```python
import math

import jax
import jax.numpy as jnp
import numpy as np
from jax import lax
from jax.experimental import pallas as pl
from jax.experimental.pallas import tpu as pltpu
from jax.sharding import PartitionSpec as P

LPAD = 4864
LANES = 128
BLOCKS = LPAD // LANES
ROWS_PAD = 80
SLOT_PAD = 32
CYCLE_PAD = 64
WAVES = 12
LINES = 8
LEAF = 8
LATS = 1200
OWN = LATS // WAVES
GRID_ROWS = OWN // 2
DEGREES = 1280
SPAN = DEGREES // LEAF
RUN = SPAN // LINES
SLOTS = 24
EARLY_ROWS = 20
STEP_ROWS = 10
UNROLL = 10
TABLE_UNROLL = 1
CUTS = tuple((start, 8) for start in range(0, 40, 8))
SIDES = ((0, 640), (640, 560))
FAR_LEAVES = (4, 3, 5, 2, 6, 1, 7)
FAR_WAVES = (6, 5, 7, 4, 8, 3, 9, 2, 10, 1, 11)
MESH = pl.DeviceIdType.MESH
NT = (((1,), (1,)), ((), ()))


def cos_sin_turns(turns):
    quarter = turns * 4.0
    whole = jnp.round(quarter)
    rest = (quarter - whole) * (0.5 * math.pi)
    square = rest * rest
    sine = rest + rest * square * (
        -1.6666666666e-1 + square * (8.3333331e-3 + square * (-1.98412698e-4 + square * 2.7557319e-6))
    )
    cosine = 1.0 + square * (
        -0.5 + square * (4.16666667e-2 + square * (-1.388888889e-3 + square * (2.48015873e-5 - square * 2.7557319e-7)))
    )
    step = whole.astype(jnp.int32) & 3
    swap = (step & 1) == 1
    cos_base = jnp.where(swap, sine, cosine)
    sin_base = jnp.where(swap, cosine, sine)
    cos_value = jnp.where((step == 1) | (step == 2), -cos_base, cos_base)
    sin_value = jnp.where(step >= 2, -sin_base, sin_base)
    return cos_value, sin_value


def turns_of(product, length, inverse):
    whole = jnp.round(product * inverse)
    return (product - whole * length) * inverse


def remote(source, target, send, receive, device):
    return pltpu.make_async_remote_copy(
        src_ref=source, dst_ref=target, send_sem=send, recv_sem=receive,
        device_id=device, device_id_type=MESH,
    )


def order_of(map_ref, wave, slot):
    return map_ref[wave * 2 + slot] * DEGREES // SLOTS


def whole_kernel(
    map_ref, len_ref, weight_ref, stored_leg_ref, stored_spec_ref, spread_ref, gather_ref, natural_ref,
    grid_out_ref, out_ref,
    grid_ref, leg_ref, spec_ref, panel_ref, lhs, part, got, four, waves_ref, turned_ref, plain_ref, cross_ref, sum_ref,
    cos_ref, sin_ref, inner_ref, ret_ref, here, fields, piece, final,
    local_sem, ring_send, ring_recv, coef_send, coef_recv, part_send, part_recv,
    wave_send, wave_recv, turn_send, turn_recv, line_send, line_recv, piece_send, piece_recv,
):
    wave = lax.axis_index("wave")
    lev = lax.axis_index("lev")
    line = lax.div(lev, LEAF)
    leaf = lax.rem(lev, LEAF)
    ring = [{"lev": lax.rem(line + d, LINES) * LEAF + leaf} for d in (1, LINES - 1)]
    leaves = [{"lev": line * LEAF + lax.rem(leaf + d, LEAF)} for d in range(1, LEAF)]
    waves = [{"wave": lax.rem(wave + d, WAVES)} for d in range(1, WAVES)]
    peers = waves + leaves + ring
    barrier = pltpu.get_barrier_semaphore()
    for device in peers:
        pl.semaphore_signal(barrier, inc=1, device_id=device, device_id_type=MESH)

    for n in range(RUN):
        leg_ref[2 * n : 2 * n + 2, :] = stored_leg_ref[n]
    for s in range(2):
        for h in range(2):
            spec_ref[4 * s + 2 * h : 4 * s + 2 * h + 2, :] = stored_spec_ref[s]

    first_lat = wave * OWN
    lane = lax.broadcasted_iota(jnp.int32, (1, LANES), 1)
    order_lane = jnp.zeros((1, LANES), jnp.int32)
    for slot in range(SLOTS):
        order_lane = jnp.where(lane % SLOT_PAD == slot, map_ref[slot] * DEGREES // SLOTS, order_lane)
    order_lane = order_lane.astype(jnp.float32)
    double = jnp.where(lane % SLOT_PAD < SLOTS, jnp.where(order_lane == 0.0, 1.0, 2.0), 0.0)
    order_sub = jnp.broadcast_to(order_lane, (LANES, LANES)).T[:SLOT_PAD]
    lane_f = lax.broadcasted_iota(jnp.int32, (ROWS_PAD, LANES), 1)
    row_f = lax.broadcasted_iota(jnp.int32, (ROWS_PAD, LANES), 0)
    block_start = (row_f // 2) * LANES
    position = block_start + lane_f
    block_start = block_start.astype(jnp.float32)
    second_lane = lane // SLOT_PAD % 2 == 1
    sign = jnp.where(lane < 64, 1.0, -1.0)
    inner_lane = lax.broadcasted_iota(jnp.int32, (SLOT_PAD, LANES), 1).astype(jnp.float32)
    inner_product = order_sub * inner_lane
    north = row_f % 2 == 0
    zero_block = jnp.zeros((SLOT_PAD, LANES), jnp.bfloat16)

    def tables(row):
        first_f = len_ref[first_lat + 2 * row].astype(jnp.float32)
        second_f = len_ref[first_lat + 2 * row + 1].astype(jnp.float32)
        length_lane = jnp.where(second_lane, second_f, first_f)
        start_lane = jnp.where(second_lane, first_f, 0.0)
        inverse_lane = 1.0 / length_lane
        inv_first = inverse_lane[:, 0:1]
        inv_second = inverse_lane[:, SLOT_PAD : SLOT_PAD + 1]
        outer = order_lane * (block_start - start_lane)
        outer_cos, outer_sin = cos_sin_turns(turns_of(outer, length_lane, inverse_lane))
        cos_ref[row] = outer_cos
        sin_ref[row] = outer_sin
        cos_a, sin_a = cos_sin_turns(turns_of(inner_product, first_f, inv_first))
        cos_b, sin_b = cos_sin_turns(turns_of(inner_product, second_f, inv_second))
        inner_ref[row] = jnp.concatenate(
            [
                jnp.concatenate([cos_a.astype(jnp.bfloat16), zero_block], 1),
                jnp.concatenate([zero_block, cos_b.astype(jnp.bfloat16)], 1),
                jnp.concatenate([(-sin_a).astype(jnp.bfloat16), zero_block], 1),
                jnp.concatenate([zero_block, (-sin_b).astype(jnp.bfloat16)], 1),
            ],
            0,
        )

    def table_rows(start, count):
        @pl.loop(0, count // TABLE_UNROLL)
        def _(step):
            for near in range(TABLE_UNROLL):
                tables(start + step * TABLE_UNROLL + near)

    table_rows(0, EARLY_ROWS)

    pl.semaphore_wait(barrier, len(peers))

    copies = []

    def send(*details):
        copy = remote(*details)
        copy.start()
        copies.append(copy)

    def ring_copy(source, block, way, hop, cut):
        start, size = CUTS[cut]
        target = panel_ref.at[block, pl.ds(start, size), :]
        return (
            target if source is None else source.at[pl.ds(start, size), :],
            target,
            ring_send.at[way, hop - 1, cut],
            ring_recv.at[way, hop - 1, cut],
            ring[way],
        )

    for cut in range(len(CUTS)):
        for way in range(2):
            send(*ring_copy(leg_ref, line, way, 1, cut))
    own_panel = pltpu.make_async_copy(leg_ref, panel_ref.at[line], local_sem.at[0])
    own_panel.start()
    for d in range(1, LEAF):
        send(spec_ref, lhs.at[leaf], coef_send.at[d - 1], coef_recv.at[d - 1], leaves[d - 1])
    own_coef = pltpu.make_async_copy(spec_ref, lhs.at[leaf], local_sem.at[1])
    own_coef.start()

    for hop in range(1, 4):
        if hop == 1:
            table_rows(EARLY_ROWS, STEP_ROWS)
        for cut in range(len(CUTS)):
            for way in range(2):
                origin = lax.rem(line + (LINES - hop if way == 0 else hop), LINES)
                remote(*ring_copy(None, origin, way, hop, cut)).wait_recv()
                if hop < 3 or cut % 2 == way:
                    send(*ring_copy(None, origin, way, hop + 1, cut))

    width = panel_ref.shape[0] * panel_ref.shape[1]
    column = lax.broadcasted_iota(jnp.int32, (1, width), 1)
    degree = column // (2 * RUN) * SPAN + leaf * RUN + column % (2 * RUN) // 2
    widen = jnp.where(lax.broadcasted_iota(jnp.int32, (DEGREES, width), 0) == degree, 1.0, 0.0)
    widen = widen.astype(jnp.bfloat16)
    four[...] = jnp.zeros_like(four)
    sum_ref[...] = jnp.zeros_like(sum_ref)
    own_coef.wait()
    for d in range(1, LEAF):
        block = lhs.at[lax.rem(leaf + LEAF - d, LEAF)]
        remote(block, block, coef_send.at[d - 1], coef_recv.at[d - 1], leaves[d - 1]).wait_recv()
    coef = jnp.dot(lhs[...].reshape(LEAF * 8, DEGREES), widen, preferred_element_type=jnp.float32)
    kind = lax.broadcasted_iota(jnp.int32, coef.shape, 0) % 8
    order = jnp.where(kind >= 4, order_of(map_ref, wave, 1), order_of(map_ref, wave, 0))
    kept = (kind // 4 == column % 2) & (degree >= order)
    negated = (kind // 2 % 2 == 1) & ((degree + order) % 2 == 1)
    coef = jnp.where(kept, coef, 0.0)
    coef = jnp.where(negated, -coef, coef).astype(jnp.bfloat16)
    own_panel.wait()
    far = lax.rem(line + LINES // 2, LINES)
    for cut in range(len(CUTS)):
        remote(*ring_copy(None, far, cut % 2, 4, cut)).wait_recv()
    for side, (low, size) in enumerate(SIDES):
        span = pl.ds(low, size)
        product = jnp.dot(
            coef, panel_ref[:, :, low : low + size].reshape(width, size), preferred_element_type=jnp.float32
        )
        part[:, :, low : low + size] = product.reshape(LEAF, 8, size)
        for d in FAR_LEAVES:
            target = lax.rem(leaf + d, LEAF)
            send(
                part.at[target, :, span], got.at[d - 1, :, span],
                part_send.at[side, d - 1], part_recv.at[side, d - 1], leaves[d - 1],
            )
    table_rows(EARLY_ROWS + STEP_ROWS, STEP_ROWS)
    total = []
    for side, (low, size) in enumerate(SIDES):
        span = pl.ds(low, size)
        piece_sum = part[leaf, :, low : low + size]
        for d in range(1, LEAF):
            block = got.at[d - 1, :, span]
            remote(
                block, block, part_send.at[side, d - 1], part_recv.at[side, d - 1], leaves[d - 1]
            ).wait_recv()
            piece_sum = piece_sum + got[d - 1, :, low : low + size]
        total.append(piece_sum)
    total = jnp.concatenate(total, 1)
    for w in range(WAVES):
        four[w, :, :OWN] = total[:, w * OWN : (w + 1) * OWN].astype(jnp.bfloat16)
    for d in FAR_WAVES:
        target = lax.rem(wave + d, WAVES)
        send(four.at[target], waves_ref.at[wave], wave_send.at[d - 1], wave_recv.at[d - 1], waves[d - 1])
    own_wave = pltpu.make_async_copy(four.at[wave], waves_ref.at[wave], local_sem.at[2])
    own_wave.start()
    table_rows(EARLY_ROWS + 2 * STEP_ROWS, STEP_ROWS)
    own_wave.wait()
    for d in range(1, WAVES):
        block = waves_ref.at[lax.rem(wave + WAVES - d, WAVES)]
        remote(block, block, wave_send.at[d - 1], wave_recv.at[d - 1], waves[d - 1]).wait_recv()

    arrived = waves_ref[...].reshape(WAVES * 8, LANES)
    turned = lax.dot_general(
        arrived, spread_ref[...], (((0,), (0,)), ((), ())), preferred_element_type=jnp.float32
    )
    for h in range(2):
        turned_ref[...] = turned[:, h * LANES : (h + 1) * LANES]
        half = jnp.where(
            second_lane, turned_ref[pl.ds(1, CYCLE_PAD, 2), :], turned_ref[pl.ds(0, CYCLE_PAD, 2), :]
        )
        half = half * double
        plain_ref[h] = half
        cross_ref[h] = -sign * pltpu.roll(half, 64, 1)

    def transform(row):
        first = len_ref[first_lat + 2 * row]
        second = len_ref[first_lat + 2 * row + 1]
        length_lane = jnp.where(second_lane, second.astype(jnp.float32), first.astype(jnp.float32))
        weight_lane = jnp.where(
            second_lane, weight_ref[first_lat + 2 * row + 1], weight_ref[first_lat + 2 * row]
        )
        resolved = 2.0 * order_lane < length_lane
        factor = jnp.where(resolved, weight_lane / length_lane, 0.0)
        inner = inner_ref[row]
        plain = jnp.where(north, plain_ref[0, pl.ds(row, 1), :], plain_ref[1, pl.ds(row, 1), :])
        crossed = jnp.where(north, cross_ref[0, pl.ds(row, 1), :], cross_ref[1, pl.ds(row, 1), :])
        spread = jnp.where(resolved, plain * cos_ref[row] + crossed * sin_ref[row], 0.0).astype(jnp.bfloat16)
        images = jnp.dot(spread, inner, preferred_element_type=jnp.float32)
        in_first = position < first
        occupied = position < first + second
        values = jnp.where(in_first, images[:, :LANES], jnp.where(occupied, images[:, LANES:], 0.0))
        values = values.astype(jnp.bfloat16)
        for block in range(BLOCKS):
            grid_ref[row, :, block * LANES : (block + 1) * LANES] = values[2 * block : 2 * block + 2]
        wide = values.astype(jnp.float32)
        squared = wide * wide
        by_cycle = jnp.concatenate(
            [
                jnp.where(in_first, squared, 0.0).astype(jnp.bfloat16),
                jnp.where(in_first, 0.0, squared).astype(jnp.bfloat16),
            ],
            1,
        )
        partial = lax.dot_general(by_cycle, inner, NT, preferred_element_type=jnp.float32)
        cos_sum = jnp.sum((partial * cos_ref[row]).reshape(ROWS_PAD // 8, 8, LANES), 0)
        sin_sum = jnp.sum((partial * sin_ref[row]).reshape(ROWS_PAD // 8, 8, LANES), 0)
        total = cos_sum + sign * pltpu.roll(sin_sum, 64, 1)
        total = total + pltpu.roll(total, 4, 0)
        total = total + pltpu.roll(total, 2, 0)
        sum_ref[0, pl.ds(row, 1), :] = total[0:1, :] * factor
        sum_ref[1, pl.ds(row, 1), :] = total[1:2, :] * factor

    @pl.loop(0, GRID_ROWS // UNROLL)
    def _(step):
        for near in range(UNROLL):
            transform(step * UNROLL + near)

    own_grid = pltpu.make_async_copy(grid_ref, grid_out_ref, local_sem.at[6])
    own_grid.start()
    sums = jnp.concatenate([sum_ref[0], sum_ref[1]], 1).astype(jnp.bfloat16)
    returned = jnp.concatenate(
        [
            lax.dot_general(gather_ref[cycle], sums, NT, preferred_element_type=jnp.float32)
            for cycle in range(2)
        ],
        1,
    )
    returned = jnp.dot(returned.astype(jnp.bfloat16), natural_ref[...], preferred_element_type=jnp.float32)
    ret_ref[...] = returned.astype(jnp.bfloat16).reshape(WAVES, 8, LANES)

    for d in FAR_WAVES:
        target = lax.rem(wave + d, WAVES)
        send(ret_ref.at[target], here.at[wave], turn_send.at[d - 1], turn_recv.at[d - 1], waves[d - 1])
    own_turn = pltpu.make_async_copy(ret_ref.at[wave], here.at[wave], local_sem.at[3])
    own_turn.start()
    own_turn.wait()
    for d in range(1, WAVES):
        block = here.at[lax.rem(wave + WAVES - d, WAVES)]
        remote(block, block, turn_send.at[d - 1], turn_recv.at[d - 1], waves[d - 1]).wait_recv()
    for d in FAR_LEAVES:
        send(here, fields.at[leaf], line_send.at[d - 1], line_recv.at[d - 1], leaves[d - 1])
    own_line = pltpu.make_async_copy(here, fields.at[leaf], local_sem.at[4])
    own_line.start()
    own_line.wait()
    for d in range(1, LEAF):
        block = fields.at[lax.rem(leaf + LEAF - d, LEAF)]
        remote(block, block, line_send.at[d - 1], line_recv.at[d - 1], leaves[d - 1]).wait_recv()
    columns = jnp.concatenate(
        [fields[:, w].reshape(LEAF * 8, LANES)[:, :OWN].astype(jnp.float32) for w in range(WAVES)], 1
    ).astype(jnp.bfloat16)
    product = lax.dot_general(
        columns, panel_ref[...].reshape(width, LATS), NT, preferred_element_type=jnp.float32
    )
    product = jnp.where(kept, product, 0.0)
    product = jnp.where(negated, -product, product)
    narrow = lax.broadcasted_iota(jnp.int32, (width, SPAN), 0) // 2 == lax.broadcasted_iota(jnp.int32, (width, SPAN), 1)
    product = jnp.dot(
        product, jnp.where(narrow, 1.0, 0.0), precision=lax.Precision.HIGHEST, preferred_element_type=jnp.float32
    )
    piece[...] = product.reshape(LEAF, 8, SPAN)
    for d in FAR_LEAVES:
        target = lax.rem(leaf + d, LEAF)
        send(piece.at[target], final.at[leaf], piece_send.at[d - 1], piece_recv.at[d - 1], leaves[d - 1])
    own_piece = pltpu.make_async_copy(piece.at[leaf], final.at[leaf], local_sem.at[5])
    own_piece.start()
    own_piece.wait()
    for d in range(1, LEAF):
        block = final.at[lax.rem(leaf + LEAF - d, LEAF)]
        remote(block, block, piece_send.at[d - 1], piece_recv.at[d - 1], leaves[d - 1]).wait_recv()
    pieces = [final[k] for k in range(LEAF)]
    result = jnp.concatenate(
        [pieces[k][:, y * RUN : (y + 1) * RUN] for y in range(LINES) for k in range(LEAF)], 1
    )
    for s in range(2):
        out_ref[s] = result[4 * s : 4 * s + 2] + result[4 * s + 2 : 4 * s + 4]
    for copy in copies:
        copy.wait_send()
    own_grid.wait()


def put_kernel(source, small_source, target, small_target, held, small, arrive, leave):
    count, size = held.shape[0], held.shape[1]
    spans = [pl.ds(part * size, size) for part in range(count)]
    incoming = [pltpu.make_async_copy(source.at[spans[i]], held.at[i], arrive.at[i]) for i in range(count)]
    outgoing = [pltpu.make_async_copy(held.at[i], target.at[spans[i]], leave.at[i]) for i in range(count)]
    incoming.append(pltpu.make_async_copy(small_source, small, arrive.at[count]))
    outgoing.append(pltpu.make_async_copy(small, small_target, leave.at[count]))
    for copy in incoming:
        copy.start()
    for i in range(count + 1):
        incoming[i].wait()
        outgoing[i].start()
    for copy in outgoing:
        copy.wait()


def per_device(spec, legendre, gauss_w, cycle_len, wave_map):
    slots_dev = spec.shape[0]
    depth = legendre.shape[1] * slots_dev
    panel = legendre.transpose(1, 0, 2)
    coefficients = spec.reshape(slots_dev, 2, DEGREES)
    line = np.arange(WAVES * 8)
    line_slot, line_half, line_part = line // 8 * 2 + line % 8 // 4, line // 2 % 2, line % 2
    both = np.arange(2 * LANES)
    both_half, both_part, both_cycle, both_slot = both // LANES, both // 64 % 2, both // 32 % 2, both % 32
    match = (
        (line_slot[:, None] == both_slot) & (line_half[:, None] == both_half) & (line_part[:, None] == both_part)
    )
    spread = jnp.asarray(match, jnp.bfloat16)
    packed = np.arange(LANES)
    natural = (packed % CYCLE_PAD < GRID_ROWS)[:, None] & (
        (packed % CYCLE_PAD * 2 + packed // CYCLE_PAD)[:, None] == packed[None, :]
    )
    natural = jnp.asarray(natural, jnp.bfloat16)
    gather = jnp.asarray(np.stack([match & (both_cycle == 0), match & (both_cycle == 1)]), jnp.bfloat16)

    vmem = pl.BlockSpec(memory_space=pltpu.VMEM)
    smem = pl.BlockSpec(memory_space=pltpu.SMEM)
    anywhere = pl.BlockSpec(memory_space=pl.ANY)
    dma = pltpu.SemaphoreType.DMA
    bf16, f32 = jnp.bfloat16, jnp.float32
    grid, spec_out = pl.pallas_call(
        whole_kernel,
        out_shape=(
            jax.ShapeDtypeStruct((GRID_ROWS, 2, LPAD), bf16),
            jax.ShapeDtypeStruct((slots_dev, 2, DEGREES), f32),
        ),
        in_specs=[smem] * 3 + [vmem] * 5,
        out_specs=(anywhere, vmem),
        scratch_shapes=[
            pltpu.VMEM((GRID_ROWS, 2, LPAD), bf16),
            pltpu.VMEM((depth, LATS), bf16),
            pltpu.VMEM((8, DEGREES), bf16),
            pltpu.VMEM((LINES, depth, LATS), bf16),
            pltpu.VMEM((LEAF, 8, DEGREES), bf16),
            pltpu.VMEM((LEAF, 8, LATS), f32),
            pltpu.VMEM((LEAF - 1, 8, LATS), f32),
            pltpu.VMEM((WAVES, 8, LANES), bf16),
            pltpu.VMEM((WAVES, 8, LANES), bf16),
            pltpu.VMEM((LANES, LANES), f32),
            pltpu.VMEM((2, CYCLE_PAD, LANES), f32),
            pltpu.VMEM((2, CYCLE_PAD, LANES), f32),
            pltpu.VMEM((2, CYCLE_PAD, LANES), f32),
            pltpu.VMEM((GRID_ROWS, ROWS_PAD, LANES), f32),
            pltpu.VMEM((GRID_ROWS, ROWS_PAD, LANES), f32),
            pltpu.VMEM((GRID_ROWS, LANES, 2 * LANES), bf16),
            pltpu.VMEM((WAVES, 8, LANES), bf16),
            pltpu.VMEM((WAVES, 8, LANES), bf16),
            pltpu.VMEM((LEAF, WAVES, 8, LANES), bf16),
            pltpu.VMEM((LEAF, 8, SPAN), f32),
            pltpu.VMEM((LEAF, 8, SPAN), f32),
            dma((7,)), dma((2, 4, len(CUTS))), dma((2, 4, len(CUTS))),
            dma((LEAF - 1,)), dma((LEAF - 1,)), dma((2, LEAF - 1)), dma((2, LEAF - 1)),
            dma((WAVES - 1,)), dma((WAVES - 1,)), dma((WAVES - 1,)), dma((WAVES - 1,)),
            dma((LEAF - 1,)), dma((LEAF - 1,)), dma((LEAF - 1,)), dma((LEAF - 1,)),
        ],
        compiler_params=pltpu.CompilerParams(collective_id=0, has_side_effects=True),
        name="whole",
    )(wave_map, cycle_len, gauss_w, panel, coefficients, spread, gather, natural)
    grid, spec_out = pl.pallas_call(
        put_kernel,
        out_shape=(
            jax.ShapeDtypeStruct(grid.shape, bf16),
            jax.ShapeDtypeStruct(spec_out.shape, f32),
        ),
        in_specs=[anywhere] * 2,
        out_specs=(anywhere,) * 2,
        scratch_shapes=[
            pltpu.VMEM((5, GRID_ROWS // 5, 2, LPAD), bf16),
            pltpu.VMEM(spec_out.shape, f32),
            dma((6,)), dma((6,)),
        ],
        name="put",
    )(grid, spec_out)
    grid = grid.transpose(1, 0, 2).reshape(2, GRID_ROWS, 1, LPAD)
    return (grid, spec_out.reshape(slots_dev, 1, 2, DEGREES))


def solution(mesh):
    placed = (P("wave", "lev", None, None), P("wave", "lev", None), P(), P(), P())
    return jax.shard_map(
        per_device,
        mesh=mesh,
        in_specs=placed,
        out_specs=(P(None, "wave", "lev", None), P("wave", "lev", None, None)),
        check_vma=False,
    )
```
